32 devices in a mesh: fsdp: 8 (over z, x), sp: 4 (over y, core).
Axes of the slice: x: 2, y: 2, z: 4, core: 2. Of those that a mesh axis runs over, the one named last changes fastest.
Arguments:
- tokens: bfloat16 [8, 2048, 2048], P('fsdp', 'sp'), may hold values from -6 to 6
- seg_ids: int32 [8, 2048], P('fsdp', 'sp'), may hold values from 0 to 255, as said below
- pad_mask: int32 [8, 2048], P('fsdp', 'sp'), may hold values from 0 to 1, as said below
- positions: int32 [8, 2048], P('fsdp', 'sp'), may hold values from 0 to 2047, as said below
- attn_gain: bfloat16 [2048], P('fsdp'), may hold values from 0.25 to 1.75
- w_query: bfloat16 [2048, 1536], P('fsdp'), may hold values from -0.125 to 0.125
- w_key: bfloat16 [2048, 384], P('fsdp'), may hold values from -0.125 to 0.125
- w_value: bfloat16 [2048, 384], P('fsdp'), may hold values from -0.125 to 0.125
- query_gain: bfloat16 [64], replicated, may hold values from 0.25 to 1.75
- key_gain: bfloat16 [64], replicated, may hold values from 0.25 to 1.75
- w_out: bfloat16 [1536, 2048], P('fsdp'), may hold values from -0.625 to 0.625
- ffn_gain: bfloat16 [2048], P('fsdp'), may hold values from 0.25 to 1.75
- w_gate: bfloat16 [2048, 4864], P('fsdp'), may hold values from -0.125 to 0.125
- w_up: bfloat16 [2048, 4864], P('fsdp'), may hold values from -0.125 to 0.125
- w_down: bfloat16 [4864, 2048], P('fsdp'), may hold values from -0.078125 to 0.078125
- cotangent: bfloat16 [8, 2048, 2048], P('fsdp', 'sp'), may hold values from -6 to 6
Outputs:
- layer_out: bfloat16 [8, 2048, 2048], P('fsdp', 'sp')
- tokens_grad: bfloat16 [8, 2048, 2048], P('fsdp', 'sp')
- attn_gain_grad: float32 [2048], P('fsdp')
- w_query_grad: float32 [2048, 1536], P('fsdp')
- w_key_grad: float32 [2048, 384], P('fsdp')
- w_value_grad: float32 [2048, 384], P('fsdp')
- query_gain_grad: float32 [64], replicated
- key_gain_grad: float32 [64], replicated
- w_out_grad: float32 [1536, 2048], P('fsdp')
- ffn_gain_grad: float32 [2048], P('fsdp')
- w_gate_grad: float32 [2048, 4864], P('fsdp')
- w_up_grad: float32 [2048, 4864], P('fsdp')
- w_down_grad: float32 [4864, 2048], P('fsdp')
The draws below stay inside these ranges and needn't reach their ends.
Inputs may be any that keep to these rules, and one draw needn't show every extreme that they name: `seg_ids`: within a sequence, document numbers start at 0 and never fall; each document but the last has 8 or more tokens. `positions`: A token's offset from the first token of its document. `pad_mask`: 1 on a leading run of each sequence, 0 on its last 1 to 256 tokens.
All inputs are finite; a program needn't handle non-finite values.
Results may differ from the reference program's by a relative error of at most 0.02.
Values may be sent and summed in bfloat16 or wider, within the bound.
A program may use at most 384 MiB of HBM per device.

```python
import jax
import jax.numpy as jnp
from jax import lax

D = 2048
Q_HEADS = 24
KV_HEADS = 6
HEAD_DIM = 64
FF = 4864
SEQ_LEN = 2048
Q_WIDTH = 1536
KV_WIDTH = 384
BATCH = 8


def documents(key):
    keys_all = jax.random.split(jax.random.fold_in(key, 41), BATCH)
    top_power = SEQ_LEN.bit_length() - 1
    doc_slots = SEQ_LEN // 8
    offsets = jnp.arange(SEQ_LEN, dtype=jnp.int32)

    def one_sequence(members):
        sub_key, seq_index = members
        power_key, extra_key, pad_key = jax.random.split(sub_key, 3)
        powers = jax.random.randint(power_key, (doc_slots,), 3, top_power + 1)
        lengths = jnp.left_shift(jnp.ones_like(powers), powers) + jax.random.randint(extra_key, (doc_slots,), 0, 8)
        lengths = jnp.where(seq_index == 0, SEQ_LEN, jnp.where(seq_index == 1, 8, lengths)).astype(jnp.int32)
        ends = jnp.cumsum(lengths).astype(jnp.int32)
        finished = ends[None, :] <= offsets[:, None]
        doc_ids = jnp.sum(finished.astype(jnp.int32), axis=1)
        starts = jnp.max(jnp.where(finished, ends[None, :], 0), axis=1)
        padding = jax.random.randint(pad_key, (), 1, SEQ_LEN // 8 + 1)
        live_mask = (offsets < SEQ_LEN - padding).astype(jnp.int32)
        return (doc_ids.astype(jnp.int32), (offsets - starts).astype(jnp.int32), live_mask)
    return lax.map(one_sequence, (keys_all, jnp.arange(BATCH, dtype=jnp.int32)))


def draw_seg_ids(key, part):
    return documents(key)[0]


def draw_positions(key, part):
    return documents(key)[1]


def draw_pad_mask(key, part):
    return documents(key)[2]


def strengthened(values, rng, source, target, shards_of, factor):
    def block_of(position):
        return (jnp.arange(values.shape[position]) // (values.shape[position] // shards_of)).reshape((-1,) + (1,) * (values.ndim - 1 - position))

    near = jax.random.permutation(rng, shards_of)[block_of(target)]
    second = (block_of(target) + shards_of // 2) % shards_of
    return jnp.where((block_of(source) == near) | (block_of(source) == second), factor * values, values)


def shard_levels(stream_key, dims, cuts, least, largest):
    loudness = 1.0
    for dim, parts in cuts:
        heights = jax.random.uniform(jax.random.fold_in(jax.random.fold_in(stream_key, 6), dim), (parts,), jnp.float32, least / len(cuts), largest / len(cuts))
        loudness = loudness * jnp.repeat(jnp.exp(heights), dims[dim] // parts).reshape((-1,) + (1,) * (len(dims) - 1 - dim))
    return loudness


def bell_draw(stream_key, shape, scale, limit, cuts=(), kind=jnp.bfloat16):
    values = scale * jax.random.normal(stream_key, shape, jnp.float32)
    if cuts:
        values = values * shard_levels(stream_key, shape, cuts, -0.22, 0.18)
    return jnp.clip(values, -limit, limit).astype(kind)


def bell_draw_with(stream_key, shape, scale, most, pieces, heavy, kind=jnp.bfloat16):
    values = scale * jax.random.normal(stream_key, shape, jnp.float32)
    if pieces:
        values = values * shard_levels(stream_key, shape, pieces, -0.22, 0.18)
    return jnp.clip(strengthened(values, jax.random.fold_in(stream_key, 3), *heavy), -most, most).astype(kind)


def setup_inputs(seed: int = 0) -> dict:
    key_of = jax.random.split(jax.random.key(seed), 17)
    return {
        "tokens": bell_draw_with(key_of[0], (BATCH, SEQ_LEN, D), 1.0, 6.0, ((0, 8), (1, 4)), (0, 2, 8, 2.0)),
        "seg_ids": draw_seg_ids(jax.random.fold_in(key_of[16], 71), 0),
        "pad_mask": draw_pad_mask(jax.random.fold_in(key_of[16], 71), 0),
        "positions": draw_positions(jax.random.fold_in(key_of[16], 71), 0),
        "attn_gain": jnp.clip(1.0 + 0.15 * jax.random.normal(key_of[4], (D,), jnp.float32), 0.25, 1.75).astype(jnp.bfloat16),
        "w_query": bell_draw(key_of[5], (D, Q_WIDTH), D ** -0.5, 0.125, ((0, 8),)),
        "w_key": bell_draw(key_of[6], (D, KV_WIDTH), D ** -0.5, 0.125, ((0, 8),)),
        "w_value": bell_draw(key_of[7], (D, KV_WIDTH), D ** -0.5, 0.125, ((0, 8),)),
        "query_gain": jnp.clip(1.0 + 0.15 * jax.random.normal(key_of[8], (HEAD_DIM,), jnp.float32), 0.25, 1.75).astype(jnp.bfloat16),
        "key_gain": jnp.clip(1.0 + 0.15 * jax.random.normal(key_of[9], (HEAD_DIM,), jnp.float32), 0.25, 1.75).astype(jnp.bfloat16),
        "w_out": bell_draw(key_of[10], (Q_WIDTH, D), (Q_WIDTH // 16) ** -0.5, 0.625, ((0, 8),)),
        "ffn_gain": jnp.clip(1.0 + 0.15 * jax.random.normal(key_of[11], (D,), jnp.float32), 0.25, 1.75).astype(jnp.bfloat16),
        "w_gate": bell_draw(key_of[12], (D, FF), D ** -0.5, 0.125, ((0, 8),)),
        "w_up": bell_draw(key_of[13], (D, FF), D ** -0.5, 0.125, ((0, 8),)),
        "w_down": bell_draw(key_of[14], (FF, D), FF ** -0.5, 0.078125, ((0, 8),)),
        "cotangent": bell_draw_with(key_of[15], (BATCH, SEQ_LEN, D), 1.0, 6.0, ((0, 8), (1, 4)), (0, 2, 8, 2.0)),
    }


epsilon = 1e-06
rope_base = 10000.0
masked_score = -1e+30

@jax.custom_vjp
def low(v):
    return lax.optimization_barrier(v.astype(jnp.bfloat16)).astype(jnp.float32)

@jax.custom_vjp
def low_back(v):
    return v

def low_keep(v):
    return (low(v), None)

def low_pass(kept, grad):
    return (grad,)

def back_keep(v):
    return (v, None)

def back_low(kept, grad):
    return (low(grad),)
low.defvjp(low_keep, low_pass)
low_back.defvjp(back_keep, back_low)

def highest(left_side, right_side):
    return jnp.dot(left_side, right_side, precision=lax.Precision.HIGHEST)

def rms_scale(values, norm_gain):
    return values * lax.rsqrt(lax.optimization_barrier(jnp.mean(values * values, axis=-1, keepdims=True)) + epsilon) * norm_gain

def rotate(values, cosine, sine_table):
    half_dim = values.shape[-1] // 2
    turned = jnp.concatenate([-values[..., half_dim:], values[..., :half_dim]], axis=-1)
    return values * cosine + turned * sine_table

def rope_tables(offsets, head_dim):
    half_dim = head_dim // 2
    inverse = rope_base ** (-(jnp.arange(half_dim, dtype=jnp.float32) * 2.0) / head_dim)
    angles = offsets.astype(jnp.float32)[..., None] * inverse
    return (jnp.concatenate([jnp.cos(angles), jnp.cos(angles)], axis=-1), jnp.concatenate([jnp.sin(angles), jnp.sin(angles)], axis=-1))

def allowed_mask(doc_ids, live_keys):
    offsets = jnp.arange(doc_ids.shape[0])
    same_doc = doc_ids[:, None] == doc_ids[None, :]
    causal = offsets[None, :] <= offsets[:, None]
    live_pair = (live_keys[None, :] == 1) | (offsets[None, :] == offsets[:, None])
    return same_doc & causal & live_pair

def forward_seq(inputs, params, cosine, sine_table, allowed):
    attn_gain, w_query, w_key, w_value, query_gain, key_gain, w_out, ffn_gain, w_gate, w_up, w_down = params
    length = inputs.shape[0]
    normed = low(rms_scale(inputs, attn_gain))
    queries = low_back(highest(normed, w_query)).reshape(length, Q_HEADS, HEAD_DIM)
    key_heads = low_back(highest(normed, w_key)).reshape(length, KV_HEADS, HEAD_DIM)
    values = low_back(low(highest(normed, w_value))).reshape(length, KV_HEADS, HEAD_DIM)
    queries = low_back(low(rotate(rms_scale(queries, query_gain), cosine[:, None], sine_table[:, None])))
    key_heads = low_back(low(rotate(rms_scale(key_heads, key_gain), cosine[:, None], sine_table[:, None])))
    group_size = Q_HEADS // KV_HEADS
    keys_all = jnp.repeat(key_heads, group_size, axis=1)
    values_all = jnp.repeat(values, group_size, axis=1)
    block_rows = min(512, length)
    block_count = length // block_rows

    def attend(block_pair):
        query_block, allowed_block = block_pair
        scores = low_back(jnp.einsum('qhd,khd->hqk', query_block, keys_all, precision=lax.Precision.HIGHEST) * HEAD_DIM ** (-0.5))
        scores = jnp.where(allowed_block[None], scores, masked_score)
        highest_score = lax.optimization_barrier(jnp.max(scores, axis=-1, keepdims=True))
        log_total = highest_score + jnp.log(lax.optimization_barrier(jnp.sum(jnp.exp(scores - highest_score), axis=-1, keepdims=True)))
        probabilities = low(jnp.exp(scores - log_total))
        return jnp.einsum('hqk,khd->qhd', probabilities, values_all, precision=lax.Precision.HIGHEST)
    attended = lax.map(jax.checkpoint(attend), (queries.reshape(block_count, block_rows, Q_HEADS, HEAD_DIM), allowed.reshape(block_count, block_rows, length)))
    attended = low_back(low(attended.reshape(length, Q_HEADS * HEAD_DIM)))
    branch = low_back(highest(attended, w_out))
    middle = inputs + branch
    normed_two = low(rms_scale(middle, ffn_gain))
    gate_part = low_back(highest(normed_two, w_gate))
    up_part = low_back(highest(normed_two, w_up))
    hidden = low(jax.nn.silu(gate_part) * up_part)
    return middle + highest(hidden, w_down)

def reference(tokens, seg_ids, pad_mask, positions, attn_gain, w_query, w_key, w_value, query_gain, key_gain, w_out, ffn_gain, w_gate, w_up, w_down, cotangent):
    weights = tuple((weight.astype(jnp.float32) for weight in (attn_gain, w_query, w_key, w_value, query_gain, key_gain, w_out, ffn_gain, w_gate, w_up, w_down)))
    zeros_init = tuple((jnp.zeros_like(weight) for weight in weights))

    def one_sequence(totals, members):
        inputs, doc_ids, live_keys, offsets, grad_out = members
        cosine, sine_table = rope_tables(offsets, HEAD_DIM)
        allowed = allowed_mask(doc_ids, live_keys)

        def forward(values, params):
            return forward_seq(values, params, cosine, sine_table, allowed)
        result, pullback = jax.vjp(forward, inputs.astype(jnp.float32), weights)
        grad_in, grad_params = pullback(grad_out.astype(jnp.float32))
        totals = tuple((total_part + grad_part for total_part, grad_part in zip(totals, grad_params)))
        return (totals, (result.astype(jnp.bfloat16), grad_in.astype(jnp.bfloat16)))
    grad_sums, outputs = lax.scan(one_sequence, zeros_init, (tokens, seg_ids, pad_mask, positions, cotangent))
    return (outputs[0], outputs[1], grad_sums[0], grad_sums[1], grad_sums[2], grad_sums[3], grad_sums[4], grad_sums[5], grad_sums[6], grad_sums[7], grad_sums[8], grad_sums[9], grad_sums[10])
```

```python
import functools, math
import jax, jax.numpy as jnp
from jax import lax
from jax.experimental import pallas as pl
from jax.experimental.pallas import tpu as pltpu
bf16=jnp.bfloat16; f32=jnp.float32
NEG=-1e30
NT=(((1,),(1,)),((),()))
NN=(((1,),(0,)),((),()))
TN=(((0,),(0,)),((),()))

def dg(a,b,dims):
    return lax.dot_general(a,b,dims,preferred_element_type=f32)

def lane_iota(rows, cols):
    return lax.broadcasted_iota(jnp.int32,(rows,cols),1)

def split3(v):
    hi=v.astype(bf16); r=v-hi.astype(f32)
    mid=r.astype(bf16); lo=(r-mid.astype(f32)).astype(bf16)
    return hi,mid,lo

def aug_lanes(v):
    hi,mid,lo=split3(v)
    lane=lane_iota(*v.shape)%64
    z=jnp.zeros_like(v)
    return jnp.where(lane==0,hi.astype(f32),jnp.where(lane==1,mid.astype(f32),jnp.where(lane==2,lo.astype(f32),z))).astype(bf16)

def fwd_kernel(nb, blk, sub, c, kvsel, info, q_ref, k_ref, v_ref, start_ref, o_ref, laug_ref, ka, kb, ra, rb, ral, rbl):
    p=pl.program_id(0)
    s=info[0]; nlive=info[1]
    T=q_ref.shape[0]
    per=blk//sub
    nsub=T//sub
    lane=lane_iota(T,128)
    low=lane<64
    first=info[2+p]==0
    kk=k_ref[...].astype(f32); vv=v_ref[...].astype(f32)
    ksw=pltpu.roll(kk,64,1); vsw=pltpu.roll(vv,64,1)
    k0=jnp.where(first,kk,ksw)
    k1=jnp.where(first,ksw,kk)
    v0=jnp.where(first,vv,vsw); v1=jnp.where(first,vsw,vv)
    zero=jnp.zeros_like(kk)
    ka[...]=jnp.where(low,k0,zero).astype(bf16)
    kb[...]=jnp.where(low,zero,k1).astype(bf16)
    va=jnp.where(low,v0,zero); vb=jnp.where(low,zero,v1)
    one_a=jnp.where(low,1.0,0.0).astype(f32); one_b=1.0-one_a
    ra[:,:128]=va.astype(bf16); rb[:,:128]=vb.astype(bf16)
    ra[:,128:]=one_a.astype(bf16); rb[:,128:]=one_b.astype(bf16)
    rows=lax.broadcasted_iota(jnp.int32,(T,128),0)
    true_row=((rows//blk)^s)*blk+rows%blk
    live=true_row<nlive
    ral[:,:128]=jnp.where(live,va,0.0).astype(bf16); rbl[:,:128]=jnp.where(live,vb,0.0).astype(bf16)
    ral[:,128:]=jnp.where(live,one_a,0.0).astype(bf16); rbl[:,128:]=jnp.where(live,one_b,0.0).astype(bf16)

    def pos(t):
        return pl.multiple_of(((t//per)^s)*blk+(t%per)*sub, sub)

    def qblock(i,_):
        qo=pos(i)
        q=q_ref[pl.ds(qo,sub),:]
        st=start_ref[pl.ds(qo,sub),:]
        kcol=lane_iota(sub,sub)
        qrow=lax.broadcasted_iota(jnp.int32,(sub,sub),0)
        first_key=info[8+i]
        stl=st-i*sub
        ok=(kcol>=stl)&(kcol<=qrow)&((kcol<nlive-i*sub)|(kcol==qrow))
        s0=dg(q,ka[pl.ds(qo,sub),:],NT); s1=dg(q,kb[pl.ds(qo,sub),:],NT)
        p0=jnp.where(ok,jnp.exp2(s0*c),0.0).astype(bf16)
        p1=jnp.where(ok,jnp.exp2(s1*c),0.0).astype(bf16)
        acc=dg(p0,ra[pl.ds(qo,sub),:],NN)+dg(p1,rb[pl.ds(qo,sub),:],NN)
        def kblock(j,acc):
            ko=pos(j)
            s0=dg(q,ka[pl.ds(ko,sub),:],NT); s1=dg(q,kb[pl.ds(ko,sub),:],NT)
            ok=kcol>=(st-j*sub)
            p0=jnp.where(ok,jnp.exp2(s0*c),0.0).astype(bf16)
            p1=jnp.where(ok,jnp.exp2(s1*c),0.0).astype(bf16)
            return acc+dg(p0,ral[pl.ds(ko,sub),:],NN)+dg(p1,rbl[pl.ds(ko,sub),:],NN)
        acc=lax.fori_loop(first_key,i,kblock,acc)
        l=acc[:,128:]
        o_ref[pl.ds(qo,sub),:]=(acc[:,:128]/l).astype(bf16)
        laug_ref[pl.ds(qo,sub),:]=aug_lanes(jnp.log(l)*(-8.0))
        return 0
    lax.fori_loop(0,nsub,qblock,0)

def flash_fwd(info,q,k,v,start,*,blk,sub,head_dim=64):
    T=q.shape[0]; pairs=q.shape[1]//128
    c=math.log2(math.e)*head_dim**-0.5
    kern=functools.partial(fwd_kernel,T//blk,blk,sub,c,None)
    full=lambda n: pl.BlockSpec((T,n),lambda p,*_:(0,0))
    pair=pl.BlockSpec((T,128),lambda p,*_:(0,p))
    return pl.pallas_call(kern,
        grid_spec=pltpu.PrefetchScalarGridSpec(num_scalar_prefetch=1,grid=(pairs,),
            in_specs=[pair,full(128),full(128),full(1)],out_specs=[pair,pair],
            scratch_shapes=[pltpu.VMEM((T,128),bf16)]*2+[pltpu.VMEM((T,256),bf16)]*4),
        out_shape=[jax.ShapeDtypeStruct((T,pairs*128),bf16)]*2,
        compiler_params=pltpu.CompilerParams(dimension_semantics=("arbitrary",),vmem_limit_bytes=60*2**20),
        cost_estimate=pl.CostEstimate(flops=int(pairs*2*T*T*64*2*2*0.6),bytes_accessed=6*T*128*pairs,transcendentals=pairs*T*T),
        name="flash_fwd")(info,q,k,v,start)

def bwd_kernel(blk, sub, c, scale, info, q_ref, laug_ref, do_ref, o_ref, k_ref, v_ref, start_ref,
               dq_ref, dk_ref, dv_ref, qa, qb, qaug, doa, dob, doaug, ka, kb, kaug0, kaug1, vaug0, vaug1, dqacc):
    p=pl.program_id(0)
    s=info[0]; nlive=info[1]
    T=q_ref.shape[0]
    per=blk//sub; nsub=T//sub
    lane=lane_iota(T,128); low=lane<64
    first=info[2+p]==0
    kk=k_ref[...].astype(f32); vv=v_ref[...].astype(f32)
    ksw=pltpu.roll(kk,64,1); vsw=pltpu.roll(vv,64,1)
    k0=jnp.where(first,kk,ksw); k1=jnp.where(first,ksw,kk)
    v0=jnp.where(first,vv,vsw); v1=jnp.where(first,vsw,vv)
    zero=jnp.zeros_like(kk)
    kA=jnp.where(low,k0,zero).astype(bf16); kB=jnp.where(low,zero,k1).astype(bf16)
    vA=jnp.where(low,v0,zero).astype(bf16); vB=jnp.where(low,zero,v1).astype(bf16)
    ka[...]=kA; kb[...]=kB
    onesA=jnp.where(lane<3,1.0,0.0).astype(bf16)
    onesB=jnp.where((lane>=64)&(lane<67),1.0,0.0).astype(bf16)
    kaug0[:,:128]=kA; kaug0[:,128:]=onesA
    kaug1[:,:128]=kB; kaug1[:,128:]=onesB
    vaug0[:,:128]=vA; vaug0[:,128:]=onesA
    vaug1[:,:128]=vB; vaug1[:,128:]=onesB
    q=q_ref[...]
    qf=q.astype(f32)
    qaug[:,:128]=q; qaug[:,128:]=laug_ref[...]
    qa[...]=jnp.where(low,qf,zero).astype(bf16); qb[...]=jnp.where(low,zero,qf).astype(bf16)
    do=do_ref[...]; dof=do.astype(f32)
    doa[...]=jnp.where(low,dof,zero).astype(bf16); dob[...]=jnp.where(low,zero,dof).astype(bf16)
    doaug[:,:128]=do
    prod=dof*o_ref[...].astype(f32)
    r128=lax.broadcasted_iota(jnp.int32,(128,128),0)//64; c128=lane_iota(128,128)//64
    same=jnp.where(r128==c128,1.0,0.0).astype(bf16)
    hi,mid,lo=split3(prod)
    delta=dg(hi,same,NN)+dg(mid,same,NN)+dg(lo,same,NN)
    doaug[:,128:]=aug_lanes(-delta)
    dqacc[...]=jnp.zeros_like(dqacc)
    def pos(t):
        return pl.multiple_of(((t//per)^s)*blk+(t%per)*sub, sub)
    krow=lax.broadcasted_iota(jnp.int32,(sub,sub),0)
    qcol=lane_iota(sub,sub)
    def kblock(j,_):
        ko=pos(j)
        ksl=pl.ds(ko,sub)
        def step(qo,ok,dk,dv):
            qsl=pl.ds(qo,sub)
            qg=qaug[qsl,:]; dg_=doaug[qsl,:]
            s0=dg(kaug0[ksl,:],qg,NT); s1=dg(kaug1[ksl,:],qg,NT)
            e0=jnp.where(ok,jnp.exp2(s0*c),0.0); e1=jnp.where(ok,jnp.exp2(s1*c),0.0)
            dp0=dg(vaug0[ksl,:],dg_,NT); dp1=dg(vaug1[ksl,:],dg_,NT)
            ds0=(e0*dp0).astype(bf16); ds1=(e1*dp1).astype(bf16)
            dv=dv+dg(e0.astype(bf16),doa[qsl,:],NN)+dg(e1.astype(bf16),dob[qsl,:],NN)
            dk=dk+dg(ds0,qa[qsl,:],NN)+dg(ds1,qb[qsl,:],NN)
            dqacc[qsl,:]+=dg(ds0,ka[ksl,:],TN)+dg(ds1,kb[ksl,:],TN)
            return dk,dv
        st=start_ref[:,pl.ds(ko,sub)]-j*sub
        ok=(krow>=st)&(krow<=qcol)&((krow<nlive-j*sub)|(krow==qcol))
        z=jnp.zeros((sub,128),f32)
        dk,dv=step(ko,ok,z,z)
        def qblock(i,carry):
            dk,dv=carry
            qo=pos(i)
            st=start_ref[:,pl.ds(qo,sub)]-j*sub
            ok=(krow>=st)&(krow<nlive-j*sub)
            return step(qo,ok,dk,dv)
        dk,dv=lax.fori_loop(j+1,info[24+j],qblock,(dk,dv))
        dk_ref[ksl,:]=(dk*scale)
        dv_ref[ksl,:]=dv
        return 0
    lax.fori_loop(0,nsub,kblock,0)
    dq_ref[...]=(dqacc[...]*scale).astype(bf16)

def flash_bwd(info,q,laug,do,o,k,v,start_row,*,blk,sub,head_dim=64):
    T=q.shape[0]; pairs=q.shape[1]//128
    scale=head_dim**-0.5
    c=math.log2(math.e)*scale
    kern=functools.partial(bwd_kernel,blk,sub,c,scale)
    full=lambda n: pl.BlockSpec((T,n),lambda p,*_:(0,0))
    pair=pl.BlockSpec((T,128),lambda p,*_:(0,p))
    return pl.pallas_call(kern,
        grid_spec=pltpu.PrefetchScalarGridSpec(num_scalar_prefetch=1,grid=(pairs,),
            in_specs=[pair,pair,pair,pair,full(128),full(128),pl.BlockSpec((1,T),lambda p,*_:(0,0))],out_specs=[pair,pair,pair],
            scratch_shapes=[pltpu.VMEM((T,128),bf16)]*2+[pltpu.VMEM((T,256),bf16)]+[pltpu.VMEM((T,128),bf16)]*2+[pltpu.VMEM((T,256),bf16)]+[pltpu.VMEM((T,128),bf16)]*2+[pltpu.VMEM((T,256),bf16)]*4+[pltpu.VMEM((T,128),f32)]),
        out_shape=[jax.ShapeDtypeStruct((T,pairs*128),bf16),jax.ShapeDtypeStruct((T,pairs*128),f32),jax.ShapeDtypeStruct((T,pairs*128),f32)],
        compiler_params=pltpu.CompilerParams(dimension_semantics=("arbitrary",),vmem_limit_bytes=60*2**20),
        cost_estimate=pl.CostEstimate(flops=int(pairs*2*T*T*64*2*5*0.6),bytes_accessed=16*T*128*pairs,transcendentals=pairs*T*T),
        name="flash_bwd")(info,q,laug,do,o,k,v,start_row)

def make_info(s,nlive,start,kvmap,pairs,sub):
    T=start.shape[0]; nsub=T//sub
    fk=jnp.min(start.reshape(nsub,sub),axis=1)//sub
    i=jnp.arange(nsub)
    sees=(fk[None,:]<=i[:,None])
    lastq=jnp.max(jnp.where(sees,i[None,:]+1,0),axis=1)
    info=jnp.zeros((40,),jnp.int32)
    info=info.at[0].set(s).at[1].set(nlive).at[2:2+pairs].set(kvmap).at[8:8+nsub].set(fk).at[24:24+nsub].set(lastq)
    return info


from jax.sharding import PartitionSpec as P

epsilon = 1e-06
rope_base = 10000.0


def perm_f(x, m):
    n = lax.axis_size("fsdp")
    return lax.ppermute(x, "fsdp", [(i, i ^ m) for i in range(n)])


def perm_s(x, m):
    n = lax.axis_size("sp")
    return lax.ppermute(x, "sp", [(i, i ^ m) for i in range(n)])


def gather_f(x):
    outer = lax.axis_size("fsdp") // 2
    firsts = [x] + [perm_f(x, 2 * m) for m in range(1, outer)]
    pieces = []
    for first in firsts:
        pieces += [first, perm_f(first, 1)]
    return pieces


def gather_s(x):
    far = perm_s(x, 2)
    near = perm_s(x, 1)
    return [x, near, far, perm_s(far, 1)]


def place(pieces, me):
    out = jnp.zeros((len(pieces),) + pieces[0].shape, pieces[0].dtype)
    for r, piece in enumerate(pieces):
        out = lax.dynamic_update_index_in_dim(out, piece, me ^ r, 0)
    return out


def scatter_f(blocks):
    outer = blocks.shape[0] // 2
    me = lax.axis_index("fsdp")
    pairs = blocks.reshape((outer, 2) + blocks.shape[1:])
    mine = lax.dynamic_index_in_dim(pairs, me % 2, 1, keepdims=False)
    other = lax.dynamic_index_in_dim(pairs, 1 - me % 2, 1, keepdims=False)
    got = perm_f(other, 1)
    both = (mine.astype(f32) + got.astype(f32)).astype(bf16)
    at = me // 2
    total = lax.dynamic_index_in_dim(both, at, 0, keepdims=False).astype(f32)
    for m in range(1, outer):
        part = perm_f(lax.dynamic_index_in_dim(both, at ^ m, 0, keepdims=False), 2 * m)
        total = total + part.astype(f32)
    return total.astype(bf16)


def scatter_s(parts):
    got3 = perm_s(parts[3], 1)
    got1 = perm_s(parts[1], 1)
    far = perm_s((parts[2].astype(f32) + got3.astype(f32)).astype(bf16), 2)
    return parts[0].astype(f32) + got1.astype(f32) + far.astype(f32)


def half_swap(v):
    lane = lane_iota(*v.shape) % 64
    return jnp.where(lane < 32, pltpu.roll(v, 96, 1), pltpu.roll(v, 32, 1))


def head_sums(v):
    row = lax.broadcasted_iota(jnp.int32, (128, 128), 0) // 64
    col = lane_iota(128, 128) // 64
    same = jnp.where(row == col, 1.0, 0.0).astype(bf16)
    hi, mid, lo = split3(v)
    return dg(hi, same, NN) + dg(mid, same, NN) + dg(lo, same, NN)


def qkv_kernel(count, pairs, *refs):
    x_refs = refs[:count]
    w_ref, cos_ref, sin_ref, gain_ref = refs[count : count + 4]
    xh_ref, q_ref, k_ref, v_ref, raw_ref = refs[-5:]
    for n in range(count):
        x = x_refs[n][...].astype(f32)
        scale = lax.rsqrt(jnp.mean(x * x, axis=-1, keepdims=True) + epsilon)
        xh = (x * scale).astype(bf16)
        xh_ref[n] = xh
        raw = dg(xh, w_ref[...], NN)
        cosine, sine = cos_ref[n], sin_ref[n]
        for p in range(pairs + 1):
            part = raw[:, 128 * p : 128 * (p + 1)]
            raw_ref[n, :, 128 * p : 128 * (p + 1)] = part
            inv = lax.rsqrt(head_sums(part * part) * (1.0 / 64) + epsilon)
            normal = part * inv * gain_ref[(0 if p < pairs else 1) : (1 if p < pairs else 2), :]
            turned = (normal * cosine + half_swap(normal) * sine).astype(bf16)
            if p < pairs:
                q_ref[n, :, 128 * p : 128 * (p + 1)] = turned
            else:
                k_ref[n] = turned
        v_ref[n] = raw[:, 128 * (pairs + 1) :].astype(bf16)


def qkv_call(chunk, chunks, xs, weight, cosine, sine, gains, earlier, tile=256):
    count = len(xs)
    rows, width = xs[0].shape
    cols = weight.shape[1]
    pairs = cols // 128 - 2
    widths = (width, pairs * 128, 128, 128, (pairs + 1) * 128)
    types = (bf16, bf16, bf16, bf16, f32)
    n_in = count + 4
    return pl.pallas_call(
        functools.partial(qkv_kernel, count, pairs),
        grid=(rows // tile,),
        in_specs=[pl.BlockSpec((tile, width), lambda i: (i, 0))] * count
        + [pl.BlockSpec(weight.shape, lambda i: (0, 0))]
        + [pl.BlockSpec((count, tile, 128), lambda i: (chunk, i, 0))] * 2
        + [pl.BlockSpec((8, 128), lambda i: (0, 0))]
        + [pl.BlockSpec(memory_space=pl.ANY)] * len(earlier),
        out_specs=[pl.BlockSpec((count, tile, n), lambda i: (chunk, i, 0)) for n in widths],
        out_shape=[
            jax.ShapeDtypeStruct((chunks * count, rows, n), t) for n, t in zip(widths, types)
        ],
        input_output_aliases={n_in + i: i for i in range(len(earlier))},
        compiler_params=pltpu.CompilerParams(vmem_limit_bytes=60 * 2**20),
        cost_estimate=pl.CostEstimate(
            flops=2 * count * rows * width * cols,
            bytes_accessed=count * rows * width * 4 + width * cols * 2,
            transcendentals=0,
        ),
        name="qkv",
    )(*xs, weight, cosine, sine, gains, *earlier)


def ffn_kernel(count, n_in, *refs):
    n2_refs, dy_refs = refs[:count], refs[count : 2 * count]
    wg_ref, wu_ref, wd_ref = refs[2 * count : 2 * count + 3]
    hid_ref, dg_ref, du_ref, n2_out, dn_ref, acc = refs[n_in:]
    step = pl.program_id(0)
    wg, wu, wd = wg_ref[0], wu_ref[0], wd_ref[...]
    for n in range(count):
        n2, dy = n2_refs[n][...], dy_refs[n][...]
        gate = dg(n2, wg, NN)
        up = dg(n2, wu, NN)
        dhid = dg(dy, wd, NT)
        sig = jax.nn.sigmoid(gate)
        act = gate * sig
        hid_ref[n] = (act * up).astype(bf16)
        dup = (dhid * act).astype(bf16)
        dgate = (dhid * up * (sig * (1.0 + gate * (1.0 - sig)))).astype(bf16)
        dg_ref[n] = dgate
        du_ref[n] = dup
        grad = dg(dgate, wg, NT) + dg(dup, wu, NT)

        @pl.when(step == 0)
        def _():
            acc[n] = grad
            n2_out[n] = n2

        @pl.when(step > 0)
        def _():
            acc[n] += grad

        @pl.when(step == pl.num_programs(0) - 1)
        def _():
            dn_ref[n] = acc[n].astype(bf16)


def ffn_call(chunk, chunks, n2s, dys, w_gu, w_d, earlier, tile=256):
    count = len(n2s)
    rows, width = n2s[0].shape
    units = w_d.shape[0]
    n_in = 2 * count + 3 + len(earlier)
    once = pl.Buffered(1)
    big = jax.ShapeDtypeStruct((chunks * count, rows, units), bf16)
    return pl.pallas_call(
        functools.partial(ffn_kernel, count, n_in),
        grid=(units // tile,),
        in_specs=[pl.BlockSpec((rows, width), lambda j: (0, 0), pipeline_mode=once)] * (2 * count)
        + [
            pl.BlockSpec((1, width, tile), lambda j: (0, 0, j)),
            pl.BlockSpec((1, width, tile), lambda j: (1, 0, j)),
            pl.BlockSpec((tile, width), lambda j: (j, 0)),
        ]
        + [pl.BlockSpec(memory_space=pl.ANY)] * len(earlier),
        out_specs=[pl.BlockSpec((count, rows, tile), lambda j: (chunk, 0, j))] * 3
        + [
            pl.BlockSpec((count, rows, width), lambda j: (chunk, 0, 0)),
            pl.BlockSpec((count, rows, width), lambda j: (0, 0, 0)),
        ],
        out_shape=[big, big, big]
        + [
            jax.ShapeDtypeStruct((chunks * count, rows, width), bf16),
            jax.ShapeDtypeStruct((count, rows, width), bf16),
        ],
        scratch_shapes=[pltpu.VMEM((count, rows, width), f32)],
        input_output_aliases={2 * count + 3 + i: i for i in range(len(earlier))},
        compiler_params=pltpu.CompilerParams(vmem_limit_bytes=62 * 2**20),
        cost_estimate=pl.CostEstimate(
            flops=10 * count * rows * width * units,
            bytes_accessed=8 * count * rows * width + 6 * width * units,
            transcendentals=count * rows * units,
        ),
        name="ffn",
    )(*n2s, *dys, w_gu, w_gu, w_d, *earlier)


def back_kernel(pairs, info, dq_ref, dk_ref, dv_ref, raw_ref, cos_ref, sin_ref, gain_ref, w_ref, dqkv_ref, dn_ref, dgain_ref):
    odd = info[0] % 2 == 1
    rows = dq_ref.shape[0]
    low = lane_iota(rows, 128) < 64

    def fold(ref):
        sums = []
        for p in range(pairs):
            part = ref[:, 128 * p : 128 * (p + 1)]
            sums.append(part + pltpu.roll(part, 64, 1))
        first, second = jnp.zeros_like(sums[0]), jnp.zeros_like(sums[0])
        for p in range(pairs):
            at_first = info[2 + p] == 0
            first = first + jnp.where(at_first, sums[p], 0.0)
            second = second + jnp.where(at_first, 0.0, sums[p])
        return jnp.where(low, first, second)

    @pl.when(pl.program_id(0) == 0)
    def _():
        dgain_ref[...] = jnp.zeros_like(dgain_ref)

    cosine, sine = cos_ref[...], sin_ref[...]
    outs = []
    sums = [jnp.zeros((8, 128), f32), jnp.zeros((8, 128), f32)]
    for p in range(pairs + 1):
        which = 0 if p < pairs else 1
        if p < pairs:
            grad = dq_ref[:, 128 * p : 128 * (p + 1)].astype(f32)
        else:
            grad = fold(dk_ref).astype(bf16).astype(f32)
        raw = raw_ref[:, 128 * p : 128 * (p + 1)]
        inv = lax.rsqrt(head_sums(raw * raw) * (1.0 / 64) + epsilon)
        normal = raw * inv
        grad = grad * cosine - half_swap(grad) * sine
        sums[which] = sums[which] + jnp.sum((grad * normal).reshape(rows // 8, 8, 128), axis=0)
        grad = grad * gain_ref[which : which + 1, :]
        mean = head_sums(grad * normal) * (1.0 / 64)
        outs.append((inv * (grad - normal * mean)).astype(bf16))
    outs.append(fold(dv_ref).astype(bf16))
    for p, out in enumerate(outs):
        dqkv_ref[:, 128 * p : 128 * (p + 1)] = out
    dgain_ref[0] += sums[0]
    dgain_ref[1] += sums[1]
    dn_ref[...] = dg(dqkv_ref[...], w_ref[...], NT).astype(bf16)


def back_call(first, count, blk, info, dq, dk, dv, raw, cosine, sine, gains, weight, earlier, tile=256):
    rows = dq.shape[0]
    width, cols = weight.shape
    pairs = cols // 128 - 2
    per = blk // tile
    n = count * per
    base = first * per

    def spec(w):
        return pl.BlockSpec((tile, w), lambda i, *_: (base + i, 0))

    def body(*refs):
        back_kernel(pairs, *refs[:9], *refs[9 + len(earlier) :])

    return pl.pallas_call(
        body,
        grid_spec=pltpu.PrefetchScalarGridSpec(
            num_scalar_prefetch=1,
            grid=(n,),
            in_specs=[
                spec(pairs * 128),
                spec(pairs * 128),
                spec(pairs * 128),
                spec((pairs + 1) * 128),
                spec(128),
                spec(128),
                pl.BlockSpec((8, 128), lambda i, *_: (0, 0)),
                pl.BlockSpec(weight.shape, lambda i, *_: (0, 0)),
            ]
            + [pl.BlockSpec(memory_space=pl.ANY)] * len(earlier),
            out_specs=[
                spec(cols),
                pl.BlockSpec((tile, width), lambda i, *_: (i, 0)),
                pl.BlockSpec((2, 8, 128), lambda i, *_: (0, 0, 0)),
            ],
        ),
        out_shape=[
            jax.ShapeDtypeStruct((rows, cols), bf16),
            jax.ShapeDtypeStruct((count * blk, width), bf16),
            jax.ShapeDtypeStruct((2, 8, 128), f32),
        ],
        input_output_aliases={9 + i: i for i in range(len(earlier))},
        compiler_params=pltpu.CompilerParams(vmem_limit_bytes=60 * 2**20),
        cost_estimate=pl.CostEstimate(
            flops=2 * count * blk * width * cols,
            bytes_accessed=count * blk * (width * 2 + cols * 12) + width * cols * 2,
            transcendentals=0,
        ),
        name="qkv_back",
    )(info, dq, dk, dv, raw, cosine, sine, gains, weight, *earlier)


def pick_kernel(members, shards, shard, unit, info, gain_ref, wg_ref, wu_ref, out_ref):
    out_ref[...] = jnp.zeros_like(out_ref)
    for k in range(members):
        width = min(unit, shard - k * unit)

        @pl.when(info[0] == k)
        def _():
            for n, ref in enumerate((wg_ref, wu_ref)):
                for j in range(shards):
                    part = ref[:, j * shard + k * unit : j * shard + k * unit + width].astype(f32)
                    out_ref[n, :, j * unit : j * unit + width] = (part * gain_ref[...]).astype(bf16)


def pick_call(info, gain, w_gate, w_up, members, shards, shard, unit):
    rows, cols = w_gate.shape
    tile = min(64, rows)
    return pl.pallas_call(
        functools.partial(pick_kernel, members, shards, shard, unit),
        grid_spec=pltpu.PrefetchScalarGridSpec(
            num_scalar_prefetch=1,
            grid=(rows // tile,),
            in_specs=[pl.BlockSpec((tile, 1), lambda i, *_: (i, 0))]
            + [pl.BlockSpec((tile, cols), lambda i, *_: (i, 0))] * 2,
            out_specs=pl.BlockSpec((2, tile, shards * unit), lambda i, *_: (0, i, 0)),
        ),
        out_shape=jax.ShapeDtypeStruct((2, rows, shards * unit), bf16),
        compiler_params=pltpu.CompilerParams(vmem_limit_bytes=60 * 2**20),
        name="pick_units",
    )(info, gain, w_gate, w_up)


def join_kernel(members, shards, shard, unit, gain_ref, m_ref, w_ref, out_ref, sum_ref):
    for k in range(members):
        width = min(unit, shard - k * unit)
        for j in range(shards):
            part = m_ref[k, :, j * unit : j * unit + width].astype(f32)
            out_ref[:, j * shard + k * unit : j * shard + k * unit + width] = part
    full = out_ref[...]
    sum_ref[...] = jnp.broadcast_to(
        jnp.sum(full * w_ref[...].astype(f32), axis=-1, keepdims=True), sum_ref.shape
    )
    out_ref[...] = full * gain_ref[...]


def join_call(gain, stacked, weight, members, shards, shard, unit):
    rows, cols = weight.shape
    tile = min(64, rows)
    return pl.pallas_call(
        functools.partial(join_kernel, members, shards, shard, unit),
        grid=(rows // tile,),
        in_specs=[
            pl.BlockSpec((tile, 1), lambda i: (i, 0)),
            pl.BlockSpec((members, tile, shards * unit), lambda i: (0, i, 0)),
            pl.BlockSpec((tile, cols), lambda i: (i, 0)),
        ],
        out_specs=[
            pl.BlockSpec((tile, cols), lambda i: (i, 0)),
            pl.BlockSpec((tile, 128), lambda i: (i, 0)),
        ],
        out_shape=[
            jax.ShapeDtypeStruct((rows, cols), f32),
            jax.ShapeDtypeStruct((rows, 128), f32),
        ],
        compiler_params=pltpu.CompilerParams(vmem_limit_bytes=60 * 2**20),
        name="join_units",
    )(gain, stacked, weight)


def dot_bf(a, b, dims):
    return dg(a, b, dims).astype(bf16)


def local(
    tokens, seg_ids, pad_mask, positions, attn_gain, w_query, w_key, w_value, query_gain,
    key_gain, w_out, ffn_gain, w_gate, w_up, w_down, cotangent,
):
    nf, ns = lax.axis_size("fsdp"), lax.axis_size("sp")
    f, s = lax.axis_index("fsdp"), lax.axis_index("sp")
    seq_count, blk, width = tokens.shape
    assert seq_count == 1 and ns == 4
    length = blk * ns
    head = query_gain.shape[0]
    q_heads, kv_heads = w_query.shape[1] // head, w_key.shape[1] // head
    group = q_heads // kv_heads
    q_local = q_heads // ns
    kv_base = [(q_local * k) // group for k in range(ns)]
    pairs = q_local // 2
    q_cols = q_local * head
    kv_map = jnp.array(
        [[(q_local * k + 2 * p) // group - kv_base[k] for p in range(pairs)] for k in range(ns)],
        jnp.int32,
    )[s]
    base = jnp.array(kv_base, jnp.int32)[s] * head
    shard = w_down.shape[0]
    unit = -(-(-(-shard // ns)) // 16) * 16
    units = unit * nf
    out_rows = w_out.shape[0]
    quarter = out_rows // ns
    sub = 512

    x = tokens[0]
    dy = cotangent[0]
    gain_one = attn_gain.astype(f32)[:, None]
    gain_two = ffn_gain.astype(f32)[:, None]

    small = jnp.stack([positions[0], pad_mask[0]])
    small_all = jnp.stack(gather_s(small))
    pos_rel = small_all[:, 0]
    n_live = jnp.sum(small_all[:, 1])

    xs = gather_s(x)

    kv_cols = 2 * head
    mine = jnp.concatenate(
        [
            lax.dynamic_slice_in_dim(w_query, s * q_cols, q_cols, 1),
            lax.dynamic_slice_in_dim(w_key, base, kv_cols, 1),
            lax.dynamic_slice_in_dim(w_value, base, kv_cols, 1),
        ],
        axis=1,
    )
    mine = (mine.astype(f32) * gain_one).astype(bf16)
    w_qkv = place(gather_f(mine), f).reshape(width, q_cols + 2 * kv_cols)

    out_mine = lax.dynamic_slice_in_dim(w_out, s * quarter, quarter, 0)
    out_part = place(gather_f(out_mine), f)
    out_all = place(gather_s(out_part), s)
    out_true = out_all.transpose(1, 0, 2, 3).reshape(ns, q_cols, width)
    w_out_rel = jnp.concatenate(
        [lax.dynamic_index_in_dim(out_true, s ^ r, 0, keepdims=False) for r in range(ns)]
    )

    dys = gather_s(dy)

    one_info = jnp.reshape(s, (1,)).astype(jnp.int32)
    gu_mine = pick_call(one_info, gain_two, w_gate, w_up, ns, nf, shard, unit)
    down_pad = jnp.concatenate(
        [w_down, jnp.zeros((unit * ns - shard, width), bf16)]
    )
    down_mine = lax.dynamic_slice_in_dim(down_pad, s * unit, unit, 0)
    gu_pieces = gather_f(gu_mine)
    down_pieces = gather_f(down_mine)
    w_gu = jnp.zeros((2, nf, gu_mine.shape[1], units), bf16)
    for r, piece in enumerate(gu_pieces):
        w_gu = lax.dynamic_update_slice_in_dim(w_gu, piece[:, None], f ^ r, 1)
    w_gu = w_gu.reshape(2, width, units)
    w_d = place(down_pieces, f).reshape(units, width)

    half = head // 2
    inverse = rope_base ** (-(jnp.arange(half, dtype=f32) * 2.0) / head)
    angles = pos_rel.astype(f32)[..., None] * inverse
    co, si = jnp.cos(angles), jnp.sin(angles)
    cosine = jnp.concatenate([co] * 4, axis=-1)
    sine = jnp.concatenate([-si, si, -si, si], axis=-1)
    gains = jnp.concatenate(
        [
            jnp.tile(query_gain.astype(f32), 2)[None],
            jnp.tile(key_gain.astype(f32), 2)[None],
            jnp.zeros((6, 2 * head), f32),
        ]
    )

    first = qkv_call(0, 2, xs[:2], w_qkv, cosine, sine, gains, [])
    xh, q, k, v, raw = qkv_call(1, 2, xs[2:], w_qkv, cosine, sine, gains, first)
    xh, q, k, v, raw = [a.reshape(length, -1) for a in (xh, q, k, v, raw)]

    true_block = s ^ jnp.arange(ns)
    start_rel = true_block[:, None] * blk + jnp.arange(blk)[None] - pos_rel
    start_true = place([start_rel[r] for r in range(ns)], s).reshape(length)
    info = make_info(s, n_live, start_true, kv_map, pairs, sub)
    start_rel = start_rel.reshape(length)
    attended, laug = flash_fwd(info, q, k, v, start_rel[:, None], blk=blk, sub=sub)

    att = [attended[:blk]] + [perm_s(attended[r * blk : (r + 1) * blk], r) for r in range(1, ns)]
    att = jnp.concatenate(att, axis=1)
    xf = x.astype(f32)
    middle = xf + dg(att, w_out_rel, NN)
    inv_two = lax.rsqrt(jnp.mean(middle * middle, axis=-1, keepdims=True) + epsilon)
    n2s = gather_s((middle * inv_two).astype(bf16))

    first = ffn_call(0, 2, n2s[:2], dys[:2], w_gu, w_d, [])
    second = ffn_call(1, 2, n2s[2:], dys[2:], w_gu, w_d, first[:4])
    hidden, dgate, dup, n2_all = [a.reshape(length, -1) for a in second[:4]]
    dn2 = [first[4][0], first[4][1], second[4][0], second[4][1]]
    dn2_own = scatter_s(dn2)
    hat_two = middle * inv_two
    dmiddle = dy.astype(f32) + inv_two * (
        dn2_own - hat_two * jnp.mean(dn2_own * hat_two, axis=-1, keepdims=True)
    )
    dmid = dmiddle.astype(bf16)
    datt = dot_bf(dmid, w_out_rel, NT)
    datt = [datt[:, :q_cols]] + [
        perm_s(datt[:, r * q_cols : (r + 1) * q_cols], r) for r in range(1, ns)
    ]
    datt = jnp.concatenate(datt)

    dy_all = jnp.concatenate(dys)
    grad_d = dot_bf(hidden, dy_all, TN).reshape(nf, unit, width)
    grad_g = dot_bf(n2_all, dgate, TN).reshape(nf, width // nf, units)
    grad_u = dot_bf(n2_all, dup, TN).reshape(nf, width // nf, units)
    out_part_sum = dot_bf(hidden, w_d, NN).reshape(ns, blk, width)
    sum_d = gather_s(scatter_f(grad_d))
    sum_g = gather_s(scatter_f(grad_g))
    sum_u = gather_s(scatter_f(grad_u))
    layer_out = (middle + scatter_s([out_part_sum[r] for r in range(ns)])).astype(bf16)
    w_down_grad = place(sum_d, s).reshape(ns * unit, width)[:shard].astype(f32)
    w_gate_grad, gate_sum = join_call(gain_two, place(sum_g, s), w_gate, ns, nf, shard, unit)
    w_up_grad, up_sum = join_call(gain_two, place(sum_u, s), w_up, ns, nf, shard, unit)
    ffn_gain_grad = (gate_sum + up_sum)[:, 0]

    grad_o = dot_bf(att, dmid, TN).reshape(ns, q_cols, width)
    grad_o = jnp.stack(
        [lax.dynamic_index_in_dim(grad_o, s ^ t, 0, keepdims=False) for t in range(ns)]
    ).reshape(nf, ns, quarter, width)
    parts = [lax.dynamic_index_in_dim(grad_o, s ^ r, 1, keepdims=False) for r in range(ns)]
    sum_o = gather_s(scatter_f(scatter_s(parts).astype(bf16)))
    w_out_grad = place(sum_o, s).reshape(out_rows, width).astype(f32)

    dq, dk, dv = flash_bwd(
        info, q, laug, datt, attended, k, v, start_rel[None, :], blk=blk, sub=sub
    )
    cos2, sin2 = cosine.reshape(length, -1), sine.reshape(length, -1)
    dqkv, dn_far, dgain_far = back_call(
        2, 2, blk, info, dq, dk, dv, raw, cos2, sin2, gains, w_qkv, []
    )
    dqkv, dn_near, dgain_near = back_call(
        0, 2, blk, info, dq, dk, dv, raw, cos2, sin2, gains, w_qkv, [dqkv]
    )
    dn_own = scatter_s([dn_near[:blk], dn_near[blk:], dn_far[:blk], dn_far[blk:]])
    inv_one = lax.rsqrt(jnp.mean(xf * xf, axis=-1, keepdims=True) + epsilon)
    hat_one = xf * inv_one
    tokens_grad = (
        dmiddle + inv_one * (dn_own - hat_one * jnp.mean(dn_own * hat_one, axis=-1, keepdims=True))
    ).astype(bf16)

    dgain = jnp.sum(dgain_far + dgain_near, axis=1)
    dgain = jnp.pad((dgain[:, :head] + dgain[:, head:]).reshape(1, -1), ((0, 7), (0, 0)))
    m = 1
    while m < ns:
        dgain = dgain + perm_s(dgain, m)
        m *= 2
    m = 1
    while m < nf:
        dgain = dgain + perm_f(dgain, m)
        m *= 2
    query_gain_grad, key_gain_grad = dgain[0, :head], dgain[0, head:]

    grad_qkv = dot_bf(xh, dqkv, TN).reshape(nf, width // nf, -1)
    sum_qkv = place(gather_s(scatter_f(grad_qkv)), s).astype(f32)
    m_query = jnp.concatenate([sum_qkv[k][:, :q_cols] for k in range(ns)], axis=1)

    def heads_of(offset):
        cols = []
        for h in range(kv_heads):
            total = 0.0
            for k in range(ns):
                if 0 <= h - kv_base[k] < 2:
                    at = offset + (h - kv_base[k]) * head
                    total = total + sum_qkv[k][:, at : at + head]
            cols.append(total)
        return jnp.concatenate(cols, axis=1)

    m_key, m_value = heads_of(q_cols), heads_of(q_cols + kv_cols)
    attn_gain_grad = (
        jnp.sum(m_query * w_query.astype(f32), axis=1)
        + jnp.sum(m_key * w_key.astype(f32), axis=1)
        + jnp.sum(m_value * w_value.astype(f32), axis=1)
    )
    return (
        layer_out[None], tokens_grad[None], attn_gain_grad, m_query * gain_one, m_key * gain_one,
        m_value * gain_one, query_gain_grad, key_gain_grad, w_out_grad, ffn_gain_grad,
        w_gate_grad, w_up_grad, w_down_grad,
    )


def solution(mesh):
    row, vec = P("fsdp", None), P("fsdp")
    tok, ids = P("fsdp", "sp", None), P("fsdp", "sp")
    in_specs = (tok, ids, ids, ids, vec, row, row, row, P(), P(), row, vec, row, row, row, tok)
    out_specs = (tok, tok, vec, row, row, row, P(), P(), row, vec, row, row, row)
    return jax.shard_map(local, mesh=mesh, in_specs=in_specs, out_specs=out_specs, check_vma=False)
```

```python
import functools, math
import jax, jax.numpy as jnp
from jax import lax
from jax.experimental import pallas as pl
from jax.experimental.pallas import tpu as pltpu
bf16=jnp.bfloat16; f32=jnp.float32
tiny=pl.CostEstimate(flops=1000000,bytes_accessed=1000000,transcendentals=0)
NT=(((1,),(1,)),((),()))
NN=(((1,),(0,)),((),()))
TN=(((0,),(0,)),((),()))

def dg(a,b,dims):
    return lax.dot_general(a,b,dims,preferred_element_type=f32)

def lane_iota(rows, cols):
    return lax.broadcasted_iota(jnp.int32,(rows,cols),1)

def split3(v):
    hi=v.astype(bf16); r=v-hi.astype(f32)
    mid=r.astype(bf16); lo=(r-mid.astype(f32)).astype(bf16)
    return hi,mid,lo

def aug_lanes(v):
    hi,mid,lo=split3(v)
    lane=lane_iota(*v.shape)%64
    z=jnp.zeros_like(v)
    return jnp.where(lane==0,hi.astype(f32),jnp.where(lane==1,mid.astype(f32),jnp.where(lane==2,lo.astype(f32),z))).astype(bf16)

def fwd_kernel(nb, blk, sub, c, kvsel, info, q_ref, k_ref, v_ref, start_ref, o_ref, laug_ref, ka, kb, ra, rb, ral, rbl):
    p=pl.program_id(0)
    s=info[0]; nlive=info[1]
    T=q_ref.shape[0]
    per=blk//sub
    nsub=T//sub
    lane=lane_iota(T,128)
    low=lane<64
    first=info[2+p]==0
    kk=k_ref[...].astype(f32); vv=v_ref[...].astype(f32)
    ksw=pltpu.roll(kk,64,1); vsw=pltpu.roll(vv,64,1)
    k0=jnp.where(first,kk,ksw)
    k1=jnp.where(first,ksw,kk)
    v0=jnp.where(first,vv,vsw); v1=jnp.where(first,vsw,vv)
    zero=jnp.zeros_like(kk)
    ka[...]=jnp.where(low,k0,zero).astype(bf16)
    kb[...]=jnp.where(low,zero,k1).astype(bf16)
    va=jnp.where(low,v0,zero); vb=jnp.where(low,zero,v1)
    one_a=jnp.where(low,1.0,0.0).astype(f32); one_b=1.0-one_a
    ra[:,:128]=va.astype(bf16); rb[:,:128]=vb.astype(bf16)
    ra[:,128:]=one_a.astype(bf16); rb[:,128:]=one_b.astype(bf16)
    rows=lax.broadcasted_iota(jnp.int32,(T,128),0)
    true_row=((rows//blk)^s)*blk+rows%blk
    live=true_row<nlive
    ral[:,:128]=jnp.where(live,va,0.0).astype(bf16); rbl[:,:128]=jnp.where(live,vb,0.0).astype(bf16)
    ral[:,128:]=jnp.where(live,one_a,0.0).astype(bf16); rbl[:,128:]=jnp.where(live,one_b,0.0).astype(bf16)

    def pos(t):
        return pl.multiple_of(((t//per)^s)*blk+(t%per)*sub, sub)

    def qblock(i,_):
        qo=pos(i)
        q=q_ref[pl.ds(qo,sub),:]
        st=start_ref[pl.ds(qo,sub),:]
        kcol=lane_iota(sub,sub)
        qrow=lax.broadcasted_iota(jnp.int32,(sub,sub),0)
        first_key=info[8+i]
        stl=st-i*sub
        ok=(kcol>=stl)&(kcol<=qrow)&((kcol<nlive-i*sub)|(kcol==qrow))
        s0=dg(q,ka[pl.ds(qo,sub),:],NT); s1=dg(q,kb[pl.ds(qo,sub),:],NT)
        p0=jnp.where(ok,jnp.exp2(s0*c),0.0).astype(bf16)
        p1=jnp.where(ok,jnp.exp2(s1*c),0.0).astype(bf16)
        acc=dg(p0,ra[pl.ds(qo,sub),:],NN)+dg(p1,rb[pl.ds(qo,sub),:],NN)
        def kblock(j,acc):
            ko=pos(j)
            s0=dg(q,ka[pl.ds(ko,sub),:],NT); s1=dg(q,kb[pl.ds(ko,sub),:],NT)
            ok=kcol>=(st-j*sub)
            p0=jnp.where(ok,jnp.exp2(s0*c),0.0).astype(bf16)
            p1=jnp.where(ok,jnp.exp2(s1*c),0.0).astype(bf16)
            return acc+dg(p0,ral[pl.ds(ko,sub),:],NN)+dg(p1,rbl[pl.ds(ko,sub),:],NN)
        acc=lax.fori_loop(first_key,i,kblock,acc)
        l=acc[:,128:]
        o_ref[pl.ds(qo,sub),:]=(acc[:,:128]/l).astype(bf16)
        laug_ref[pl.ds(qo,sub),:]=aug_lanes(jnp.log(l)*(-8.0))
        return 0
    lax.fori_loop(0,nsub,qblock,0)

def flash_fwd(info,q,k,v,start,*,blk,sub,head_dim=64):
    T=q.shape[0]; pairs=q.shape[1]//128
    c=math.log2(math.e)*head_dim**-0.5
    kern=functools.partial(fwd_kernel,T//blk,blk,sub,c,None)
    full=lambda n: pl.BlockSpec((T,n),lambda p,*_:(0,0))
    pair=pl.BlockSpec((T,128),lambda p,*_:(0,p))
    return pl.pallas_call(kern,
        grid_spec=pltpu.PrefetchScalarGridSpec(num_scalar_prefetch=1,grid=(pairs,),
            in_specs=[pair,full(128),full(128),full(1)],out_specs=[pair,pair],
            scratch_shapes=[pltpu.VMEM((T,128),bf16)]*2+[pltpu.VMEM((T,256),bf16)]*4),
        out_shape=[jax.ShapeDtypeStruct((T,pairs*128),bf16)]*2,
        compiler_params=pltpu.CompilerParams(dimension_semantics=("arbitrary",),vmem_limit_bytes=60*2**20),
        cost_estimate=tiny,
        name="flash_fwd")(info,q,k,v,start)

def bwd_kernel(blk, sub, c, scale, info, q_ref, laug_ref, do_ref, o_ref, k_ref, v_ref, start_ref,
               dq_ref, dk_ref, dv_ref, qa, qb, qaug, doa, dob, doaug, ka, kb, kaug0, kaug1, vaug0, vaug1, dqacc):
    p=pl.program_id(0)
    s=info[0]; nlive=info[1]
    T=q_ref.shape[0]
    per=blk//sub; nsub=T//sub
    lane=lane_iota(T,128); low=lane<64
    first=info[2+p]==0
    kk=k_ref[...].astype(f32); vv=v_ref[...].astype(f32)
    ksw=pltpu.roll(kk,64,1); vsw=pltpu.roll(vv,64,1)
    k0=jnp.where(first,kk,ksw); k1=jnp.where(first,ksw,kk)
    v0=jnp.where(first,vv,vsw); v1=jnp.where(first,vsw,vv)
    zero=jnp.zeros_like(kk)
    kA=jnp.where(low,k0,zero).astype(bf16); kB=jnp.where(low,zero,k1).astype(bf16)
    vA=jnp.where(low,v0,zero).astype(bf16); vB=jnp.where(low,zero,v1).astype(bf16)
    ka[...]=kA; kb[...]=kB
    onesA=jnp.where(lane<3,1.0,0.0).astype(bf16)
    onesB=jnp.where((lane>=64)&(lane<67),1.0,0.0).astype(bf16)
    kaug0[:,:128]=kA; kaug0[:,128:]=onesA
    kaug1[:,:128]=kB; kaug1[:,128:]=onesB
    vaug0[:,:128]=vA; vaug0[:,128:]=onesA
    vaug1[:,:128]=vB; vaug1[:,128:]=onesB
    q=q_ref[...]
    qf=q.astype(f32)
    qaug[:,:128]=q; qaug[:,128:]=laug_ref[...]
    qa[...]=jnp.where(low,qf,zero).astype(bf16); qb[...]=jnp.where(low,zero,qf).astype(bf16)
    do=do_ref[...]; dof=do.astype(f32)
    doa[...]=jnp.where(low,dof,zero).astype(bf16); dob[...]=jnp.where(low,zero,dof).astype(bf16)
    doaug[:,:128]=do
    prod=dof*o_ref[...].astype(f32)
    r128=lax.broadcasted_iota(jnp.int32,(128,128),0)//64; c128=lane_iota(128,128)//64
    same=jnp.where(r128==c128,1.0,0.0).astype(bf16)
    hi,mid,lo=split3(prod)
    delta=dg(hi,same,NN)+dg(mid,same,NN)+dg(lo,same,NN)
    doaug[:,128:]=aug_lanes(-delta)
    dqacc[...]=jnp.zeros_like(dqacc)
    def pos(t):
        return pl.multiple_of(((t//per)^s)*blk+(t%per)*sub, sub)
    krow=lax.broadcasted_iota(jnp.int32,(sub,sub),0)
    qcol=lane_iota(sub,sub)
    def kblock(j,_):
        ko=pos(j)
        ksl=pl.ds(ko,sub)
        def step(qo,ok,dk,dv):
            qsl=pl.ds(qo,sub)
            qg=qaug[qsl,:]; dg_=doaug[qsl,:]
            s0=dg(kaug0[ksl,:],qg,NT); s1=dg(kaug1[ksl,:],qg,NT)
            e0=jnp.where(ok,jnp.exp2(s0*c),0.0); e1=jnp.where(ok,jnp.exp2(s1*c),0.0)
            dp0=dg(vaug0[ksl,:],dg_,NT); dp1=dg(vaug1[ksl,:],dg_,NT)
            ds0=(e0*dp0).astype(bf16); ds1=(e1*dp1).astype(bf16)
            dv=dv+dg(e0.astype(bf16),doa[qsl,:],NN)+dg(e1.astype(bf16),dob[qsl,:],NN)
            dk=dk+dg(ds0,qa[qsl,:],NN)+dg(ds1,qb[qsl,:],NN)
            dqacc[qsl,:]+=dg(ds0,ka[ksl,:],TN)+dg(ds1,kb[ksl,:],TN)
            return dk,dv
        st=start_ref[:,pl.ds(ko,sub)]-j*sub
        ok=(krow>=st)&(krow<=qcol)&((krow<nlive-j*sub)|(krow==qcol))
        z=jnp.zeros((sub,128),f32)
        dk,dv=step(ko,ok,z,z)
        def qblock(i,carry):
            dk,dv=carry
            qo=pos(i)
            st=start_ref[:,pl.ds(qo,sub)]-j*sub
            ok=(krow>=st)&(krow<nlive-j*sub)
            return step(qo,ok,dk,dv)
        dk,dv=lax.fori_loop(j+1,info[24+j],qblock,(dk,dv))
        dk_ref[ksl,:]=(dk*scale)
        dv_ref[ksl,:]=dv
        return 0
    lax.fori_loop(0,nsub,kblock,0)
    dq_ref[...]=(dqacc[...]*scale).astype(bf16)

def flash_bwd(info,q,laug,do,o,k,v,start_row,*,blk,sub,head_dim=64):
    T=q.shape[0]; pairs=q.shape[1]//128
    scale=head_dim**-0.5
    c=math.log2(math.e)*scale
    kern=functools.partial(bwd_kernel,blk,sub,c,scale)
    full=lambda n: pl.BlockSpec((T,n),lambda p,*_:(0,0))
    pair=pl.BlockSpec((T,128),lambda p,*_:(0,p))
    return pl.pallas_call(kern,
        grid_spec=pltpu.PrefetchScalarGridSpec(num_scalar_prefetch=1,grid=(pairs,),
            in_specs=[pair,pair,pair,pair,full(128),full(128),pl.BlockSpec((1,T),lambda p,*_:(0,0))],out_specs=[pair,pair,pair],
            scratch_shapes=[pltpu.VMEM((T,128),bf16)]*2+[pltpu.VMEM((T,256),bf16)]+[pltpu.VMEM((T,128),bf16)]*2+[pltpu.VMEM((T,256),bf16)]+[pltpu.VMEM((T,128),bf16)]*2+[pltpu.VMEM((T,256),bf16)]*4+[pltpu.VMEM((T,128),f32)]),
        out_shape=[jax.ShapeDtypeStruct((T,pairs*128),bf16),jax.ShapeDtypeStruct((T,pairs*128),f32),jax.ShapeDtypeStruct((T,pairs*128),f32)],
        compiler_params=pltpu.CompilerParams(dimension_semantics=("arbitrary",),vmem_limit_bytes=60*2**20),
        cost_estimate=tiny,
        name="flash_bwd")(info,q,laug,do,o,k,v,start_row)

def make_info(s,nlive,start,kvmap,pairs,sub):
    T=start.shape[0]; nsub=T//sub
    fk=jnp.min(start.reshape(nsub,sub),axis=1)//sub
    i=jnp.arange(nsub)
    sees=(fk[None,:]<=i[:,None])
    lastq=jnp.max(jnp.where(sees,i[None,:]+1,0),axis=1)
    info=jnp.zeros((40,),jnp.int32)
    info=info.at[0].set(s).at[1].set(nlive).at[2:2+pairs].set(kvmap).at[8:8+nsub].set(fk).at[24:24+nsub].set(lastq)
    return info


from jax.sharding import PartitionSpec as P

epsilon = 1e-06
rope_base = 10000.0


def perm_f(x, m):
    n = lax.axis_size("fsdp")
    return lax.ppermute(x, "fsdp", [(i, i ^ m) for i in range(n)])


def perm_s(x, m):
    n = lax.axis_size("sp")
    return lax.ppermute(x, "sp", [(i, i ^ m) for i in range(n)])


def after(x, *deps):
    return lax.optimization_barrier((x,) + deps)[0]


def gather_f(x, *deps):
    outer = lax.axis_size("fsdp") // 2
    x_z = after(x, *deps) if deps else x
    firsts = [x] + [perm_f(x_z, 2 * m) for m in range(1, outer)]
    pieces = []
    for first in firsts:
        pieces += [first, perm_f(first, 1)]
    return pieces


def gather_s(x):
    far = perm_s(x, 2)
    near = perm_s(x, 1)
    return [x, near, far, perm_s(far, 1)]


def place(pieces, me):
    out = jnp.zeros((len(pieces),) + pieces[0].shape, pieces[0].dtype)
    for r, piece in enumerate(pieces):
        out = lax.dynamic_update_index_in_dim(out, piece, me ^ r, 0)
    return out


def scatter_f(blocks, *deps):
    outer = blocks.shape[0] // 2
    me = lax.axis_index("fsdp")
    pairs = blocks.reshape((outer, 2) + blocks.shape[1:])
    mine = lax.dynamic_index_in_dim(pairs, me % 2, 1, keepdims=False)
    other = lax.dynamic_index_in_dim(pairs, 1 - me % 2, 1, keepdims=False)
    got = perm_f(other, 1)
    if deps:
        got = after(got, *deps)
    both = (mine.astype(f32) + got.astype(f32)).astype(bf16)
    at = me // 2
    total = lax.dynamic_index_in_dim(both, at, 0, keepdims=False).astype(f32)
    for m in range(1, outer):
        part = perm_f(lax.dynamic_index_in_dim(both, at ^ m, 0, keepdims=False), 2 * m)
        total = total + part.astype(f32)
    return total.astype(bf16)


def scatter_s(parts):
    got3 = perm_s(parts[3], 1)
    got1 = perm_s(parts[1], 1)
    far = perm_s((parts[2].astype(f32) + got3.astype(f32)).astype(bf16), 2)
    return parts[0].astype(f32) + got1.astype(f32) + far.astype(f32)


def half_swap(v):
    lane = lane_iota(*v.shape) % 64
    return jnp.where(lane < 32, pltpu.roll(v, 96, 1), pltpu.roll(v, 32, 1))


def head_sums(v):
    row = lax.broadcasted_iota(jnp.int32, (128, 128), 0) // 64
    col = lane_iota(128, 128) // 64
    same = jnp.where(row == col, 1.0, 0.0).astype(bf16)
    hi, mid, lo = split3(v)
    return dg(hi, same, NN) + dg(mid, same, NN) + dg(lo, same, NN)


def xor_small(a, b, bits=2):
    out = 0
    for i in range(bits):
        p = (a // (1 << i)) % 2
        q = (b // (1 << i)) % 2
        out = out + (p + q - 2 * p * q) * (1 << i)
    return out


class Ring:
    def __init__(self, own, slot, sems, base, outer, f, s):
        self.own, self.slot, self.sems, self.base = own, slot, sems, base
        self.outer, self.f, self.s = outer, f, s
        self.at, self.inner = f // 2, f % 2

    def copy(self, src, dst, send, recv, to):
        return pltpu.make_async_remote_copy(
            src, dst, self.sems.at[0, self.base + send], self.sems.at[1, self.base + recv],
            device_id=(to, self.s), device_id_type=pl.DeviceIdType.MESH,
        )

    def line(self, k, sign):
        n = self.outer
        lane = 0 if sign > 0 else n
        b = self.f - 2 * k * sign
        src = self.own if k == 0 else self.slot(b)
        return self.copy(src, self.slot(b), lane + k, lane + k + 1, self.f + 2 * sign)

    def line_wait(self, k, sign):
        n = self.outer
        lane = 0 if sign > 0 else n
        b = self.f - 2 * k * sign
        return self.copy(self.slot(b), self.slot(b), lane + k, lane + k, self.f + 2 * sign)

    def cross(self, k, sign):
        n = self.outer
        lane = 2 * n if sign > 0 else 3 * n
        b = self.f - 2 * k * sign
        src = self.own if k == 0 else self.slot(b)
        return self.copy(src, self.slot(b), lane + k, lane + k, self.f + 1 - 2 * self.inner)

    def cross_wait(self, k, sign):
        n = self.outer
        lane = 2 * n if sign > 0 else 3 * n
        b = self.f + 1 - 2 * self.inner - 2 * k * sign
        return self.copy(self.slot(b), self.slot(b), lane + k, lane + k, self.f + 1 - 2 * self.inner)

    def has(self, k, sign):
        return self.at >= k if sign > 0 else self.at + k <= self.outer - 1

    def onward(self, k, sign):
        more = self.at < self.outer - 1 if sign > 0 else self.at > 0
        return more if k == 0 else jnp.logical_and(more, self.has(k, sign))

    def start(self):
        for sign in (1, -1):
            pl.when(self.onward(0, sign))(lambda sign=sign: self.line(0, sign).start())

    def start_cross(self):
        self.cross(0, 1).start()

    def step(self, k):
        for sign in (1, -1):
            @pl.when(self.has(k, sign))
            def _(sign=sign):
                self.line_wait(k, sign).wait_recv()

                @pl.when(self.onward(0, sign))
                def _():
                    self.line(k, sign).start()

                self.cross(k, sign).start()

    def finish(self):
        for k in range(self.outer):
            for sign in (1, -1) if k else (1,):
                if k:
                    @pl.when(self.has(k, sign))
                    def _(k=k, sign=sign):
                        self.cross_wait(k, sign).wait_recv()
                        self.cross(k, sign).wait_send()
                else:
                    self.cross_wait(0, 1).wait_recv()
                    self.cross(0, 1).wait_send()
        for k in range(self.outer - 1):
            for sign in (1, -1):
                @pl.when(self.onward(k, sign))
                def _(k=k, sign=sign):
                    self.line(k, sign).wait_send()


def ring_sems(outer):
    return 4 * outer


def front_kernel(outer, ns, pairs, group, c, inv_log,
                 x_hbm, dy_hbm, small_ref, qkv_hbm, out_hbm, down_hbm, gu_hbm, gain_ref,
                 xh_hbm, dy_all, n2_all, w_d, w_gu, w_qkv_out, w_out_out, att_tok_out,
                 q_ref, k_ref, v_ref, raw_ref, cos_ref, sin_ref, o_ref, laug_ref, mid_ref, small_out,
                 xv, wq, ow, smalls, start_col, att_in, nv, ka, kb, ra, rb, ral, rbl,
                 rsem, tsem, lsem):
    f, s = lax.axis_index("fsdp"), lax.axis_index("sp")
    nf = 2 * outer
    core = s % 2
    near, far = s + 1 - 2 * core, s + 2 - 4 * (s // 2)
    diag = far + 1 - 2 * core
    at, inner = f // 2, f % 2
    blk, width = x_hbm.shape
    T = ns * blk
    q_cols = pairs * 128
    drows = qkv_hbm.shape[0]
    quarter = out_hbm.shape[0]

    barrier = pltpu.get_barrier_semaphore()

    def greet(ff, ss):
        pl.semaphore_signal(barrier, inc=1, device_id=(ff, ss), device_id_type=pl.DeviceIdType.MESH)

    greet(f, near)
    greet(f, far)
    greet(f, diag)
    greet(f + 1 - 2 * inner, s)
    pl.when(at < outer - 1)(lambda: greet(f + 2, s))
    pl.when(at > 0)(lambda: greet(f - 2, s))
    middle_of_line = jnp.logical_and(at > 0, at < outer - 1)
    pl.when(middle_of_line)(lambda: pl.semaphore_wait(barrier, 6))
    pl.when(jnp.logical_not(middle_of_line))(lambda: pl.semaphore_wait(barrier, 5))

    def send(src, dst, n, to):
        return pltpu.make_async_remote_copy(
            src, dst, tsem.at[0, n], tsem.at[1, n], device_id=(f, to), device_id_type=pl.DeviceIdType.MESH
        )

    def keep(src, dst, n):
        return pltpu.make_async_copy(src, dst, lsem.at[n])

    per = ring_sems(outer)
    qkv = Ring(qkv_hbm, lambda b: wq.at[pl.ds(pl.multiple_of(b * drows, drows), drows)], rsem, 0, outer, f, s)
    out = Ring(out_hbm, lambda b: ow.at[b, s], rsem, per, outer, f, s)
    down = Ring(down_hbm, lambda b: w_d.at[b], rsem, 2 * per, outer, f, s)
    gate = Ring(gu_hbm.at[0], lambda b: w_gu.at[0, b], rsem, 3 * per, outer, f, s)
    up = Ring(gu_hbm.at[1], lambda b: w_gu.at[1, b], rsem, 4 * per, outer, f, s)

    def triple(base, own, slot):
        return (
            send(own, slot(1), base, near), send(own, slot(2), base + 1, far), send(slot(2), slot(3), base + 2, near),
        )

    small_t = triple(0, small_ref, lambda r: smalls.at[r])
    tok_t = triple(3, x_hbm, lambda r: xv.at[r])
    dy_t = triple(9, dy_hbm, lambda r: dy_all.at[r])
    small_t[0].start()
    small_t[1].start()
    tok_t[1].start()
    tok_t[0].start()
    load_x = keep(x_hbm, xv.at[0], 0)
    load_x.start()
    load_q = keep(qkv_hbm, wq.at[pl.ds(pl.multiple_of(f * drows, drows), drows)], 1)
    load_q.start()
    load_o = keep(out_hbm, ow.at[f, s], 2)
    load_o.start()
    qkv.start()
    qkv.start_cross()
    out.start()
    out.start_cross()
    smalls[0] = small_ref[...]
    small_t[1].wait_recv()
    small_t[2].start()
    for k in range(1, outer):
        qkv.step(k)
        out.step(k)
    down.start()
    down.start_cross()
    gate.start()
    gate.start_cross()

    small_t[0].wait_recv()
    small_t[2].wait_recv()
    half = 32
    lane = lane_iota(blk, 128)
    freq = jnp.exp((lane % half).astype(f32) * inv_log)
    sign = jnp.where(lane % 64 < half, -1.0, 1.0)
    row = lax.broadcasted_iota(jnp.int32, (blk, 1), 0)
    live = jnp.zeros((1, 1), f32)
    for r in range(ns):
        ints = smalls[r]
        small_out[r] = ints
        col = jnp.transpose(ints)[:, 0:1]
        angle = col * freq
        cos_ref[r] = jnp.cos(angle)
        sin_ref[r] = jnp.sin(angle) * sign
        t = xor_small(s, r)
        start_col[r] = t * blk + row - col.astype(jnp.int32)
        live = live + jnp.sum(ints[1:2, :], axis=1, keepdims=True)
    n_live = live.astype(jnp.int32)

    def project_block(r):
        tile = min(256, blk)

        @pl.loop(0, blk // tile)
        def _(i):
            rows = pl.ds(pl.multiple_of(i * tile, tile), tile)
            x = xv[r, rows, :].astype(f32)
            scale = lax.rsqrt(jnp.mean(x * x, axis=-1, keepdims=True) + epsilon)
            xh = (x * scale).astype(bf16)
            xv[r, rows, :] = xh
            raw = dg(xh, wq[...], NN)
            cosine, sine = cos_ref[r, rows, :], sin_ref[r, rows, :]
            to = pl.ds(pl.multiple_of(r * blk + i * tile, tile), tile)
            for p in range(pairs + 1):
                part = raw[:, 128 * p : 128 * (p + 1)]
                raw_ref[to, 128 * p : 128 * (p + 1)] = part
                inv = lax.rsqrt(head_sums(part * part) * (1.0 / 64) + epsilon)
                normal = part * inv * gain_ref[(0 if p < pairs else 1) : (1 if p < pairs else 2), :]
                turned = (normal * cosine + half_swap(normal) * sine).astype(bf16)
                if p < pairs:
                    q_ref[to, 128 * p : 128 * (p + 1)] = turned
                else:
                    k_ref[to, :] = turned
            v_ref[to, :] = raw[:, 128 * (pairs + 1) :].astype(bf16)

    load_x.wait()
    load_q.wait()
    load_o.wait()
    qkv.finish()
    out.finish()
    out_t = (
        send(ow.at[:, s], ow.at[:, s], 6, near),
        send(ow.at[:, s], ow.at[:, s], 7, far),
        send(ow.at[:, far], ow.at[:, far], 8, near),
    )
    out_w = (
        send(ow.at[:, near], ow.at[:, near], 6, near),
        send(ow.at[:, far], ow.at[:, far], 7, far),
        send(ow.at[:, diag], ow.at[:, diag], 8, near),
    )
    out_t[0].start()
    out_t[1].start()
    dy_t[1].start()
    dy_t[0].start()
    project_block(0)
    keep(xv.at[0], xh_hbm.at[0], 0).start()
    tok_t[1].wait_recv()
    tok_t[2].start()
    tok_t[0].wait_recv()
    down.step(1)
    project_block(1)
    keep(xv.at[1], xh_hbm.at[1], 1).start()
    tok_t[2].wait_send()
    project_block(2)
    keep(xv.at[2], xh_hbm.at[2], 2).start()
    tok_t[2].wait_recv()
    up.start()
    up.start_cross()
    project_block(3)
    keep(xv.at[3], xh_hbm.at[3], 3).start()
    tok_t[0].wait_send()
    tok_t[1].wait_send()

    low = lane_iota(blk, 128) < 64
    row_b = lax.broadcasted_iota(jnp.int32, (blk, 128), 0)

    def pos(t):
        return pl.multiple_of(xor_small(t, s) * blk, blk)

    def prepare(p):
        kv = (pairs * 2 * s + 2 * p) // group - (pairs * 2 * s) // group
        first = kv == 0
        one_a = jnp.where(low, 1.0, 0.0)
        one_b = 1.0 - one_a
        for r in range(ns):
            here = slice(r * blk, (r + 1) * blk)
            kk, vv = k_ref[here, :].astype(f32), v_ref[here, :].astype(f32)
            ksw, vsw = pltpu.roll(kk, 64, 1), pltpu.roll(vv, 64, 1)
            k0, k1 = jnp.where(first, kk, ksw), jnp.where(first, ksw, kk)
            v0, v1 = jnp.where(first, vv, vsw), jnp.where(first, vsw, vv)
            ka[here, :] = jnp.where(low, k0, 0.0).astype(bf16)
            kb[here, :] = jnp.where(low, 0.0, k1).astype(bf16)
            va, vb = jnp.where(low, v0, 0.0), jnp.where(low, 0.0, v1)
            seen = row_b < n_live - xor_small(s, r) * blk
            ra[here, :128], ra[here, 128:] = va.astype(bf16), one_a.astype(bf16)
            rb[here, :128], rb[here, 128:] = vb.astype(bf16), one_b.astype(bf16)
            ral[here, :128] = jnp.where(seen, va, 0.0).astype(bf16)
            ral[here, 128:] = jnp.where(seen, one_a, 0.0).astype(bf16)
            rbl[here, :128] = jnp.where(seen, vb, 0.0).astype(bf16)
            rbl[here, 128:] = jnp.where(seen, one_b, 0.0).astype(bf16)

    kcol = lane_iota(blk, blk)
    qrow = lax.broadcasted_iota(jnp.int32, (blk, blk), 0)

    def query_block(p, i):
        qo = pos(i)
        here = pl.ds(qo, blk)
        lanes = slice(128 * p, 128 * (p + 1))
        q = q_ref[here, lanes]
        st = start_col[xor_small(i, s)]
        ok = (kcol >= st - i * blk) & (kcol <= qrow) & ((kcol < n_live - i * blk) | (kcol == qrow))
        p0 = jnp.where(ok, jnp.exp2(dg(q, ka[here, :], NT) * c), 0.0).astype(bf16)
        p1 = jnp.where(ok, jnp.exp2(dg(q, kb[here, :], NT) * c), 0.0).astype(bf16)
        acc = dg(p0, ra[here, :], NN) + dg(p1, rb[here, :], NN)

        def key_block(j, acc):
            there = pl.ds(pos(j), blk)
            ok = kcol >= (st - j * blk)
            p0 = jnp.where(ok, jnp.exp2(dg(q, ka[there, :], NT) * c), 0.0).astype(bf16)
            p1 = jnp.where(ok, jnp.exp2(dg(q, kb[there, :], NT) * c), 0.0).astype(bf16)
            return acc + dg(p0, ral[there, :], NN) + dg(p1, rbl[there, :], NN)

        acc = lax.fori_loop(0, i, key_block, acc)
        total = acc[:, 128:]
        o_ref[here, lanes] = (acc[:, :128] / total).astype(bf16)
        laug_ref[here, lanes] = aug_lanes(jnp.log(total) * (-8.0))

    jobs = [
        lambda: (gate.step(1), out_t[0].wait_send()),
        lambda: (down.step(2), out_w[1].wait_recv(), out_t[2].start()),
        lambda: gate.step(2),
        lambda: (down.step(3), up.step(1)) if outer > 3 else None,
        lambda: gate.step(3) if outer > 3 else None,
        lambda: up.step(2) if outer > 3 else None,
    ]
    for p in range(pairs):
        prepare(p)
        pl.loop(0, ns - 1)(lambda i, p=p: query_block(p, i))
        if 2 * p < len(jobs):
            jobs[2 * p]()
        query_block(p, ns - 1)
        if 2 * p + 1 < len(jobs):
            jobs[2 * p + 1]()
    for job in jobs[2 * pairs :]:
        job()
    for k in range(4, outer):
        down.step(k)
        gate.step(k)

    att_t = [
        send(o_ref.at[pl.ds(r * blk, blk)], att_in.at[r], 11 + r, to) for r, to in ((1, near), (2, far), (3, diag))
    ]
    att_t[1].start()
    att_t[2].start()
    att_t[0].start()
    for n in range(4):
        keep(xv.at[n], xh_hbm.at[n], n).wait()
    reload = keep(x_hbm, xv.at[0], 0)
    reload.start()
    out_w[0].wait_recv()
    out_w[2].wait_recv()
    out_t[1].wait_send()
    out_t[2].wait_send()
    att_in[0] = o_ref[pl.ds(0, blk), :]
    reload.wait()
    for a in att_t:
        a.wait_recv()
    tile = 512
    shards = nf // ns
    squares = jnp.zeros((blk, 1), f32)
    for n in range(width // tile):
        cols = slice(n * tile, (n + 1) * tile)
        acc = xv[0, :, cols].astype(f32)
        for r in range(ns):
            t = xor_small(s, r)
            w = ow[pl.ds(t * shards, shards), :, :, cols].reshape(q_cols, tile)
            acc = acc + dg(att_in[r], w, NN)
        mid_ref[:, cols] = acc
        squares = squares + jnp.sum(acc * acc, axis=-1, keepdims=True)
    inv = lax.rsqrt(squares * (1.0 / width) + epsilon)
    for n in range(width // tile):
        cols = slice(n * tile, (n + 1) * tile)
        nv[:, cols] = (mid_ref[:, cols] * inv).astype(bf16)
    n2_t = triple(15, nv, lambda r: n2_all.at[r])
    n2_t[1].start()
    n2_t[0].start()
    keeps = [keep(nv, n2_all.at[0], 0), keep(wq, w_qkv_out, 1)]
    for r in range(ns):
        part = ow.at[pl.ds(xor_small(s, r) * shards, shards)]
        keeps.append(keep(part, w_out_out.at[r], 2 + r))
        keeps.append(keep(att_in.at[r], att_tok_out.at[:, pl.ds(r * q_cols, q_cols)], 2 + ns + r))
    for a in keeps:
        a.start()
    for k in range(3, outer):
        up.step(k)
    if outer <= 3:
        for k in range(2, outer):
            up.step(k)
    down.finish()
    gate.finish()
    dy_t[1].wait_recv()
    dy_t[2].start()
    dy_t[0].wait()
    dy_t[1].wait_send()
    dy_t[2].wait()
    small_t[0].wait_send()
    small_t[1].wait_send()
    small_t[2].wait_send()
    for a in att_t:
        a.wait_send()
    n2_t[1].wait_recv()
    n2_t[2].start()
    up.finish()
    n2_t[2].wait()
    n2_t[0].wait()
    n2_t[1].wait_send()
    for a in keeps:
        a.wait()


def front_call(x, dy, small, qkv_mine, out_mine, down_mine, gu_mine, gains, nf, ns, group, head):
    outer = nf // 2
    blk, width = x.shape
    T = blk * ns
    cols = qkv_mine.shape[1]
    pairs = cols // 128 - 2
    q_cols = pairs * 128
    hbm, vmem = pl.BlockSpec(memory_space=pl.ANY), pl.BlockSpec(memory_space=pltpu.VMEM)
    c = math.log2(math.e) * head**-0.5
    inv_log = -2.0 / head * math.log(rope_base)
    S = jax.ShapeDtypeStruct
    quarter = out_mine.shape[0]
    return pl.pallas_call(
        functools.partial(front_kernel, outer, ns, pairs, group, c, inv_log),
        in_specs=[hbm, hbm, vmem, hbm, hbm, hbm, hbm, vmem],
        out_specs=[hbm] * 8 + [vmem] * 10,
        out_shape=[
            S((ns, blk, width), bf16), S((ns, blk, width), bf16), S((ns, blk, width), bf16),
            S((nf,) + down_mine.shape, bf16), S((2, nf) + gu_mine.shape[1:], bf16),
            S((width, cols), bf16), S((ns, nf // ns, ns, quarter, width), bf16), S((blk, ns * q_cols), bf16),
            S((T, q_cols), bf16), S((T, 128), bf16), S((T, 128), bf16), S((T, q_cols + 128), f32),
            S((ns, blk, 128), f32), S((ns, blk, 128), f32), S((T, q_cols), bf16), S((T, q_cols), bf16),
            S((blk, width), f32), S((ns,) + small.shape, f32),
        ],
        scratch_shapes=[
            pltpu.VMEM((ns, blk, width), bf16), pltpu.VMEM((width, cols), bf16),
            pltpu.VMEM((nf, ns, quarter, width), bf16), pltpu.VMEM((ns,) + small.shape, f32),
            pltpu.VMEM((ns, blk, 1), jnp.int32), pltpu.VMEM((ns, blk, q_cols), bf16), pltpu.VMEM((blk, width), bf16),
        ]
        + [pltpu.VMEM((T, 128), bf16)] * 2
        + [pltpu.VMEM((T, 256), bf16)] * 4
        + [
            pltpu.SemaphoreType.DMA((2, 5 * ring_sems(outer))), pltpu.SemaphoreType.DMA((2, 18)),
            pltpu.SemaphoreType.DMA((2 + 2 * ns,)),
        ],
        compiler_params=pltpu.CompilerParams(
            collective_id=0, has_side_effects=True, vmem_limit_bytes=62 * 2**20
        ),
        cost_estimate=tiny,
        name="front",
    )(x, dy, small, qkv_mine, out_mine, down_mine, gu_mine, gains)


def ffn_kernel(count, n_in, *refs):
    n2_ref, dy_ref, wg_ref, wu_ref, wd_ref = refs[:5]
    hid_ref, dg_ref, du_ref, dn_ref, acc = refs[n_in:]
    step = pl.program_id(0)
    wg, wu, wd = wg_ref[0], wu_ref[0], wd_ref[...]
    for n in range(count):
        n2, dy = n2_ref[n], dy_ref[n]
        gate = dg(n2, wg, NN)
        up = dg(n2, wu, NN)
        dhid = dg(dy, wd, NT)
        sig = jax.nn.sigmoid(gate)
        act = gate * sig
        hid_ref[n] = (act * up).astype(bf16)
        dup = (dhid * act).astype(bf16)
        dgate = (dhid * up * (sig * (1.0 + gate * (1.0 - sig)))).astype(bf16)
        dg_ref[n] = dgate
        du_ref[n] = dup
        grad = dg(dgate, wg, NT) + dg(dup, wu, NT)

        @pl.when(step == 0)
        def _():
            acc[n] = grad

        @pl.when(step > 0)
        def _():
            acc[n] += grad

        @pl.when(step == pl.num_programs(0) - 1)
        def _():
            dn_ref[n] = acc[n].astype(bf16)


def ffn_call(chunk, chunks, n2_all, dy_all, w_gu, w_d, earlier, tile=256):
    members, rows, width = n2_all.shape
    count = members // chunks
    units = w_d.shape[0]
    n_in = 5 + len(earlier)
    once = pl.Buffered(1)
    big = jax.ShapeDtypeStruct((members, rows, units), bf16)
    return pl.pallas_call(
        functools.partial(ffn_kernel, count, n_in),
        grid=(units // tile,),
        in_specs=[pl.BlockSpec((count, rows, width), lambda j: (chunk, 0, 0), pipeline_mode=once)] * 2
        + [
            pl.BlockSpec((1, width, tile), lambda j: (0, 0, j)),
            pl.BlockSpec((1, width, tile), lambda j: (1, 0, j)),
            pl.BlockSpec((tile, width), lambda j: (j, 0)),
        ]
        + [pl.BlockSpec(memory_space=pl.ANY)] * len(earlier),
        out_specs=[pl.BlockSpec((count, rows, tile), lambda j: (chunk, 0, j))] * 3
        + [pl.BlockSpec((count, rows, width), lambda j: (0, 0, 0))],
        out_shape=[big, big, big] + [jax.ShapeDtypeStruct((count, rows, width), bf16)],
        scratch_shapes=[pltpu.VMEM((count, rows, width), f32)],
        input_output_aliases={5 + i: i for i in range(len(earlier))},
        compiler_params=pltpu.CompilerParams(vmem_limit_bytes=62 * 2**20),
        cost_estimate=tiny,
        name="ffn",
    )(n2_all, dy_all, w_gu, w_gu, w_d, *earlier)


def back_kernel(pairs, info, dq_ref, dk_ref, dv_ref, raw_ref, cos_ref, sin_ref, gain_ref, w_ref, dqkv_ref, dn_ref, dgain_ref):
    odd = info[0] % 2 == 1
    rows = dq_ref.shape[0]
    low = lane_iota(rows, 128) < 64

    def fold(ref):
        sums = []
        for p in range(pairs):
            part = ref[:, 128 * p : 128 * (p + 1)]
            sums.append(part + pltpu.roll(part, 64, 1))
        first, second = jnp.zeros_like(sums[0]), jnp.zeros_like(sums[0])
        for p in range(pairs):
            at_first = info[2 + p] == 0
            first = first + jnp.where(at_first, sums[p], 0.0)
            second = second + jnp.where(at_first, 0.0, sums[p])
        return jnp.where(low, first, second)

    @pl.when(pl.program_id(0) == 0)
    def _():
        dgain_ref[...] = jnp.zeros_like(dgain_ref)

    cosine, sine = cos_ref[...], sin_ref[...]
    outs = []
    sums = [jnp.zeros((8, 128), f32), jnp.zeros((8, 128), f32)]
    for p in range(pairs + 1):
        which = 0 if p < pairs else 1
        if p < pairs:
            grad = dq_ref[:, 128 * p : 128 * (p + 1)].astype(f32)
        else:
            grad = fold(dk_ref).astype(bf16).astype(f32)
        raw = raw_ref[:, 128 * p : 128 * (p + 1)]
        inv = lax.rsqrt(head_sums(raw * raw) * (1.0 / 64) + epsilon)
        normal = raw * inv
        grad = grad * cosine - half_swap(grad) * sine
        sums[which] = sums[which] + jnp.sum((grad * normal).reshape(rows // 8, 8, 128), axis=0)
        grad = grad * gain_ref[which : which + 1, :]
        mean = head_sums(grad * normal) * (1.0 / 64)
        outs.append((inv * (grad - normal * mean)).astype(bf16))
    outs.append(fold(dv_ref).astype(bf16))
    for p, out in enumerate(outs):
        dqkv_ref[:, 128 * p : 128 * (p + 1)] = out
    dgain_ref[0] += sums[0]
    dgain_ref[1] += sums[1]
    dn_ref[...] = dg(dqkv_ref[...], w_ref[...], NT).astype(bf16)


def back_call(first, count, blk, info, dq, dk, dv, raw, cosine, sine, gains, weight, earlier, tile=256):
    rows = dq.shape[0]
    width, cols = weight.shape
    pairs = cols // 128 - 2
    per = blk // tile
    n = count * per
    base = first * per

    def spec(w):
        return pl.BlockSpec((tile, w), lambda i, *_: (base + i, 0))

    def body(*refs):
        back_kernel(pairs, *refs[:9], *refs[9 + len(earlier) :])

    return pl.pallas_call(
        body,
        grid_spec=pltpu.PrefetchScalarGridSpec(
            num_scalar_prefetch=1,
            grid=(n,),
            in_specs=[
                spec(pairs * 128),
                spec(pairs * 128),
                spec(pairs * 128),
                spec((pairs + 1) * 128),
                spec(128),
                spec(128),
                pl.BlockSpec((8, 128), lambda i, *_: (0, 0)),
                pl.BlockSpec(weight.shape, lambda i, *_: (0, 0)),
            ]
            + [pl.BlockSpec(memory_space=pl.ANY)] * len(earlier),
            out_specs=[
                spec(cols),
                pl.BlockSpec((tile, width), lambda i, *_: (i, 0)),
                pl.BlockSpec((2, 8, 128), lambda i, *_: (0, 0, 0)),
            ],
        ),
        out_shape=[
            jax.ShapeDtypeStruct((rows, cols), bf16),
            jax.ShapeDtypeStruct((count * blk, width), bf16),
            jax.ShapeDtypeStruct((2, 8, 128), f32),
        ],
        input_output_aliases={9 + i: i for i in range(len(earlier))},
        compiler_params=pltpu.CompilerParams(vmem_limit_bytes=60 * 2**20),
        cost_estimate=tiny,
        name="qkv_back",
    )(info, dq, dk, dv, raw, cosine, sine, gains, weight, *earlier)


def pick_kernel(members, shards, shard, unit, info, gain_ref, wg_ref, wu_ref, out_ref):
    out_ref[...] = jnp.zeros_like(out_ref)
    for k in range(members):
        width = min(unit, shard - k * unit)

        @pl.when(info[0] == k)
        def _():
            for n, ref in enumerate((wg_ref, wu_ref)):
                for j in range(shards):
                    part = ref[:, j * shard + k * unit : j * shard + k * unit + width].astype(f32)
                    out_ref[n, :, j * unit : j * unit + width] = (part * gain_ref[...]).astype(bf16)


def pick_call(info, gain, w_gate, w_up, members, shards, shard, unit):
    rows, cols = w_gate.shape
    tile = min(64, rows)
    return pl.pallas_call(
        functools.partial(pick_kernel, members, shards, shard, unit),
        grid_spec=pltpu.PrefetchScalarGridSpec(
            num_scalar_prefetch=1,
            grid=(rows // tile,),
            in_specs=[pl.BlockSpec((tile, 1), lambda i, *_: (i, 0))]
            + [pl.BlockSpec((tile, cols), lambda i, *_: (i, 0))] * 2,
            out_specs=pl.BlockSpec((2, tile, shards * unit), lambda i, *_: (0, i, 0)),
        ),
        out_shape=jax.ShapeDtypeStruct((2, rows, shards * unit), bf16),
        compiler_params=pltpu.CompilerParams(vmem_limit_bytes=60 * 2**20),
        name="pick_units",
    )(info, gain, w_gate, w_up)


def join_kernel(members, shards, shard, unit, gain_ref, m_ref, w_ref, out_ref, sum_ref):
    for k in range(members):
        width = min(unit, shard - k * unit)
        for j in range(shards):
            part = m_ref[k, :, j * unit : j * unit + width].astype(f32)
            out_ref[:, j * shard + k * unit : j * shard + k * unit + width] = part
    full = out_ref[...]
    sum_ref[...] = jnp.broadcast_to(
        jnp.sum(full * w_ref[...].astype(f32), axis=-1, keepdims=True), sum_ref.shape
    )
    out_ref[...] = full * gain_ref[...]


def join_call(gain, stacked, weight, members, shards, shard, unit):
    rows, cols = weight.shape
    tile = min(64, rows)
    return pl.pallas_call(
        functools.partial(join_kernel, members, shards, shard, unit),
        grid=(rows // tile,),
        in_specs=[
            pl.BlockSpec((tile, 1), lambda i: (i, 0)),
            pl.BlockSpec((members, tile, shards * unit), lambda i: (0, i, 0)),
            pl.BlockSpec((tile, cols), lambda i: (i, 0)),
        ],
        out_specs=[
            pl.BlockSpec((tile, cols), lambda i: (i, 0)),
            pl.BlockSpec((tile, 128), lambda i: (i, 0)),
        ],
        out_shape=[
            jax.ShapeDtypeStruct((rows, cols), f32),
            jax.ShapeDtypeStruct((rows, 128), f32),
        ],
        compiler_params=pltpu.CompilerParams(vmem_limit_bytes=60 * 2**20),
        name="join_units",
    )(gain, stacked, weight)


def dot_bf(a, b, dims):
    return dg(a, b, dims).astype(bf16)


def local(
    tokens, seg_ids, pad_mask, positions, attn_gain, w_query, w_key, w_value, query_gain,
    key_gain, w_out, ffn_gain, w_gate, w_up, w_down, cotangent,
):
    nf, ns = lax.axis_size("fsdp"), lax.axis_size("sp")
    f, s = lax.axis_index("fsdp"), lax.axis_index("sp")
    seq_count, blk, width = tokens.shape
    assert seq_count == 1 and ns == 4
    length = blk * ns
    head = query_gain.shape[0]
    q_heads, kv_heads = w_query.shape[1] // head, w_key.shape[1] // head
    group = q_heads // kv_heads
    q_local = q_heads // ns
    kv_base = [(q_local * k) // group for k in range(ns)]
    pairs = q_local // 2
    q_cols = q_local * head
    kv_map = jnp.array(
        [[(q_local * k + 2 * p) // group - kv_base[k] for p in range(pairs)] for k in range(ns)],
        jnp.int32,
    )[s]
    base = jnp.array(kv_base, jnp.int32)[s] * head
    shard = w_down.shape[0]
    unit = -(-(-(-shard // ns)) // 16) * 16
    units = unit * nf
    out_rows = w_out.shape[0]
    quarter = out_rows // ns
    sub = 512

    x = tokens[0]
    dy = cotangent[0]
    gain_one = attn_gain.astype(f32)[:, None]
    gain_two = ffn_gain.astype(f32)[:, None]

    kv_cols = 2 * head
    mine = jnp.concatenate(
        [
            lax.dynamic_slice_in_dim(w_query, s * q_cols, q_cols, 1),
            lax.dynamic_slice_in_dim(w_key, base, kv_cols, 1),
            lax.dynamic_slice_in_dim(w_value, base, kv_cols, 1),
        ],
        axis=1,
    )
    mine = (mine.astype(f32) * gain_one).astype(bf16)
    out_mine = lax.dynamic_slice_in_dim(w_out, s * quarter, quarter, 0)
    down_pad = jnp.concatenate([w_down, jnp.zeros((unit * ns - shard, width), bf16)])
    down_mine = lax.dynamic_slice_in_dim(down_pad, s * unit, unit, 0)
    one_info = jnp.reshape(s, (1,)).astype(jnp.int32)
    gu_mine = pick_call(one_info, gain_two, w_gate, w_up, ns, nf, shard, unit)
    small = jnp.concatenate(
        [positions.astype(f32), pad_mask.astype(f32), jnp.zeros((6, blk), f32)]
    )
    gains = jnp.concatenate(
        [
            jnp.tile(query_gain.astype(f32), 2)[None],
            jnp.tile(key_gain.astype(f32), 2)[None],
            jnp.zeros((6, 2 * head), f32),
        ]
    )
    (
        xh, dy_all, n2_all, w_d, w_gu, w_qkv, w_out_rel, att, q, k, v, raw, cosine, sine,
        attended, laug, middle, small_all,
    ) = front_call(x, dy, small, mine, out_mine, down_mine, gu_mine, gains, nf, ns, group, head)
    xh = xh.reshape(length, width)
    dy_all = lax.dynamic_update_index_in_dim(dy_all, dy, 0, 0)
    w_d = lax.dynamic_update_index_in_dim(w_d, down_mine, f, 0).reshape(units, width)
    w_gu = lax.dynamic_update_slice_in_dim(w_gu, gu_mine[:, None], f, 1).reshape(2, width, units)
    w_out_rel = w_out_rel.reshape(ns * q_cols, width)
    pos_rel = small_all[:, 0].astype(jnp.int32)
    n_live = jnp.sum(small_all[:, 1]).astype(jnp.int32)
    true_block = s ^ jnp.arange(ns)
    start_rel = true_block[:, None] * blk + jnp.arange(blk)[None] - pos_rel
    start_true = place([start_rel[r] for r in range(ns)], s).reshape(length)
    info = make_info(s, n_live, start_true, kv_map, pairs, sub)
    start_rel = start_rel.reshape(length)
    xf = x.astype(f32)
    inv_two = lax.rsqrt(jnp.mean(middle * middle, axis=-1, keepdims=True) + epsilon)

    first = ffn_call(0, 2, n2_all, dy_all, w_gu, w_d, [])
    second = ffn_call(1, 2, n2_all, dy_all, w_gu, w_d, first[:3])
    hidden, dgate, dup = [a.reshape(length, -1) for a in second[:3]]
    n2_all = n2_all.reshape(length, width)
    dn2 = [first[3][0], first[3][1], second[3][0], second[3][1]]
    dn2_own = scatter_s(dn2)
    hat_two = middle * inv_two
    dmiddle = dy.astype(f32) + inv_two * (
        dn2_own - hat_two * jnp.mean(dn2_own * hat_two, axis=-1, keepdims=True)
    )
    dmid = dmiddle.astype(bf16)
    datt = dot_bf(dmid, w_out_rel, NT)
    datt = [datt[:, :q_cols]] + [
        perm_s(datt[:, r * q_cols : (r + 1) * q_cols], r) for r in range(1, ns)
    ]
    datt = jnp.concatenate(datt)

    dy_all = dy_all.reshape(length, width)
    grad_d = dot_bf(hidden, dy_all, TN).reshape(nf, unit, width)
    grad_g = dot_bf(n2_all, dgate, TN).reshape(nf, width // nf, units)
    grad_u = dot_bf(n2_all, dup, TN).reshape(nf, width // nf, units)
    out_part_sum = dot_bf(hidden, w_d, NN).reshape(ns, blk, width)
    sum_d = gather_s(scatter_f(grad_d, dmid))
    sum_g = gather_s(scatter_f(grad_g, datt))
    sum_u = gather_s(scatter_f(grad_u, datt))
    out_part_sum = after(out_part_sum, dmid)
    layer_out = (middle + scatter_s([out_part_sum[r] for r in range(ns)])).astype(bf16)
    w_down_grad = place(sum_d, s).reshape(ns * unit, width)[:shard].astype(f32)
    w_gate_grad, gate_sum = join_call(gain_two, place(sum_g, s), w_gate, ns, nf, shard, unit)
    w_up_grad, up_sum = join_call(gain_two, place(sum_u, s), w_up, ns, nf, shard, unit)
    ffn_gain_grad = (gate_sum + up_sum)[:, 0]

    grad_o = dot_bf(att, dmid, TN).reshape(ns, q_cols, width)
    grad_o = jnp.stack(
        [lax.dynamic_index_in_dim(grad_o, s ^ t, 0, keepdims=False) for t in range(ns)]
    ).reshape(nf, ns, quarter, width)
    parts = [lax.dynamic_index_in_dim(grad_o, s ^ r, 1, keepdims=False) for r in range(ns)]
    sum_o = gather_s(scatter_f(scatter_s(parts).astype(bf16)))
    w_out_grad = place(sum_o, s).reshape(out_rows, width).astype(f32)

    dq, dk, dv = flash_bwd(
        info, q, laug, datt, attended, k, v, start_rel[None, :], blk=blk, sub=sub
    )
    cos2, sin2 = cosine.reshape(length, -1), sine.reshape(length, -1)
    dqkv, dn_far, dgain_far = back_call(
        2, 2, blk, info, dq, dk, dv, raw, cos2, sin2, gains, w_qkv, []
    )
    dqkv, dn_near, dgain_near = back_call(
        0, 2, blk, info, dq, dk, dv, raw, cos2, sin2, gains, w_qkv, [dqkv]
    )
    dn_own = scatter_s([dn_near[:blk], dn_near[blk:], dn_far[:blk], dn_far[blk:]])
    inv_one = lax.rsqrt(jnp.mean(xf * xf, axis=-1, keepdims=True) + epsilon)
    hat_one = xf * inv_one
    tokens_grad = (
        dmiddle + inv_one * (dn_own - hat_one * jnp.mean(dn_own * hat_one, axis=-1, keepdims=True))
    ).astype(bf16)

    dgain = jnp.sum(dgain_far + dgain_near, axis=1)
    dgain = jnp.pad((dgain[:, :head] + dgain[:, head:]).reshape(1, -1), ((0, 7), (0, 0)))
    m = 1
    while m < ns:
        dgain = dgain + perm_s(dgain, m)
        m *= 2
    m = 1
    while m < nf:
        dgain = dgain + perm_f(dgain, m)
        m *= 2
    query_gain_grad, key_gain_grad = dgain[0, :head], dgain[0, head:]

    grad_qkv = dot_bf(xh, dqkv, TN).reshape(nf, width // nf, -1)
    sum_qkv = place(gather_s(scatter_f(grad_qkv)), s).astype(f32)
    m_query = jnp.concatenate([sum_qkv[k][:, :q_cols] for k in range(ns)], axis=1)

    def heads_of(offset):
        cols = []
        for h in range(kv_heads):
            total = 0.0
            for k in range(ns):
                if 0 <= h - kv_base[k] < 2:
                    at = offset + (h - kv_base[k]) * head
                    total = total + sum_qkv[k][:, at : at + head]
            cols.append(total)
        return jnp.concatenate(cols, axis=1)

    m_key, m_value = heads_of(q_cols), heads_of(q_cols + kv_cols)
    attn_gain_grad = (
        jnp.sum(m_query * w_query.astype(f32), axis=1)
        + jnp.sum(m_key * w_key.astype(f32), axis=1)
        + jnp.sum(m_value * w_value.astype(f32), axis=1)
    )
    return (
        layer_out[None], tokens_grad[None], attn_gain_grad, m_query * gain_one, m_key * gain_one,
        m_value * gain_one, query_gain_grad, key_gain_grad, w_out_grad, ffn_gain_grad,
        w_gate_grad, w_up_grad, w_down_grad,
    )


def solution(mesh):
    row, vec = P("fsdp", None), P("fsdp")
    tok, ids = P("fsdp", "sp", None), P("fsdp", "sp")
    in_specs = (tok, ids, ids, ids, vec, row, row, row, P(), P(), row, vec, row, row, row, tok)
    out_specs = (tok, tok, vec, row, row, row, P(), P(), row, vec, row, row, row)
    return jax.shard_map(local, mesh=mesh, in_specs=in_specs, out_specs=out_specs, check_vma=False)
```

```python
import functools, math
import jax, jax.numpy as jnp
from jax import lax
from jax.experimental import pallas as pl
from jax.experimental.pallas import tpu as pltpu
bf16=jnp.bfloat16; f32=jnp.float32
tiny=pl.CostEstimate(flops=1000000,bytes_accessed=1000000,transcendentals=0)
NT=(((1,),(1,)),((),()))
NN=(((1,),(0,)),((),()))
TN=(((0,),(0,)),((),()))

def dg(a,b,dims):
    return lax.dot_general(a,b,dims,preferred_element_type=f32)

def lane_iota(rows, cols):
    return lax.broadcasted_iota(jnp.int32,(rows,cols),1)

def split3(v):
    hi=v.astype(bf16); r=v-hi.astype(f32)
    mid=r.astype(bf16); lo=(r-mid.astype(f32)).astype(bf16)
    return hi,mid,lo

def aug_lanes(v):
    hi,mid,lo=split3(v)
    lane=lane_iota(*v.shape)%64
    z=jnp.zeros_like(v)
    return jnp.where(lane==0,hi.astype(f32),jnp.where(lane==1,mid.astype(f32),jnp.where(lane==2,lo.astype(f32),z))).astype(bf16)


from jax.sharding import PartitionSpec as P

epsilon = 1e-06
rope_base = 10000.0


def perm_f(x, m):
    n = lax.axis_size("fsdp")
    return lax.ppermute(x, "fsdp", [(i, i ^ m) for i in range(n)])


def perm_s(x, m):
    n = lax.axis_size("sp")
    return lax.ppermute(x, "sp", [(i, i ^ m) for i in range(n)])


def after(x, *deps):
    return lax.optimization_barrier((x,) + deps)[0]


def gather_f(x, *deps):
    outer = lax.axis_size("fsdp") // 2
    x_z = after(x, *deps) if deps else x
    firsts = [x] + [perm_f(x_z, 2 * m) for m in range(1, outer)]
    pieces = []
    for first in firsts:
        pieces += [first, perm_f(first, 1)]
    return pieces


def gather_s(x):
    far = perm_s(x, 2)
    near = perm_s(x, 1)
    return [x, near, far, perm_s(far, 1)]


def place(pieces, me):
    out = jnp.zeros((len(pieces),) + pieces[0].shape, pieces[0].dtype)
    for r, piece in enumerate(pieces):
        out = lax.dynamic_update_index_in_dim(out, piece, me ^ r, 0)
    return out


def scatter_f(blocks, *deps):
    outer = blocks.shape[0] // 2
    me = lax.axis_index("fsdp")
    pairs = blocks.reshape((outer, 2) + blocks.shape[1:])
    mine = lax.dynamic_index_in_dim(pairs, me % 2, 1, keepdims=False)
    other = lax.dynamic_index_in_dim(pairs, 1 - me % 2, 1, keepdims=False)
    got = perm_f(other, 1)
    if deps:
        got = after(got, *deps)
    both = (mine.astype(f32) + got.astype(f32)).astype(bf16)
    at = me // 2
    total = lax.dynamic_index_in_dim(both, at, 0, keepdims=False).astype(f32)
    for m in range(1, outer):
        part = perm_f(lax.dynamic_index_in_dim(both, at ^ m, 0, keepdims=False), 2 * m)
        total = total + part.astype(f32)
    return total.astype(bf16)


def scatter_s(parts):
    got3 = perm_s(parts[3], 1)
    got1 = perm_s(parts[1], 1)
    far = perm_s((parts[2].astype(f32) + got3.astype(f32)).astype(bf16), 2)
    return parts[0].astype(f32) + got1.astype(f32) + far.astype(f32)


def half_swap(v):
    lane = lane_iota(*v.shape) % 64
    return jnp.where(lane < 32, pltpu.roll(v, 96, 1), pltpu.roll(v, 32, 1))


def head_sums(v):
    row = lax.broadcasted_iota(jnp.int32, (128, 128), 0) // 64
    col = lane_iota(128, 128) // 64
    same = jnp.where(row == col, 1.0, 0.0).astype(bf16)
    hi, mid, lo = split3(v)
    return dg(hi, same, NN) + dg(mid, same, NN) + dg(lo, same, NN)


def xor_small(a, b, bits=2):
    out = 0
    for i in range(bits):
        p = (a // (1 << i)) % 2
        q = (b // (1 << i)) % 2
        out = out + (p + q - 2 * p * q) * (1 << i)
    return out


class Ring:
    def __init__(self, own, slot, sems, base, outer, f, s):
        self.own, self.slot, self.sems, self.base = own, slot, sems, base
        self.outer, self.f, self.s = outer, f, s
        self.at, self.inner = f // 2, f % 2

    def copy(self, src, dst, send, recv, to):
        return pltpu.make_async_remote_copy(
            src, dst, self.sems.at[0, self.base + send], self.sems.at[1, self.base + recv],
            device_id=(to, self.s), device_id_type=pl.DeviceIdType.MESH,
        )

    def line(self, k, sign):
        n = self.outer
        lane = 0 if sign > 0 else n
        b = self.f - 2 * k * sign
        src = self.own if k == 0 else self.slot(b)
        return self.copy(src, self.slot(b), lane + k, lane + k + 1, self.f + 2 * sign)

    def line_wait(self, k, sign):
        n = self.outer
        lane = 0 if sign > 0 else n
        b = self.f - 2 * k * sign
        return self.copy(self.slot(b), self.slot(b), lane + k, lane + k, self.f + 2 * sign)

    def cross(self, k, sign):
        n = self.outer
        lane = 2 * n if sign > 0 else 3 * n
        b = self.f - 2 * k * sign
        src = self.own if k == 0 else self.slot(b)
        return self.copy(src, self.slot(b), lane + k, lane + k, self.f + 1 - 2 * self.inner)

    def cross_wait(self, k, sign):
        n = self.outer
        lane = 2 * n if sign > 0 else 3 * n
        b = self.f + 1 - 2 * self.inner - 2 * k * sign
        return self.copy(self.slot(b), self.slot(b), lane + k, lane + k, self.f + 1 - 2 * self.inner)

    def has(self, k, sign):
        return self.at >= k if sign > 0 else self.at + k <= self.outer - 1

    def onward(self, k, sign):
        more = self.at < self.outer - 1 if sign > 0 else self.at > 0
        return more if k == 0 else jnp.logical_and(more, self.has(k, sign))

    def start(self):
        for sign in (1, -1):
            pl.when(self.onward(0, sign))(lambda sign=sign: self.line(0, sign).start())

    def start_cross(self):
        self.cross(0, 1).start()

    def step(self, k):
        for sign in (1, -1):
            @pl.when(self.has(k, sign))
            def _(sign=sign):
                self.line_wait(k, sign).wait_recv()

                @pl.when(self.onward(0, sign))
                def _():
                    self.line(k, sign).start()

                self.cross(k, sign).start()

    def finish(self):
        for k in range(self.outer):
            for sign in (1, -1) if k else (1,):
                if k:
                    @pl.when(self.has(k, sign))
                    def _(k=k, sign=sign):
                        self.cross_wait(k, sign).wait_recv()
                        self.cross(k, sign).wait_send()
                else:
                    self.cross_wait(0, 1).wait_recv()
                    self.cross(0, 1).wait_send()
        for k in range(self.outer - 1):
            for sign in (1, -1):
                @pl.when(self.onward(k, sign))
                def _(k=k, sign=sign):
                    self.line(k, sign).wait_send()


def ring_sems(outer):
    return 4 * outer


def front_kernel(outer, ns, pairs, group, c, inv_log,
                 x_hbm, dy_hbm, small_ref, qkv_hbm, out_hbm, down_hbm, gu_hbm, gain_ref,
                 xh_hbm, dy_all, n2_all, w_d, w_gu, w_qkv_out, w_out_out, att_tok_out,
                 q_ref, k_ref, v_ref, raw_ref, cos_ref, sin_ref, o_ref, laug_ref, mid_ref, small_out,
                 xv, wq, ow, smalls, start_col, att_in, nv, ka, kb, ra, rb, ral, rbl,
                 rsem, tsem, lsem):
    f, s = lax.axis_index("fsdp"), lax.axis_index("sp")
    nf = 2 * outer
    core = s % 2
    near, far = s + 1 - 2 * core, s + 2 - 4 * (s // 2)
    diag = far + 1 - 2 * core
    at, inner = f // 2, f % 2
    blk, width = x_hbm.shape
    T = ns * blk
    q_cols = pairs * 128
    drows = qkv_hbm.shape[0]
    quarter = out_hbm.shape[0]

    barrier = pltpu.get_barrier_semaphore()

    def greet(ff, ss):
        pl.semaphore_signal(barrier, inc=1, device_id=(ff, ss), device_id_type=pl.DeviceIdType.MESH)

    greet(f, near)
    greet(f, far)
    greet(f, diag)
    greet(f + 1 - 2 * inner, s)
    pl.when(at < outer - 1)(lambda: greet(f + 2, s))
    pl.when(at > 0)(lambda: greet(f - 2, s))
    middle_of_line = jnp.logical_and(at > 0, at < outer - 1)
    pl.when(middle_of_line)(lambda: pl.semaphore_wait(barrier, 6))
    pl.when(jnp.logical_not(middle_of_line))(lambda: pl.semaphore_wait(barrier, 5))

    def send(src, dst, n, to):
        return pltpu.make_async_remote_copy(
            src, dst, tsem.at[0, n], tsem.at[1, n], device_id=(f, to), device_id_type=pl.DeviceIdType.MESH
        )

    def keep(src, dst, n):
        return pltpu.make_async_copy(src, dst, lsem.at[n])

    per = ring_sems(outer)
    qkv = Ring(qkv_hbm, lambda b: wq.at[pl.ds(pl.multiple_of(b * drows, drows), drows)], rsem, 0, outer, f, s)
    out = Ring(out_hbm, lambda b: ow.at[b, s], rsem, per, outer, f, s)
    down = Ring(down_hbm, lambda b: w_d.at[b], rsem, 2 * per, outer, f, s)
    gate = Ring(gu_hbm.at[0], lambda b: w_gu.at[0, b], rsem, 3 * per, outer, f, s)
    up = Ring(gu_hbm.at[1], lambda b: w_gu.at[1, b], rsem, 4 * per, outer, f, s)

    def triple(base, own, slot):
        return (
            send(own, slot(1), base, near), send(own, slot(2), base + 1, far), send(slot(2), slot(3), base + 2, near),
        )

    small_t = triple(0, small_ref, lambda r: smalls.at[r])
    tok_t = triple(3, x_hbm, lambda r: xv.at[r])
    dy_t = triple(9, dy_hbm, lambda r: dy_all.at[r])
    small_t[0].start()
    small_t[1].start()
    tok_t[1].start()
    tok_t[0].start()
    load_x = keep(x_hbm, xv.at[0], 0)
    load_x.start()
    load_q = keep(qkv_hbm, wq.at[pl.ds(pl.multiple_of(f * drows, drows), drows)], 1)
    load_q.start()
    load_o = keep(out_hbm, ow.at[f, s], 2)
    load_o.start()
    qkv.start()
    qkv.start_cross()
    out.start()
    out.start_cross()
    smalls[0] = small_ref[...]
    small_t[1].wait_recv()
    small_t[2].start()
    for k in range(1, outer):
        qkv.step(k)
        out.step(k)
    down.start()
    down.start_cross()
    gate.start()
    gate.start_cross()

    small_t[0].wait_recv()
    small_t[2].wait_recv()
    half = 32
    lane = lane_iota(blk, 128)
    freq = jnp.exp((lane % half).astype(f32) * inv_log)
    sign = jnp.where(lane % 64 < half, -1.0, 1.0)
    row = lax.broadcasted_iota(jnp.int32, (blk, 1), 0)
    live = jnp.zeros((1, 1), f32)
    for r in range(ns):
        ints = smalls[r]
        small_out[r] = ints
        col = jnp.transpose(ints)[:, 0:1]
        angle = col * freq
        cos_ref[r] = jnp.cos(angle)
        sin_ref[r] = jnp.sin(angle) * sign
        t = xor_small(s, r)
        start_col[r] = t * blk + row - col.astype(jnp.int32)
        live = live + jnp.sum(ints[1:2, :], axis=1, keepdims=True)
    n_live = live.astype(jnp.int32)

    def project_block(r):
        tile = min(256, blk)

        @pl.loop(0, blk // tile)
        def _(i):
            rows = pl.ds(pl.multiple_of(i * tile, tile), tile)
            x = xv[r, rows, :].astype(f32)
            scale = lax.rsqrt(jnp.mean(x * x, axis=-1, keepdims=True) + epsilon)
            xh = (x * scale).astype(bf16)
            xv[r, rows, :] = xh
            raw = dg(xh, wq[...], NN)
            cosine, sine = cos_ref[r, rows, :], sin_ref[r, rows, :]
            to = pl.ds(pl.multiple_of(r * blk + i * tile, tile), tile)
            for p in range(pairs + 1):
                part = raw[:, 128 * p : 128 * (p + 1)]
                raw_ref[to, 128 * p : 128 * (p + 1)] = part
                inv = lax.rsqrt(head_sums(part * part) * (1.0 / 64) + epsilon)
                normal = part * inv * gain_ref[(0 if p < pairs else 1) : (1 if p < pairs else 2), :]
                turned = (normal * cosine + half_swap(normal) * sine).astype(bf16)
                if p < pairs:
                    q_ref[to, 128 * p : 128 * (p + 1)] = turned
                else:
                    k_ref[to, :] = turned
            v_ref[to, :] = raw[:, 128 * (pairs + 1) :].astype(bf16)

    load_x.wait()
    load_q.wait()
    load_o.wait()
    qkv.finish()
    out.finish()
    out_t = (
        send(ow.at[:, s], ow.at[:, s], 6, near),
        send(ow.at[:, s], ow.at[:, s], 7, far),
        send(ow.at[:, far], ow.at[:, far], 8, near),
    )
    out_w = (
        send(ow.at[:, near], ow.at[:, near], 6, near),
        send(ow.at[:, far], ow.at[:, far], 7, far),
        send(ow.at[:, diag], ow.at[:, diag], 8, near),
    )
    out_t[0].start()
    out_t[1].start()
    dy_t[1].start()
    dy_t[0].start()
    project_block(0)
    keep(xv.at[0], xh_hbm.at[0], 0).start()
    tok_t[1].wait_recv()
    tok_t[2].start()
    tok_t[0].wait_recv()
    down.step(1)
    project_block(1)
    keep(xv.at[1], xh_hbm.at[1], 1).start()
    tok_t[2].wait_send()
    project_block(2)
    keep(xv.at[2], xh_hbm.at[2], 2).start()
    tok_t[2].wait_recv()
    up.start()
    up.start_cross()
    project_block(3)
    keep(xv.at[3], xh_hbm.at[3], 3).start()
    tok_t[0].wait_send()
    tok_t[1].wait_send()

    low = lane_iota(blk, 128) < 64
    row_b = lax.broadcasted_iota(jnp.int32, (blk, 128), 0)

    def pos(t):
        return pl.multiple_of(xor_small(t, s) * blk, blk)

    def prepare(p):
        kv = (pairs * 2 * s + 2 * p) // group - (pairs * 2 * s) // group
        first = kv == 0
        one_a = jnp.where(low, 1.0, 0.0)
        one_b = 1.0 - one_a
        for r in range(ns):
            here = slice(r * blk, (r + 1) * blk)
            kk, vv = k_ref[here, :].astype(f32), v_ref[here, :].astype(f32)
            ksw, vsw = pltpu.roll(kk, 64, 1), pltpu.roll(vv, 64, 1)
            k0, k1 = jnp.where(first, kk, ksw), jnp.where(first, ksw, kk)
            v0, v1 = jnp.where(first, vv, vsw), jnp.where(first, vsw, vv)
            ka[here, :] = jnp.where(low, k0, 0.0).astype(bf16)
            kb[here, :] = jnp.where(low, 0.0, k1).astype(bf16)
            va, vb = jnp.where(low, v0, 0.0), jnp.where(low, 0.0, v1)
            seen = row_b < n_live - xor_small(s, r) * blk
            ra[here, :128], ra[here, 128:] = va.astype(bf16), one_a.astype(bf16)
            rb[here, :128], rb[here, 128:] = vb.astype(bf16), one_b.astype(bf16)
            ral[here, :128] = jnp.where(seen, va, 0.0).astype(bf16)
            ral[here, 128:] = jnp.where(seen, one_a, 0.0).astype(bf16)
            rbl[here, :128] = jnp.where(seen, vb, 0.0).astype(bf16)
            rbl[here, 128:] = jnp.where(seen, one_b, 0.0).astype(bf16)

    kcol = lane_iota(blk, blk)
    qrow = lax.broadcasted_iota(jnp.int32, (blk, blk), 0)

    def query_block(p, i):
        qo = pos(i)
        here = pl.ds(qo, blk)
        lanes = slice(128 * p, 128 * (p + 1))
        q = q_ref[here, lanes]
        st = start_col[xor_small(i, s)]
        ok = (kcol >= st - i * blk) & (kcol <= qrow) & ((kcol < n_live - i * blk) | (kcol == qrow))
        p0 = jnp.where(ok, jnp.exp2(dg(q, ka[here, :], NT) * c), 0.0).astype(bf16)
        p1 = jnp.where(ok, jnp.exp2(dg(q, kb[here, :], NT) * c), 0.0).astype(bf16)
        acc = dg(p0, ra[here, :], NN) + dg(p1, rb[here, :], NN)

        def key_block(j, acc):
            there = pl.ds(pos(j), blk)
            ok = kcol >= (st - j * blk)
            p0 = jnp.where(ok, jnp.exp2(dg(q, ka[there, :], NT) * c), 0.0).astype(bf16)
            p1 = jnp.where(ok, jnp.exp2(dg(q, kb[there, :], NT) * c), 0.0).astype(bf16)
            return acc + dg(p0, ral[there, :], NN) + dg(p1, rbl[there, :], NN)

        acc = lax.fori_loop(0, i, key_block, acc)
        total = acc[:, 128:]
        o_ref[here, lanes] = (acc[:, :128] / total).astype(bf16)
        laug_ref[here, lanes] = aug_lanes(jnp.log(total) * (-8.0))

    jobs = [
        lambda: (gate.step(1), out_t[0].wait_send()),
        lambda: (down.step(2), out_w[1].wait_recv(), out_t[2].start()),
        lambda: gate.step(2),
        lambda: (down.step(3), up.step(1)) if outer > 3 else None,
        lambda: gate.step(3) if outer > 3 else None,
        lambda: up.step(2) if outer > 3 else None,
    ]
    for p in range(pairs):
        prepare(p)
        pl.loop(0, ns - 1)(lambda i, p=p: query_block(p, i))
        if 2 * p < len(jobs):
            jobs[2 * p]()
        query_block(p, ns - 1)
        if 2 * p + 1 < len(jobs):
            jobs[2 * p + 1]()
    for job in jobs[2 * pairs :]:
        job()
    for k in range(4, outer):
        down.step(k)
        gate.step(k)

    att_t = [
        send(o_ref.at[pl.ds(r * blk, blk)], att_in.at[r], 11 + r, to) for r, to in ((1, near), (2, far), (3, diag))
    ]
    att_t[1].start()
    att_t[2].start()
    att_t[0].start()
    for n in range(4):
        keep(xv.at[n], xh_hbm.at[n], n).wait()
    reload = keep(x_hbm, xv.at[0], 0)
    reload.start()
    out_w[0].wait_recv()
    out_w[2].wait_recv()
    out_t[1].wait_send()
    out_t[2].wait_send()
    att_in[0] = o_ref[pl.ds(0, blk), :]
    reload.wait()
    for a in att_t:
        a.wait_recv()
    tile = 512
    shards = nf // ns
    squares = jnp.zeros((blk, 1), f32)
    for n in range(width // tile):
        cols = slice(n * tile, (n + 1) * tile)
        acc = xv[0, :, cols].astype(f32)
        for r in range(ns):
            t = xor_small(s, r)
            w = ow[pl.ds(t * shards, shards), :, :, cols].reshape(q_cols, tile)
            acc = acc + dg(att_in[r], w, NN)
        mid_ref[:, cols] = acc
        squares = squares + jnp.sum(acc * acc, axis=-1, keepdims=True)
    inv = lax.rsqrt(squares * (1.0 / width) + epsilon)
    for n in range(width // tile):
        cols = slice(n * tile, (n + 1) * tile)
        nv[:, cols] = (mid_ref[:, cols] * inv).astype(bf16)
    n2_t = triple(15, nv, lambda r: n2_all.at[r])
    n2_t[1].start()
    n2_t[0].start()
    keeps = [keep(nv, n2_all.at[0], 0), keep(wq, w_qkv_out, 1)]
    for r in range(ns):
        part = ow.at[pl.ds(xor_small(s, r) * shards, shards)]
        keeps.append(keep(part, w_out_out.at[r], 2 + r))
        keeps.append(keep(att_in.at[r], att_tok_out.at[:, pl.ds(r * q_cols, q_cols)], 2 + ns + r))
    for a in keeps:
        a.start()
    for k in range(3, outer):
        up.step(k)
    if outer <= 3:
        for k in range(2, outer):
            up.step(k)
    down.finish()
    gate.finish()
    dy_t[1].wait_recv()
    dy_t[2].start()
    dy_t[0].wait()
    dy_t[1].wait_send()
    dy_t[2].wait()
    small_t[0].wait_send()
    small_t[1].wait_send()
    small_t[2].wait_send()
    for a in att_t:
        a.wait_send()
    n2_t[1].wait_recv()
    n2_t[2].start()
    up.finish()
    n2_t[2].wait()
    n2_t[0].wait()
    n2_t[1].wait_send()
    for a in keeps:
        a.wait()


def front_call(x, dy, small, qkv_mine, out_mine, down_mine, gu_mine, gains, nf, ns, group, head):
    outer = nf // 2
    blk, width = x.shape
    T = blk * ns
    cols = qkv_mine.shape[1]
    pairs = cols // 128 - 2
    q_cols = pairs * 128
    hbm, vmem = pl.BlockSpec(memory_space=pl.ANY), pl.BlockSpec(memory_space=pltpu.VMEM)
    c = math.log2(math.e) * head**-0.5
    inv_log = -2.0 / head * math.log(rope_base)
    S = jax.ShapeDtypeStruct
    quarter = out_mine.shape[0]
    return pl.pallas_call(
        functools.partial(front_kernel, outer, ns, pairs, group, c, inv_log),
        in_specs=[hbm, hbm, vmem, hbm, hbm, hbm, hbm, vmem],
        out_specs=[hbm] * 8 + [vmem] * 10,
        out_shape=[
            S((ns, blk, width), bf16), S((ns, blk, width), bf16), S((ns, blk, width), bf16),
            S((nf,) + down_mine.shape, bf16), S((2, nf) + gu_mine.shape[1:], bf16),
            S((width, cols), bf16), S((ns, nf // ns, ns, quarter, width), bf16), S((blk, ns * q_cols), bf16),
            S((T, q_cols), bf16), S((T, 128), bf16), S((T, 128), bf16), S((T, q_cols + 128), f32),
            S((ns, blk, 128), f32), S((ns, blk, 128), f32), S((T, q_cols), bf16), S((T, q_cols), bf16),
            S((blk, width), f32), S((ns,) + small.shape, f32),
        ],
        scratch_shapes=[
            pltpu.VMEM((ns, blk, width), bf16), pltpu.VMEM((width, cols), bf16),
            pltpu.VMEM((nf, ns, quarter, width), bf16), pltpu.VMEM((ns,) + small.shape, f32),
            pltpu.VMEM((ns, blk, 1), jnp.int32), pltpu.VMEM((ns, blk, q_cols), bf16), pltpu.VMEM((blk, width), bf16),
        ]
        + [pltpu.VMEM((T, 128), bf16)] * 2
        + [pltpu.VMEM((T, 256), bf16)] * 4
        + [
            pltpu.SemaphoreType.DMA((2, 5 * ring_sems(outer))), pltpu.SemaphoreType.DMA((2, 18)),
            pltpu.SemaphoreType.DMA((2 + 2 * ns,)),
        ],
        compiler_params=pltpu.CompilerParams(
            collective_id=0, has_side_effects=True, vmem_limit_bytes=62 * 2**20
        ),
        cost_estimate=tiny,
        name="front",
    )(x, dy, small, qkv_mine, out_mine, down_mine, gu_mine, gains)


class Scatter:
    def __init__(self, sems, base, outer, ns, f, s, xz, own, part, zr, fin, out, local):
        self.sems, self.base, self.outer, self.f, self.s = sems, base, outer, f, s
        self.at, self.inner = f // 2, f % 2
        self.near = s + 1 - 2 * (s % 2)
        self.far = s + 2 - 4 * (s // 2)
        self.diag = self.far + 1 - 2 * (s % 2)
        self.xz, self.own, self.part, self.zr, self.fin, self.out, self.local = xz, own, part, zr, fin, out, local

    def copy(self, src, dst, send, recv, to):
        return pltpu.make_async_remote_copy(
            src, dst, self.sems.at[0, self.base + send], self.sems.at[1, self.base + recv],
            device_id=to, device_id_type=pl.DeviceIdType.MESH,
        )

    def cross(self, k):
        return self.copy(self.part(k), self.xz.at[k], k, k, (self.f + 1 - 2 * self.inner, self.s))

    def line(self, k, src=None):
        n = self.outer
        src = self.xz.at[k] if src is None else src
        return self.copy(src, self.zr.at[self.at], n + k, n + self.at, (2 * k + self.inner, self.s))

    def line_wait(self, k):
        n = self.outer
        return self.copy(self.zr.at[k], self.zr.at[k], n + k, n + k, (2 * k + self.inner, self.s))

    def take(self, k):
        self.cross(k).wait_recv()
        own = self.own(k)
        self.xz[k] = (self.xz[k].astype(f32) + own.astype(f32)).astype(bf16)
        pl.when(k != self.at)(lambda: self.line(k).start())

    def total(self, own=None, fetch=None):
        n = self.outer
        acc = (self.xz[self.at] if own is None else own).astype(f32)
        for m in range(1, n):
            k = (self.at + m) % n
            self.line_wait(k).wait_recv()
            acc = acc + (self.zr[k] if fetch is None else fetch(self.zr.at[k])).astype(f32)
        self.fin[...] = acc.astype(bf16)
        n = 2 * self.outer
        self.copy(self.fin, self.out.at[self.s], n + 1, n + 1, (self.f, self.far)).start()
        self.copy(self.fin, self.out.at[self.s], n, n, (self.f, self.near)).start()
        self.local(self.fin, self.out.at[self.s]).start()

    def forward(self):
        n = 2 * self.outer
        far = self.out.at[self.far]
        self.copy(far, far, n + 1, n + 1, (self.f, self.far)).wait_recv()
        self.copy(far, far, n + 2, n + 2, (self.f, self.near)).start()

    def finish(self, sent=None, crossed=True):
        n = 2 * self.outer
        near, diag = self.out.at[self.near], self.out.at[self.diag]
        self.copy(near, near, n, n, (self.f, self.near)).wait_recv()
        self.copy(diag, diag, n + 2, n + 2, (self.f, self.near)).wait_recv()
        self.copy(self.fin, near, n, n, (self.f, self.near)).wait_send()
        self.copy(self.fin, near, n + 1, n + 1, (self.f, self.far)).wait_send()
        self.copy(near, near, n + 2, n + 2, (self.f, self.near)).wait_send()
        self.local(self.fin, self.out.at[self.s]).wait()
        for k in range(self.outer):
            if crossed:
                self.cross(k).wait_send()
            pl.when(k != self.at)(lambda k=k: self.line(k, sent and sent(k)).wait_send())


def back_kernel(
    outer, ns, pairs, group, c, scale,
    datt_hbm, q_ref, laug_ref, o_ref, k_ref, v_ref, raw_hbm, cos_hbm, sin_hbm, start_ref, live_ref, gain_ref, wq_ref,
    xh_hbm, gd_hbm, gg_hbm, gu_hbm, go_hbm, lo_hbm,
    dn_out, lo_out, sd_out, sg_out, su_out, so_out, sq_out, lo_g3, dn_g3, og1, zr_d, zr_g, zr_u, dgain_ref,
    do_v, qa, qb, qaug, doa, dob, doaug, kaug0, kaug1, vaug0, vaug1, dqacc, dq_v, dk_acc, dv_acc,
    dqkv, dnv, raw_t, cos_t, sin_t, xh_t, gq_send, xz_g, xz_u, xz_o, xz_q, zr_o, zr_q,
    fin_d, fin_g, fin_u, fin_o, fin_q, tile_g, o_t, o_g, gsum, gslot, gline, ssem, tsem, lsem,
):
    f, s = lax.axis_index("fsdp"), lax.axis_index("sp")
    core = s % 2
    near, far = s + 1 - 2 * core, s + 2 - 4 * (s // 2)
    diag = far + 1 - 2 * core
    at, inner = f // 2, f % 2
    cross_f = f + 1 - 2 * inner
    T = q_ref.shape[0]
    blk = T // ns
    q_cols = pairs * 128

    barrier = pltpu.get_barrier_semaphore()

    def greet(ff, ss):
        pl.semaphore_signal(barrier, inc=1, device_id=(ff, ss), device_id_type=pl.DeviceIdType.MESH)

    greet(f, near)
    greet(f, far)
    greet(f, diag)
    greet(cross_f, s)
    for m in range(1, outer):
        greet(2 * ((at + m) % outer) + inner, s)
    pl.semaphore_wait(barrier, 3 + outer)

    def send(src, dst, n, to, ff=None):
        return pltpu.make_async_remote_copy(
            src, dst, tsem.at[0, n], tsem.at[1, n], device_id=(f if ff is None else ff, to),
            device_id_type=pl.DeviceIdType.MESH,
        )

    def keep(src, dst, n):
        return pltpu.make_async_copy(src, dst, lsem.at[n])

    def fetch(src, dst, n=0):
        a = keep(src, dst, n)
        a.start()
        a.wait()
        return dst

    per = 2 * outer + 3

    def local(n):
        return lambda src, dst: keep(src, dst, n)

    part = lambda ref: lambda k: ref.at[2 * k + 1 - inner]
    sd = Scatter(ssem, 0, outer, ns, f, s, None, None, None, zr_d, fin_d, sd_out, local(1))
    sg = Scatter(ssem, per, outer, ns, f, s, xz_g, lambda k: fetch(gg_hbm.at[2 * k + inner], tile_g)[...], part(gg_hbm),
                 zr_g, fin_g, sg_out, local(2))
    su = Scatter(ssem, 2 * per, outer, ns, f, s, xz_u, lambda k: fetch(gu_hbm.at[2 * k + inner], tile_g)[...], part(gu_hbm),
                 zr_u, fin_u, su_out, local(3))
    so = Scatter(ssem, 3 * per, outer, ns, f, s, xz_o, lambda k: o_t[2 * k + inner], part(o_t), zr_o, fin_o, so_out, local(4))
    sq = Scatter(ssem, 4 * per, outer, ns, f, s, xz_q, None, lambda k: gq_send.at[k], zr_q, fin_q, sq_out, local(5))

    def do_part(r, to):
        return send(datt_hbm.at[:, pl.ds(r * q_cols, q_cols)], do_v.at[pl.ds(r * blk, blk)], r, to)

    datt_t = [do_part(2, far), do_part(3, diag), do_part(1, near)]
    for a in datt_t:
        a.start()
    own_do = keep(datt_hbm.at[:, pl.ds(0, q_cols)], do_v.at[pl.ds(0, blk)], 6)
    own_do.start()
    sent_d = lambda k: gd_hbm.at[k]
    for k in range(outer):
        pl.when(k != at)(lambda k=k: sd.line(k, sent_d(k)).start())
        sg.cross(k).start()
    for k in range(outer):
        su.cross(k).start()
    o1 = send(go_hbm.at[:, near], og1, 4, near)
    o3 = send(go_hbm.at[:, diag], o_g.at[0], 5, near)
    of = send(o_g.at[0], o_g.at[1], 6, far)
    lo1 = send(lo_hbm.at[1], lo_out.at[0], 7, near)
    lo3 = send(lo_hbm.at[3], lo_g3, 8, near)
    lof = send(dnv.at[2], lo_out.at[1], 9, far)
    o3.start()
    lo3.start()
    o1.start()
    lo1.start()
    o3.wait_recv()
    fetch(go_hbm.at[:, far], o_t)
    for n in range(o_t.shape[0]):
        o_g[0, n] = (o_g[0, n].astype(f32) + o_t[n].astype(f32)).astype(bf16)
    of.start()
    lo3.wait_recv()
    fetch(lo_g3, dnv.at[2])
    fetch(lo_hbm.at[2], dnv.at[0])
    chunk = 128

    @pl.loop(0, blk // chunk)
    def _(i):
        rows = pl.ds(pl.multiple_of(i * chunk, chunk), chunk)
        dnv[2, rows, :] = (dnv[2, rows, :].astype(f32) + dnv[0, rows, :].astype(f32)).astype(bf16)

    fetch(go_hbm.at[:, s], o_t)
    lof.start()
    own_do.wait()
    for a in datt_t:
        a.wait_recv()

    dk_acc[...] = jnp.zeros_like(dk_acc)
    dv_acc[...] = jnp.zeros_like(dv_acc)
    low = lane_iota(blk, 128) < 64
    lane = lane_iota(blk, 128)
    n_live = live_ref[0:1, 0:1]
    krow = lax.broadcasted_iota(jnp.int32, (blk, blk), 0)
    qcol = lane_iota(blk, blk)

    def pos(t):
        return pl.multiple_of(xor_small(t, s) * blk, blk)

    def is_first(p):
        return (pairs * 2 * s + 2 * p) // group - (pairs * 2 * s) // group == 0

    def prepare(p):
        first = is_first(p)
        lanes = slice(128 * p, 128 * (p + 1))
        ones_a = jnp.where(lane < 3, 1.0, 0.0).astype(bf16)
        ones_b = jnp.where((lane >= 64) & (lane < 67), 1.0, 0.0).astype(bf16)
        for r in range(ns):
            here = slice(r * blk, (r + 1) * blk)
            kk, vv = k_ref[here, :].astype(f32), v_ref[here, :].astype(f32)
            ksw, vsw = pltpu.roll(kk, 64, 1), pltpu.roll(vv, 64, 1)
            k_a = jnp.where(low, jnp.where(first, kk, ksw), 0.0).astype(bf16)
            k_b = jnp.where(low, 0.0, jnp.where(first, ksw, kk)).astype(bf16)
            kaug0[here, :128], kaug0[here, 128:] = k_a, ones_a
            kaug1[here, :128], kaug1[here, 128:] = k_b, ones_b
            vaug0[here, :128] = jnp.where(low, jnp.where(first, vv, vsw), 0.0).astype(bf16)
            vaug0[here, 128:] = ones_a
            vaug1[here, :128] = jnp.where(low, 0.0, jnp.where(first, vsw, vv)).astype(bf16)
            vaug1[here, 128:] = ones_b
            q = q_ref[here, lanes]
            qf = q.astype(f32)
            qaug[here, :128], qaug[here, 128:] = q, laug_ref[here, lanes]
            qa[here, :] = jnp.where(low, qf, 0.0).astype(bf16)
            qb[here, :] = jnp.where(low, 0.0, qf).astype(bf16)
            do = do_v[here, lanes]
            dof = do.astype(f32)
            doa[here, :] = jnp.where(low, dof, 0.0).astype(bf16)
            dob[here, :] = jnp.where(low, 0.0, dof).astype(bf16)
            doaug[here, :128] = do
            doaug[here, 128:] = aug_lanes(-head_sums(dof * o_ref[here, lanes].astype(f32)))
        dqacc[...] = jnp.zeros_like(dqacc)

    def step(j, here, qo, ok, dk, dv):
        there = pl.ds(qo, blk)
        qg, dg_ = qaug[there, :], doaug[there, :]
        e0 = jnp.where(ok, jnp.exp2(dg(kaug0[here, :], qg, NT) * c), 0.0)
        e1 = jnp.where(ok, jnp.exp2(dg(kaug1[here, :], qg, NT) * c), 0.0)
        ds0 = (e0 * dg(vaug0[here, :], dg_, NT)).astype(bf16)
        ds1 = (e1 * dg(vaug1[here, :], dg_, NT)).astype(bf16)
        dv = dv + dg(e0.astype(bf16), doa[there, :], NN) + dg(e1.astype(bf16), dob[there, :], NN)
        dk = dk + dg(ds0, qa[there, :], NN) + dg(ds1, qb[there, :], NN)
        dqacc[there, :] += dg(ds0, kaug0[here, :128], TN) + dg(ds1, kaug1[here, :128], TN)
        return dk, dv

    def key_block(p, j):
        here = pl.ds(pos(j), blk)
        st = start_ref[0:1, here] - j * blk
        ok = (krow >= st) & (krow <= qcol) & ((krow < n_live - j * blk) | (krow == qcol))
        z = jnp.zeros((blk, 128), f32)
        dk, dv = step(j, here, pos(j), ok, z, z)

        def query_block(i, carry):
            qo = pos(i)
            st = start_ref[0:1, pl.ds(qo, blk)] - j * blk
            ok = (krow >= st) & (krow < n_live - j * blk)
            return step(j, here, qo, ok, *carry)

        dk, dv = lax.fori_loop(j + 1, ns, query_block, (dk, dv))
        first = is_first(p)
        dk, dv = dk * scale + pltpu.roll(dk * scale, 64, 1), dv + pltpu.roll(dv, 64, 1)
        dk_acc[here, :] += jnp.where(first, jnp.where(low, dk, 0.0), jnp.where(low, 0.0, dk))
        dv_acc[here, :] += jnp.where(first, jnp.where(low, dv, 0.0), jnp.where(low, 0.0, dv))

    def own_o():
        of.wait()
        o1.wait_recv()
        fetch(og1, o_g.at[0])
        for n in range(o_t.shape[0]):
            o_t[n] = (o_t[n].astype(f32) + o_g[0, n].astype(f32) + o_g[1, n].astype(f32)).astype(bf16)
        for k in range(outer):
            so.cross(k).start()

    jobs = {
        (0, 0): lambda: sg.take(0),
        (0, 1): lambda: (sg.take(1), sg.take(2)),
        (1, 0): lambda: (sg.take(3) if outer > 3 else None, own_o()),
        (1, 1): lambda: (sd.total(fetch(gd_hbm.at[at], fin_d)[...], lambda r: fetch(r, fin_d)[...]), su.take(0)),
        (2, 0): lambda: su.take(1),
        (2, 1): lambda: (su.take(2), sd.forward()),
    }
    for p in range(pairs):
        prepare(p)
        key_block(p, 0)
        jobs.get((p, 0), lambda: None)()
        pl.loop(1, ns)(lambda j, p=p: key_block(p, j))
        dq_v[:, 128 * p : 128 * (p + 1)] = (dqacc[...] * scale).astype(bf16)
        jobs.get((p, 1), lambda: None)()

    tile = min(256, blk)
    gsum[...] = jnp.zeros_like(gsum)

    def turn_block(r):
        @pl.loop(0, blk // tile)
        def _(i):
            rows = pl.ds(pl.multiple_of(r * blk + i * tile, tile), tile)
            part_rows = pl.ds(pl.multiple_of(i * tile, tile), tile)
            loads = [
                keep(raw_hbm.at[rows], raw_t, 0), keep(cos_hbm.at[r, part_rows], cos_t, 7), keep(sin_hbm.at[r, part_rows], sin_t, 8),
            ]
            for a in loads:
                a.start()
            for a in loads:
                a.wait()
            cosine, sine = cos_t[...], sin_t[...]
            for p in range(pairs + 1):
                which = 0 if p < pairs else 1
                lanes = slice(128 * p, 128 * (p + 1))
                grad = dq_v[rows, lanes].astype(f32) if p < pairs else dk_acc[rows, :].astype(bf16).astype(f32)
                raw = raw_t[:, lanes]
                inv = lax.rsqrt(head_sums(raw * raw) * (1.0 / 64) + epsilon)
                normal = raw * inv
                grad = grad * cosine - half_swap(grad) * sine
                gsum[which] += jnp.sum((grad * normal).reshape(tile // 8, 8, 128), axis=0)
                grad = grad * gain_ref[which : which + 1, :]
                mean = head_sums(grad * normal) * (1.0 / 64)
                dqkv[rows, lanes] = (inv * (grad - normal * mean)).astype(bf16)
            dqkv[rows, 128 * (pairs + 1) :] = dv_acc[rows, :].astype(bf16)
            dnv[{3: 0, 2: 1, 1: 2, 0: 0}[r], part_rows, :] = dg(dqkv[rows, :], wq_ref[...], NT).astype(bf16)

    dn1 = send(dnv.at[2], dn_out.at[1], 10, near)
    dn3 = send(dnv.at[0], dn_g3, 11, near)
    dnf = send(dnv.at[1], dn_out.at[2], 12, far)
    turn_block(3)
    dn3.start()
    turn_block(2)
    dn3.wait()
    fetch(dn_g3, dnv.at[0])

    @pl.loop(0, blk // chunk)
    def _(i):
        rows = pl.ds(pl.multiple_of(i * chunk, chunk), chunk)
        dnv[1, rows, :] = (dnv[1, rows, :].astype(f32) + dnv[0, rows, :].astype(f32)).astype(bf16)

    dnf.start()
    lof.wait_send()
    turn_block(1)
    dn1.start()
    su.take(3) if outer > 3 else None
    turn_block(0)
    own_dn = keep(dnv.at[0], dn_out.at[0], 9)
    own_dn.start()
    for k in range(4, outer):
        sg.take(k)
        su.take(k)

    drows, span = gq_send.shape[1], xh_t.shape[1]

    def grad_block(b):
        first = (b * drows) // span
        fetch(xh_hbm.at[:, pl.ds(pl.multiple_of(first * span, span), span)], xh_t)
        grad = dg(xh_t[...], dqkv[...], TN)
        if span > drows:
            grad = jnp.where(b % 2 == 0, grad[:drows], grad[drows:])
        return grad.astype(bf16)

    for k in range(outer):
        gq_send[k] = grad_block(2 * k + 1 - inner)
    for k in range(outer):
        sq.cross(k).start()
    for k in range(outer):
        so.take(k)
    sq.own = lambda k: grad_block(2 * k + inner)

    gslot[0] = jnp.concatenate(
        [jnp.sum(gsum[0], axis=0, keepdims=True), jnp.sum(gsum[1], axis=0, keepdims=True), jnp.zeros((6, 128), f32)]
    )
    hops = [
        send(gslot.at[0], gslot.at[3], 13, near), send(gslot.at[1], gslot.at[4], 14, far),
        send(gslot.at[2], gslot.at[5], 15, s, cross_f),
    ]
    hops[0].start()
    sg.total(None, lambda r: fetch(r, fin_g)[...])
    hops[0].wait_recv()
    gslot[1] = gslot[0] + gslot[3]
    hops[1].start()
    for k in range(outer):
        sq.take(k)
    hops[1].wait_recv()
    gslot[2] = gslot[1] + gslot[4]
    hops[2].start()
    so.total()
    hops[2].wait_recv()
    gline[at] = gslot[2] + gslot[5]
    lines = [
        send(gline.at[at], gline.at[at], 16 + m, s, 2 * ((at + m) % outer) + inner) for m in range(1, outer)
    ]
    for a in lines:
        a.start()
    su.total(None, lambda r: fetch(r, fin_u)[...])
    sg.forward()
    so.forward()
    for m in range(1, outer):
        k = (at + outer - m) % outer
        send(gline.at[k], gline.at[k], 16 + m, s, 2 * k + inner).wait_recv()
    total = gline[0]
    for k in range(1, outer):
        total = total + gline[k]
    dgain_ref[...] = total + pltpu.roll(total, 64, 1)
    sq.total()
    su.forward()
    sq.forward()

    sd.finish(sent_d, False)
    for a in (sg, su, so, sq):
        a.finish()
    for a in lines + hops + datt_t + [o1, o3, lo1, lo3, dn1, dnf]:
        a.wait_send()
    for a in (lo1, lof, dn1, dnf):
        a.wait_recv()
    own_dn.wait()


def back_call(datt, q, laug, o, k, v, raw, cosine, sine, start_row, n_live, gains, w_qkv, xh, gd, gg, gu, go, lo, ns, group, head):
    outer = gd.shape[0]
    T = q.shape[0]
    blk = T // ns
    width, cols = w_qkv.shape
    pairs = cols // 128 - 2
    q_cols = pairs * 128
    scale = head**-0.5
    c = math.log2(math.e) * scale
    hbm, vmem = pl.BlockSpec(memory_space=pl.ANY), pl.BlockSpec(memory_space=pltpu.VMEM)
    S, V = jax.ShapeDtypeStruct, pltpu.VMEM
    dblk, gblk, oblk = gd.shape[1:], gg.shape[1:], (go.shape[2], width)
    drows = gblk[0]
    qblk = (drows, cols)
    half = (T, 128)
    wide = (T, 256)
    per = 2 * outer + 3
    return pl.pallas_call(
        functools.partial(back_kernel, outer, ns, pairs, group, c, scale),
        in_specs=[hbm] + [vmem] * 5 + [hbm] * 3 + [vmem] * 4 + [hbm] * 6,
        out_specs=[hbm] * 13 + [vmem],
        out_shape=[
            S((3, blk, width), bf16), S((2, blk, width), bf16),
            S((ns,) + dblk, bf16), S((ns,) + gblk, bf16), S((ns,) + gblk, bf16), S((ns,) + oblk, bf16), S((ns,) + qblk, bf16),
            S((blk, width), bf16), S((blk, width), bf16), S((2 * outer,) + oblk, bf16), S((outer,) + dblk, bf16), S((outer,) + gblk, bf16), S((outer,) + gblk, bf16),
            S((8, 128), f32),
        ],
        scratch_shapes=[
            V((T, q_cols), bf16), V(half, bf16), V(half, bf16), V(wide, bf16), V(half, bf16), V(half, bf16), V(wide, bf16),
            V(wide, bf16), V(wide, bf16), V(wide, bf16), V(wide, bf16),
            V(half, f32), V((T, q_cols), bf16), V(half, f32), V(half, f32),
            V((T, cols), bf16), V((3, blk, width), bf16),
            V((min(256, blk), q_cols + 128), f32), V((min(256, blk), 128), f32), V((min(256, blk), 128), f32),
            V((T, drows if drows % 128 == 0 else 2 * drows), bf16), V((outer,) + qblk, bf16),
            V((outer,) + gblk, bf16), V((outer,) + gblk, bf16), V((outer,) + oblk, bf16), V((outer,) + qblk, bf16),
            V((outer,) + oblk, bf16), V((outer,) + qblk, bf16),
            V(dblk, bf16), V(gblk, bf16), V(gblk, bf16), V(oblk, bf16), V(qblk, bf16),
            V(gblk, bf16), V((2 * outer,) + oblk, bf16), V((2, 2 * outer) + oblk, bf16),
            V((2, 8, 128), f32), V((6, 8, 128), f32), V((outer, 8, 128), f32),
            pltpu.SemaphoreType.DMA((2, 5 * per)), pltpu.SemaphoreType.DMA((2, 16 + outer)), pltpu.SemaphoreType.DMA((10,)),
        ],
        compiler_params=pltpu.CompilerParams(
            collective_id=1, has_side_effects=True, vmem_limit_bytes=63 * 2**20
        ),
        cost_estimate=tiny,
        name="back",
    )(datt, q, laug, o, k, v, raw, cosine, sine, start_row, n_live, gains, w_qkv, xh, gd, gg, gu, go, lo)


def ffn_kernel(count, n_in, *refs):
    n2_ref, dy_ref, wg_ref, wu_ref, wd_ref = refs[:5]
    hid_ref, dg_ref, du_ref, dn_ref, acc = refs[n_in:]
    step = pl.program_id(0)
    wg, wu, wd = wg_ref[0], wu_ref[0], wd_ref[...]
    for n in range(count):
        n2, dy = n2_ref[n], dy_ref[n]
        gate = dg(n2, wg, NN)
        up = dg(n2, wu, NN)
        dhid = dg(dy, wd, NT)
        sig = jax.nn.sigmoid(gate)
        act = gate * sig
        hid_ref[n] = (act * up).astype(bf16)
        dup = (dhid * act).astype(bf16)
        dgate = (dhid * up * (sig * (1.0 + gate * (1.0 - sig)))).astype(bf16)
        dg_ref[n] = dgate
        du_ref[n] = dup
        grad = dg(dgate, wg, NT) + dg(dup, wu, NT)

        @pl.when(step == 0)
        def _():
            acc[n] = grad

        @pl.when(step > 0)
        def _():
            acc[n] += grad

        @pl.when(step == pl.num_programs(0) - 1)
        def _():
            dn_ref[n] = acc[n].astype(bf16)


def ffn_call(chunk, chunks, n2_all, dy_all, w_gu, w_d, earlier, tile=256):
    members, rows, width = n2_all.shape
    count = members // chunks
    units = w_d.shape[0]
    n_in = 5 + len(earlier)
    once = pl.Buffered(1)
    big = jax.ShapeDtypeStruct((members, rows, units), bf16)
    return pl.pallas_call(
        functools.partial(ffn_kernel, count, n_in),
        grid=(units // tile,),
        in_specs=[pl.BlockSpec((count, rows, width), lambda j: (chunk, 0, 0), pipeline_mode=once)] * 2
        + [
            pl.BlockSpec((1, width, tile), lambda j: (0, 0, j)),
            pl.BlockSpec((1, width, tile), lambda j: (1, 0, j)),
            pl.BlockSpec((tile, width), lambda j: (j, 0)),
        ]
        + [pl.BlockSpec(memory_space=pl.ANY)] * len(earlier),
        out_specs=[pl.BlockSpec((count, rows, tile), lambda j: (chunk, 0, j))] * 3
        + [pl.BlockSpec((count, rows, width), lambda j: (0, 0, 0))],
        out_shape=[big, big, big] + [jax.ShapeDtypeStruct((count, rows, width), bf16)],
        scratch_shapes=[pltpu.VMEM((count, rows, width), f32)],
        input_output_aliases={5 + i: i for i in range(len(earlier))},
        compiler_params=pltpu.CompilerParams(vmem_limit_bytes=62 * 2**20),
        cost_estimate=tiny,
        name="ffn",
    )(n2_all, dy_all, w_gu, w_gu, w_d, *earlier)


def pick_kernel(members, shards, shard, unit, info, gain_ref, wg_ref, wu_ref, out_ref):
    out_ref[...] = jnp.zeros_like(out_ref)
    for k in range(members):
        width = min(unit, shard - k * unit)

        @pl.when(info[0] == k)
        def _():
            for n, ref in enumerate((wg_ref, wu_ref)):
                for j in range(shards):
                    part = ref[:, j * shard + k * unit : j * shard + k * unit + width].astype(f32)
                    out_ref[n, :, j * unit : j * unit + width] = (part * gain_ref[...]).astype(bf16)


def pick_call(info, gain, w_gate, w_up, members, shards, shard, unit):
    rows, cols = w_gate.shape
    tile = min(64, rows)
    return pl.pallas_call(
        functools.partial(pick_kernel, members, shards, shard, unit),
        grid_spec=pltpu.PrefetchScalarGridSpec(
            num_scalar_prefetch=1,
            grid=(rows // tile,),
            in_specs=[pl.BlockSpec((tile, 1), lambda i, *_: (i, 0))]
            + [pl.BlockSpec((tile, cols), lambda i, *_: (i, 0))] * 2,
            out_specs=pl.BlockSpec((2, tile, shards * unit), lambda i, *_: (0, i, 0)),
        ),
        out_shape=jax.ShapeDtypeStruct((2, rows, shards * unit), bf16),
        compiler_params=pltpu.CompilerParams(vmem_limit_bytes=60 * 2**20),
        name="pick_units",
    )(info, gain, w_gate, w_up)


def join_kernel(members, shards, shard, unit, gain_ref, m_ref, w_ref, out_ref, sum_ref):
    for k in range(members):
        width = min(unit, shard - k * unit)
        for j in range(shards):
            part = m_ref[k, :, j * unit : j * unit + width].astype(f32)
            out_ref[:, j * shard + k * unit : j * shard + k * unit + width] = part
    full = out_ref[...]
    sum_ref[...] = jnp.broadcast_to(
        jnp.sum(full * w_ref[...].astype(f32), axis=-1, keepdims=True), sum_ref.shape
    )
    out_ref[...] = full * gain_ref[...]


def join_call(gain, stacked, weight, members, shards, shard, unit):
    rows, cols = weight.shape
    tile = min(64, rows)
    return pl.pallas_call(
        functools.partial(join_kernel, members, shards, shard, unit),
        grid=(rows // tile,),
        in_specs=[
            pl.BlockSpec((tile, 1), lambda i: (i, 0)),
            pl.BlockSpec((members, tile, shards * unit), lambda i: (0, i, 0)),
            pl.BlockSpec((tile, cols), lambda i: (i, 0)),
        ],
        out_specs=[
            pl.BlockSpec((tile, cols), lambda i: (i, 0)),
            pl.BlockSpec((tile, 128), lambda i: (i, 0)),
        ],
        out_shape=[
            jax.ShapeDtypeStruct((rows, cols), f32),
            jax.ShapeDtypeStruct((rows, 128), f32),
        ],
        compiler_params=pltpu.CompilerParams(vmem_limit_bytes=60 * 2**20),
        name="join_units",
    )(gain, stacked, weight)


def dot_bf(a, b, dims):
    return dg(a, b, dims).astype(bf16)


def local(
    tokens, seg_ids, pad_mask, positions, attn_gain, w_query, w_key, w_value, query_gain,
    key_gain, w_out, ffn_gain, w_gate, w_up, w_down, cotangent,
):
    nf, ns = lax.axis_size("fsdp"), lax.axis_size("sp")
    f, s = lax.axis_index("fsdp"), lax.axis_index("sp")
    seq_count, blk, width = tokens.shape
    assert seq_count == 1 and ns == 4
    length = blk * ns
    head = query_gain.shape[0]
    q_heads, kv_heads = w_query.shape[1] // head, w_key.shape[1] // head
    group = q_heads // kv_heads
    q_local = q_heads // ns
    kv_base = [(q_local * k) // group for k in range(ns)]
    pairs = q_local // 2
    q_cols = q_local * head
    kv_map = jnp.array(
        [[(q_local * k + 2 * p) // group - kv_base[k] for p in range(pairs)] for k in range(ns)],
        jnp.int32,
    )[s]
    base = jnp.array(kv_base, jnp.int32)[s] * head
    shard = w_down.shape[0]
    unit = -(-(-(-shard // ns)) // 16) * 16
    units = unit * nf
    out_rows = w_out.shape[0]
    quarter = out_rows // ns
    sub = 512

    x = tokens[0]
    dy = cotangent[0]
    gain_one = attn_gain.astype(f32)[:, None]
    gain_two = ffn_gain.astype(f32)[:, None]

    kv_cols = 2 * head
    mine = jnp.concatenate(
        [
            lax.dynamic_slice_in_dim(w_query, s * q_cols, q_cols, 1),
            lax.dynamic_slice_in_dim(w_key, base, kv_cols, 1),
            lax.dynamic_slice_in_dim(w_value, base, kv_cols, 1),
        ],
        axis=1,
    )
    mine = (mine.astype(f32) * gain_one).astype(bf16)
    out_mine = lax.dynamic_slice_in_dim(w_out, s * quarter, quarter, 0)
    down_pad = jnp.concatenate([w_down, jnp.zeros((unit * ns - shard, width), bf16)])
    down_mine = lax.dynamic_slice_in_dim(down_pad, s * unit, unit, 0)
    one_info = jnp.reshape(s, (1,)).astype(jnp.int32)
    gu_mine = pick_call(one_info, gain_two, w_gate, w_up, ns, nf, shard, unit)
    small = jnp.concatenate(
        [positions.astype(f32), pad_mask.astype(f32), jnp.zeros((6, blk), f32)]
    )
    gains = jnp.concatenate(
        [
            jnp.tile(query_gain.astype(f32), 2)[None],
            jnp.tile(key_gain.astype(f32), 2)[None],
            jnp.zeros((6, 2 * head), f32),
        ]
    )
    (
        xh, dy_all, n2_all, w_d, w_gu, w_qkv, w_out_rel, att, q, k, v, raw, cosine, sine,
        attended, laug, middle, small_all,
    ) = front_call(x, dy, small, mine, out_mine, down_mine, gu_mine, gains, nf, ns, group, head)
    xh = xh.reshape(length, width)
    dy_all = lax.dynamic_update_index_in_dim(dy_all, dy, 0, 0)
    w_d = lax.dynamic_update_index_in_dim(w_d, down_mine, f, 0).reshape(units, width)
    w_gu = lax.dynamic_update_slice_in_dim(w_gu, gu_mine[:, None], f, 1).reshape(2, width, units)
    w_out_rel = w_out_rel.reshape(ns * q_cols, width)
    pos_rel = small_all[:, 0].astype(jnp.int32)
    n_live = jnp.sum(small_all[:, 1]).astype(jnp.int32)
    true_block = s ^ jnp.arange(ns)
    start_rel = (true_block[:, None] * blk + jnp.arange(blk)[None] - pos_rel).reshape(length)
    xf = x.astype(f32)
    inv_two = lax.rsqrt(jnp.mean(middle * middle, axis=-1, keepdims=True) + epsilon)

    first = ffn_call(0, 2, n2_all, dy_all, w_gu, w_d, [])
    second = ffn_call(1, 2, n2_all, dy_all, w_gu, w_d, first[:3])
    hidden, dgate, dup = [a.reshape(length, -1) for a in second[:3]]
    n2_all = n2_all.reshape(length, width)
    dn2 = [first[3][0], first[3][1], second[3][0], second[3][1]]
    got3 = perm_s(dn2[3], 1)
    got1 = perm_s(dn2[1], 1)
    pair = (dn2[2].astype(f32) + got3.astype(f32)).astype(bf16)
    dn2_far = perm_s(pair, 2)

    dy_all = dy_all.reshape(length, width)
    hidden_a = after(hidden, pair, got1)
    grad_d = dot_bf(hidden_a, dy_all, TN).reshape(nf // 2, 2, unit, width)
    d_own = lax.dynamic_index_in_dim(grad_d, f % 2, 1, keepdims=False)
    d_other = lax.dynamic_index_in_dim(grad_d, 1 - f % 2, 1, keepdims=False)
    d_got = perm_f(d_other, 1)
    dgate_a, dup_a = after(dgate, d_other), after(dup, d_other)
    grad_g = dot_bf(n2_all, dgate_a, TN).reshape(nf, width // nf, units)
    grad_u = dot_bf(n2_all, dup_a, TN).reshape(nf, width // nf, units)
    lo = dot_bf(hidden_a, w_d, NN).reshape(ns, blk, width)

    dn2_own = dn2[0].astype(f32) + got1.astype(f32) + dn2_far.astype(f32)
    hat_two = middle * inv_two
    dmiddle = dy.astype(f32) + inv_two * (
        dn2_own - hat_two * jnp.mean(dn2_own * hat_two, axis=-1, keepdims=True)
    )
    dmid = dmiddle.astype(bf16)
    datt = dot_bf(dmid, w_out_rel, NT)
    gd = (d_own.astype(f32) + after(d_got, dmid).astype(f32)).astype(bf16)

    grad_o = dot_bf(att, dmid, TN).reshape(ns, q_cols, width)
    grad_o = jnp.concatenate(
        [lax.dynamic_index_in_dim(grad_o, s ^ t, 0, keepdims=False) for t in range(ns)]
    ).reshape(nf, ns, quarter, width)

    live_row = jnp.full((8, 128), n_live, jnp.int32)
    dn, lo_got, sum_d, sum_g, sum_u, sum_o, sum_qkv, _, _, _, _, _, _, dgain = back_call(
        datt, q, laug, attended, k, v, raw, cosine, sine, jnp.broadcast_to(start_rel[None], (8, length)),
        live_row, gains, w_qkv, xh, gd, grad_g, grad_u, grad_o, lo, ns, group, head,
    )
    layer_out = (
        middle + lo[0].astype(f32) + lo_got[0].astype(f32) + lo_got[1].astype(f32)
    ).astype(bf16)
    w_down_grad = sum_d.reshape(ns * unit, width)[:shard].astype(f32)
    w_gate_grad, gate_sum = join_call(gain_two, sum_g, w_gate, ns, nf, shard, unit)
    w_up_grad, up_sum = join_call(gain_two, sum_u, w_up, ns, nf, shard, unit)
    ffn_gain_grad = (gate_sum + up_sum)[:, 0]
    w_out_grad = sum_o.reshape(out_rows, width).astype(f32)

    dn_own = dn[0].astype(f32) + dn[1].astype(f32) + dn[2].astype(f32)
    inv_one = lax.rsqrt(jnp.mean(xf * xf, axis=-1, keepdims=True) + epsilon)
    hat_one = xf * inv_one
    tokens_grad = (
        dmiddle + inv_one * (dn_own - hat_one * jnp.mean(dn_own * hat_one, axis=-1, keepdims=True))
    ).astype(bf16)
    query_gain_grad, key_gain_grad = dgain[0, :head], dgain[1, :head]

    sum_qkv = sum_qkv.astype(f32)
    m_query = jnp.concatenate([sum_qkv[k][:, :q_cols] for k in range(ns)], axis=1)

    def heads_of(offset):
        cols = []
        for h in range(kv_heads):
            total = 0.0
            for k in range(ns):
                if 0 <= h - kv_base[k] < 2:
                    at = offset + (h - kv_base[k]) * head
                    total = total + sum_qkv[k][:, at : at + head]
            cols.append(total)
        return jnp.concatenate(cols, axis=1)

    m_key, m_value = heads_of(q_cols), heads_of(q_cols + kv_cols)
    attn_gain_grad = (
        jnp.sum(m_query * w_query.astype(f32), axis=1)
        + jnp.sum(m_key * w_key.astype(f32), axis=1)
        + jnp.sum(m_value * w_value.astype(f32), axis=1)
    )
    return (
        layer_out[None], tokens_grad[None], attn_gain_grad, m_query * gain_one, m_key * gain_one,
        m_value * gain_one, query_gain_grad, key_gain_grad, w_out_grad, ffn_gain_grad,
        w_gate_grad, w_up_grad, w_down_grad,
    )


def solution(mesh):
    row, vec = P("fsdp", None), P("fsdp")
    tok, ids = P("fsdp", "sp", None), P("fsdp", "sp")
    in_specs = (tok, ids, ids, ids, vec, row, row, row, P(), P(), row, vec, row, row, row, tok)
    out_specs = (tok, tok, vec, row, row, row, P(), P(), row, vec, row, row, row)
    return jax.shard_map(local, mesh=mesh, in_specs=in_specs, out_specs=out_specs, check_vma=False)
```

```python
import functools, math
import jax, jax.numpy as jnp
from jax import lax
from jax.experimental import pallas as pl
from jax.experimental.pallas import tpu as pltpu
bf16=jnp.bfloat16; f32=jnp.float32
tiny=pl.CostEstimate(flops=1000000,bytes_accessed=1000000,transcendentals=0)
NT=(((1,),(1,)),((),()))
NN=(((1,),(0,)),((),()))
TN=(((0,),(0,)),((),()))

def dg(a,b,dims):
    return lax.dot_general(a,b,dims,preferred_element_type=f32)

def lane_iota(rows, cols):
    return lax.broadcasted_iota(jnp.int32,(rows,cols),1)

def split3(v):
    hi=v.astype(bf16); r=v-hi.astype(f32)
    mid=r.astype(bf16); lo=(r-mid.astype(f32)).astype(bf16)
    return hi,mid,lo

def aug_lanes(v):
    hi,mid,lo=split3(v)
    lane=lane_iota(*v.shape)%64
    z=jnp.zeros_like(v)
    return jnp.where(lane==0,hi.astype(f32),jnp.where(lane==1,mid.astype(f32),jnp.where(lane==2,lo.astype(f32),z))).astype(bf16)


from jax.sharding import PartitionSpec as P

epsilon = 1e-06
rope_base = 10000.0


def perm_f(x, m):
    n = lax.axis_size("fsdp")
    return lax.ppermute(x, "fsdp", [(i, i ^ m) for i in range(n)])


def perm_s(x, m):
    n = lax.axis_size("sp")
    return lax.ppermute(x, "sp", [(i, i ^ m) for i in range(n)])


def after(x, *deps):
    return lax.optimization_barrier((x,) + deps)[0]


def gather_f(x, *deps):
    outer = lax.axis_size("fsdp") // 2
    x_z = after(x, *deps) if deps else x
    firsts = [x] + [perm_f(x_z, 2 * m) for m in range(1, outer)]
    pieces = []
    for first in firsts:
        pieces += [first, perm_f(first, 1)]
    return pieces


def gather_s(x):
    far = perm_s(x, 2)
    near = perm_s(x, 1)
    return [x, near, far, perm_s(far, 1)]


def place(pieces, me):
    out = jnp.zeros((len(pieces),) + pieces[0].shape, pieces[0].dtype)
    for r, piece in enumerate(pieces):
        out = lax.dynamic_update_index_in_dim(out, piece, me ^ r, 0)
    return out


def scatter_f(blocks, *deps):
    outer = blocks.shape[0] // 2
    me = lax.axis_index("fsdp")
    pairs = blocks.reshape((outer, 2) + blocks.shape[1:])
    mine = lax.dynamic_index_in_dim(pairs, me % 2, 1, keepdims=False)
    other = lax.dynamic_index_in_dim(pairs, 1 - me % 2, 1, keepdims=False)
    got = perm_f(other, 1)
    if deps:
        got = after(got, *deps)
    both = (mine.astype(f32) + got.astype(f32)).astype(bf16)
    at = me // 2
    total = lax.dynamic_index_in_dim(both, at, 0, keepdims=False).astype(f32)
    for m in range(1, outer):
        part = perm_f(lax.dynamic_index_in_dim(both, at ^ m, 0, keepdims=False), 2 * m)
        total = total + part.astype(f32)
    return total.astype(bf16)


def scatter_s(parts):
    got3 = perm_s(parts[3], 1)
    got1 = perm_s(parts[1], 1)
    far = perm_s((parts[2].astype(f32) + got3.astype(f32)).astype(bf16), 2)
    return parts[0].astype(f32) + got1.astype(f32) + far.astype(f32)


def half_swap(v):
    lane = lane_iota(*v.shape) % 64
    return jnp.where(lane < 32, pltpu.roll(v, 96, 1), pltpu.roll(v, 32, 1))


def head_sums(v):
    row = lax.broadcasted_iota(jnp.int32, (128, 128), 0) // 64
    col = lane_iota(128, 128) // 64
    same = jnp.where(row == col, 1.0, 0.0).astype(bf16)
    hi, mid, lo = split3(v)
    return dg(hi, same, NN) + dg(mid, same, NN) + dg(lo, same, NN)


def xor_small(a, b, bits=2):
    out = 0
    for i in range(bits):
        p = (a // (1 << i)) % 2
        q = (b // (1 << i)) % 2
        out = out + (p + q - 2 * p * q) * (1 << i)
    return out


class Ring:
    def __init__(self, own, slot, sems, base, outer, f, s):
        self.own, self.slot, self.sems, self.base = own, slot, sems, base
        self.outer, self.f, self.s = outer, f, s
        self.at, self.inner = f // 2, f % 2

    def copy(self, src, dst, send, recv, to):
        return pltpu.make_async_remote_copy(
            src, dst, self.sems.at[0, self.base + send], self.sems.at[1, self.base + recv],
            device_id=(to, self.s), device_id_type=pl.DeviceIdType.MESH,
        )

    def line(self, k, sign):
        n = self.outer
        lane = 0 if sign > 0 else n
        b = self.f - 2 * k * sign
        src = self.own if k == 0 else self.slot(b)
        return self.copy(src, self.slot(b), lane + k, lane + k + 1, self.f + 2 * sign)

    def line_wait(self, k, sign):
        n = self.outer
        lane = 0 if sign > 0 else n
        b = self.f - 2 * k * sign
        return self.copy(self.slot(b), self.slot(b), lane + k, lane + k, self.f + 2 * sign)

    def cross(self, k, sign):
        n = self.outer
        lane = 2 * n if sign > 0 else 3 * n
        b = self.f - 2 * k * sign
        src = self.own if k == 0 else self.slot(b)
        return self.copy(src, self.slot(b), lane + k, lane + k, self.f + 1 - 2 * self.inner)

    def cross_wait(self, k, sign):
        n = self.outer
        lane = 2 * n if sign > 0 else 3 * n
        b = self.f + 1 - 2 * self.inner - 2 * k * sign
        return self.copy(self.slot(b), self.slot(b), lane + k, lane + k, self.f + 1 - 2 * self.inner)

    def has(self, k, sign):
        return self.at >= k if sign > 0 else self.at + k <= self.outer - 1

    def onward(self, k, sign):
        more = self.at < self.outer - 1 if sign > 0 else self.at > 0
        return more if k == 0 else jnp.logical_and(more, self.has(k, sign))

    def start(self):
        for sign in (1, -1):
            pl.when(self.onward(0, sign))(lambda sign=sign: self.line(0, sign).start())

    def start_cross(self):
        self.cross(0, 1).start()

    def step(self, k):
        for sign in (1, -1):
            @pl.when(self.has(k, sign))
            def _(sign=sign):
                self.line_wait(k, sign).wait_recv()

                @pl.when(self.onward(0, sign))
                def _():
                    self.line(k, sign).start()

                self.cross(k, sign).start()

    def finish(self):
        for k in range(self.outer):
            for sign in (1, -1) if k else (1,):
                if k:
                    @pl.when(self.has(k, sign))
                    def _(k=k, sign=sign):
                        self.cross_wait(k, sign).wait_recv()
                        self.cross(k, sign).wait_send()
                else:
                    self.cross_wait(0, 1).wait_recv()
                    self.cross(0, 1).wait_send()
        for k in range(self.outer - 1):
            for sign in (1, -1):
                @pl.when(self.onward(k, sign))
                def _(k=k, sign=sign):
                    self.line(k, sign).wait_send()


def ring_sems(outer):
    return 4 * outer


def front_kernel(outer, ns, pairs, group, c, inv_log, unit, kv_base,
                 x_hbm, dy_hbm, small_ref, wq_ref, wk_ref, wv_ref, out_hbm, down_w, gate_w, up_w, one_ref, two_ref, gain_ref,
                 xh_hbm, dy_all, n2_all, w_d, w_gu, w_qkv_out, w_out_out, att_tok_out,
                 q_ref, k_ref, v_ref, raw_ref, cos_ref, sin_ref, o_ref, laug_ref, mid_ref, inv_ref, small_out,
                 qkv_hbm, down_hbm, gu_hbm, gate_v, up_v, xv, wq, ow, smalls, start_col, att_in, nv, ka, kb, ra, rb, ral, rbl,
                 rsem, tsem, lsem):
    f, s = lax.axis_index("fsdp"), lax.axis_index("sp")
    nf = 2 * outer
    core = s % 2
    near, far = s + 1 - 2 * core, s + 2 - 4 * (s // 2)
    diag = far + 1 - 2 * core
    at, inner = f // 2, f % 2
    blk, width = x_hbm.shape
    T = ns * blk
    q_cols = pairs * 128
    drows = qkv_hbm.shape[0]
    quarter = out_hbm.shape[0]

    shard, units = down_w.shape[0], gu_hbm.shape[2]

    one = one_ref[:, 0:1]
    qkv_hbm[:, :q_cols] = (wq_ref[:, pl.ds(pl.multiple_of(s * q_cols, 128), q_cols)].astype(f32) * one).astype(bf16)
    for n in range(ns):

        @pl.when(s == n)
        def _(n=n):
            for m, ref in enumerate((wk_ref, wv_ref)):
                part = ref[:, kv_base[n] : kv_base[n] + 128].astype(f32)
                qkv_hbm[:, q_cols + 128 * m : q_cols + 128 * (m + 1)] = (part * one).astype(bf16)

    barrier = pltpu.get_barrier_semaphore()

    def greet(ff, ss):
        pl.semaphore_signal(barrier, inc=1, device_id=(ff, ss), device_id_type=pl.DeviceIdType.MESH)

    greet(f, near)
    greet(f, far)
    greet(f, diag)
    greet(f + 1 - 2 * inner, s)
    pl.when(at < outer - 1)(lambda: greet(f + 2, s))
    pl.when(at > 0)(lambda: greet(f - 2, s))
    middle_of_line = jnp.logical_and(at > 0, at < outer - 1)
    pl.when(middle_of_line)(lambda: pl.semaphore_wait(barrier, 6))
    pl.when(jnp.logical_not(middle_of_line))(lambda: pl.semaphore_wait(barrier, 5))

    def send(src, dst, n, to):
        return pltpu.make_async_remote_copy(
            src, dst, tsem.at[0, n], tsem.at[1, n], device_id=(f, to), device_id_type=pl.DeviceIdType.MESH
        )

    def keep(src, dst, n):
        return pltpu.make_async_copy(src, dst, lsem.at[n])

    per = ring_sems(outer)
    qkv = Ring(qkv_hbm, lambda b: wq.at[pl.ds(pl.multiple_of(b * drows, drows), drows)], rsem, 0, outer, f, s)
    out = Ring(out_hbm, lambda b: ow.at[b, s], rsem, per, outer, f, s)
    down = Ring(down_hbm, lambda b: w_d.at[b], rsem, 2 * per, outer, f, s)
    gate = Ring(gu_hbm.at[0], lambda b: w_gu.at[0, b], rsem, 3 * per, outer, f, s)
    up = Ring(gu_hbm.at[1], lambda b: w_gu.at[1, b], rsem, 4 * per, outer, f, s)

    def triple(base, own, slot):
        return (
            send(own, slot(1), base, near), send(own, slot(2), base + 1, far), send(slot(2), slot(3), base + 2, near),
        )

    load_g = pltpu.make_async_copy(gate_w, gate_v, lsem.at[3])
    load_u = pltpu.make_async_copy(up_w, up_v, lsem.at[4])
    small_t = triple(0, small_ref, lambda r: smalls.at[r])
    tok_t = triple(3, x_hbm, lambda r: xv.at[r])
    dy_t = triple(9, dy_hbm, lambda r: dy_all.at[r])
    small_t[0].start()
    small_t[1].start()
    tok_t[1].start()
    tok_t[0].start()
    load_x = keep(x_hbm, xv.at[0], 0)
    load_x.start()
    wq[pl.ds(pl.multiple_of(f * drows, drows), drows), :] = qkv_hbm[...]
    load_o = keep(out_hbm, ow.at[f, s], 2)
    load_o.start()
    qkv.start()
    qkv.start_cross()
    out.start()
    out.start_cross()
    smalls[0] = small_ref[...]
    load_g.start()
    load_u.start()
    down_hbm[...] = jnp.zeros_like(down_hbm)
    for n in range(ns):
        count = min(unit, shard - n * unit)
        if count <= 0:
            continue

        @pl.when(s == n)
        def _(n=n, count=count):
            a = pltpu.make_async_copy(down_w.at[pl.ds(n * unit, count)], down_hbm.at[pl.ds(0, count)], lsem.at[5])
            a.start()
            a.wait()

    small_t[1].wait_recv()
    small_t[2].start()
    for k in range(1, outer):
        qkv.step(k)
        out.step(k)
    down.start()
    down.start_cross()
    load_g.wait()
    load_u.wait()
    two = two_ref[:, 0:1]
    gu_hbm[...] = jnp.zeros_like(gu_hbm)
    for n in range(ns):
        count = min(unit, shard - n * unit)
        if count <= 0:
            continue

        @pl.when(s == n)
        def _(n=n, count=count):
            for m, ref in enumerate((gate_v, up_v)):
                for j in range(nf):
                    part = ref[:, j * shard + n * unit : j * shard + n * unit + count].astype(f32)
                    gu_hbm[m, :, j * unit : j * unit + count] = (part * two).astype(bf16)

    own_w = [keep(down_hbm, w_d.at[f], 3), keep(gu_hbm.at[0], w_gu.at[0, f], 4), keep(gu_hbm.at[1], w_gu.at[1, f], 5)]

    small_t[0].wait_recv()
    small_t[2].wait_recv()
    half = 32
    lane = lane_iota(blk, 128)
    freq = jnp.exp((lane % half).astype(f32) * inv_log)
    sign = jnp.where(lane % 64 < half, -1.0, 1.0)
    row = lax.broadcasted_iota(jnp.int32, (blk, 1), 0)
    live = jnp.zeros((1, 1), f32)
    for r in range(ns):
        ints = smalls[r]
        small_out[r] = ints
        col = jnp.transpose(ints)[:, 0:1]
        angle = col * freq
        cos_ref[r] = jnp.cos(angle)
        sin_ref[r] = jnp.sin(angle) * sign
        t = xor_small(s, r)
        start_col[r] = t * blk + row - col.astype(jnp.int32)
        live = live + jnp.sum(ints[1:2, :], axis=1, keepdims=True)
    n_live = live.astype(jnp.int32)
    gate.start()
    gate.start_cross()
    for a in own_w:
        a.start()

    def project_block(r):
        tile = min(256, blk)

        @pl.loop(0, blk // tile)
        def _(i):
            rows = pl.ds(pl.multiple_of(i * tile, tile), tile)
            x = xv[r, rows, :].astype(f32)
            scale = lax.rsqrt(jnp.mean(x * x, axis=-1, keepdims=True) + epsilon)
            xh = (x * scale).astype(bf16)
            xv[r, rows, :] = xh
            raw = dg(xh, wq[...], NN)
            cosine, sine = cos_ref[r, rows, :], sin_ref[r, rows, :]
            to = pl.ds(pl.multiple_of(r * blk + i * tile, tile), tile)
            for p in range(pairs + 1):
                part = raw[:, 128 * p : 128 * (p + 1)]
                raw_ref[to, 128 * p : 128 * (p + 1)] = part
                inv = lax.rsqrt(head_sums(part * part) * (1.0 / 64) + epsilon)
                normal = part * inv * gain_ref[(0 if p < pairs else 1) : (1 if p < pairs else 2), :]
                turned = (normal * cosine + half_swap(normal) * sine).astype(bf16)
                if p < pairs:
                    q_ref[to, 128 * p : 128 * (p + 1)] = turned
                else:
                    k_ref[to, :] = turned
            v_ref[to, :] = raw[:, 128 * (pairs + 1) :].astype(bf16)

    load_x.wait()
    load_o.wait()
    qkv.finish()
    out.finish()
    out_t = (
        send(ow.at[:, s], ow.at[:, s], 6, near),
        send(ow.at[:, s], ow.at[:, s], 7, far),
        send(ow.at[:, far], ow.at[:, far], 8, near),
    )
    out_w = (
        send(ow.at[:, near], ow.at[:, near], 6, near),
        send(ow.at[:, far], ow.at[:, far], 7, far),
        send(ow.at[:, diag], ow.at[:, diag], 8, near),
    )
    out_t[0].start()
    out_t[1].start()
    dy_t[1].start()
    dy_t[0].start()
    project_block(0)
    keep(xv.at[0], xh_hbm.at[0], 0).start()
    tok_t[1].wait_recv()
    tok_t[2].start()
    tok_t[0].wait_recv()
    down.step(1)
    project_block(1)
    keep(xv.at[1], xh_hbm.at[1], 1).start()
    tok_t[2].wait_send()
    project_block(2)
    keep(xv.at[2], xh_hbm.at[2], 2).start()
    tok_t[2].wait_recv()
    up.start()
    up.start_cross()
    project_block(3)
    for a in own_w:
        a.wait()
    keep(xv.at[3], xh_hbm.at[3], 3).start()
    tok_t[0].wait_send()
    tok_t[1].wait_send()

    low = lane_iota(blk, 128) < 64
    row_b = lax.broadcasted_iota(jnp.int32, (blk, 128), 0)

    def pos(t):
        return pl.multiple_of(xor_small(t, s) * blk, blk)

    def prepare(p):
        kv = (pairs * 2 * s + 2 * p) // group - (pairs * 2 * s) // group
        first = kv == 0
        one_a = jnp.where(low, 1.0, 0.0)
        one_b = 1.0 - one_a
        for r in range(ns):
            here = slice(r * blk, (r + 1) * blk)
            kk, vv = k_ref[here, :].astype(f32), v_ref[here, :].astype(f32)
            ksw, vsw = pltpu.roll(kk, 64, 1), pltpu.roll(vv, 64, 1)
            k0, k1 = jnp.where(first, kk, ksw), jnp.where(first, ksw, kk)
            v0, v1 = jnp.where(first, vv, vsw), jnp.where(first, vsw, vv)
            ka[here, :] = jnp.where(low, k0, 0.0).astype(bf16)
            kb[here, :] = jnp.where(low, 0.0, k1).astype(bf16)
            va, vb = jnp.where(low, v0, 0.0), jnp.where(low, 0.0, v1)
            seen = row_b < n_live - xor_small(s, r) * blk
            ra[here, :128], ra[here, 128:] = va.astype(bf16), one_a.astype(bf16)
            rb[here, :128], rb[here, 128:] = vb.astype(bf16), one_b.astype(bf16)
            ral[here, :128] = jnp.where(seen, va, 0.0).astype(bf16)
            ral[here, 128:] = jnp.where(seen, one_a, 0.0).astype(bf16)
            rbl[here, :128] = jnp.where(seen, vb, 0.0).astype(bf16)
            rbl[here, 128:] = jnp.where(seen, one_b, 0.0).astype(bf16)

    kcol = lane_iota(blk, blk)
    qrow = lax.broadcasted_iota(jnp.int32, (blk, blk), 0)

    def query_block(p, i):
        qo = pos(i)
        here = pl.ds(qo, blk)
        lanes = slice(128 * p, 128 * (p + 1))
        q = q_ref[here, lanes]
        st = start_col[xor_small(i, s)]
        ok = (kcol >= st - i * blk) & (kcol <= qrow) & ((kcol < n_live - i * blk) | (kcol == qrow))
        p0 = jnp.where(ok, jnp.exp2(dg(q, ka[here, :], NT) * c), 0.0).astype(bf16)
        p1 = jnp.where(ok, jnp.exp2(dg(q, kb[here, :], NT) * c), 0.0).astype(bf16)
        acc = dg(p0, ra[here, :], NN) + dg(p1, rb[here, :], NN)

        def key_block(j, acc):
            there = pl.ds(pos(j), blk)
            ok = kcol >= (st - j * blk)
            p0 = jnp.where(ok, jnp.exp2(dg(q, ka[there, :], NT) * c), 0.0).astype(bf16)
            p1 = jnp.where(ok, jnp.exp2(dg(q, kb[there, :], NT) * c), 0.0).astype(bf16)
            return acc + dg(p0, ral[there, :], NN) + dg(p1, rbl[there, :], NN)

        acc = lax.fori_loop(0, i, key_block, acc)
        total = acc[:, 128:]
        o_ref[here, lanes] = (acc[:, :128] / total).astype(bf16)
        laug_ref[here, lanes] = aug_lanes(jnp.log(total) * (-8.0))

    jobs = [
        lambda: (gate.step(1), out_t[0].wait_send()),
        lambda: (down.step(2), out_w[1].wait_recv(), out_t[2].start()),
        lambda: gate.step(2),
        lambda: (down.step(3), up.step(1)) if outer > 3 else None,
        lambda: gate.step(3) if outer > 3 else None,
        lambda: up.step(2) if outer > 3 else None,
    ]
    for p in range(pairs):
        prepare(p)
        pl.loop(0, ns - 1)(lambda i, p=p: query_block(p, i))
        if 2 * p < len(jobs):
            jobs[2 * p]()
        query_block(p, ns - 1)
        if 2 * p + 1 < len(jobs):
            jobs[2 * p + 1]()
    for job in jobs[2 * pairs :]:
        job()
    for k in range(4, outer):
        down.step(k)
        gate.step(k)

    att_t = [
        send(o_ref.at[pl.ds(r * blk, blk)], att_in.at[r], 11 + r, to) for r, to in ((1, near), (2, far), (3, diag))
    ]
    att_t[1].start()
    att_t[2].start()
    att_t[0].start()
    for n in range(4):
        keep(xv.at[n], xh_hbm.at[n], n).wait()
    reload = keep(x_hbm, xv.at[0], 0)
    reload.start()
    load_dy = keep(dy_hbm, xv.at[1], 1)
    load_dy.start()
    out_w[0].wait_recv()
    out_w[2].wait_recv()
    out_t[1].wait_send()
    out_t[2].wait_send()
    att_in[0] = o_ref[pl.ds(0, blk), :]
    reload.wait()
    load_dy.wait()
    own_dy = keep(xv.at[1], dy_all.at[0], 1)
    own_dy.start()
    own_dy.wait()
    for a in att_t:
        a.wait_recv()
    tile = 512
    shards = nf // ns
    squares = jnp.zeros((blk, 1), f32)
    for n in range(width // tile):
        cols = slice(n * tile, (n + 1) * tile)
        acc = xv[0, :, cols].astype(f32)
        for r in range(ns):
            t = xor_small(s, r)
            w = ow[pl.ds(t * shards, shards), :, :, cols].reshape(q_cols, tile)
            acc = acc + dg(att_in[r], w, NN)
        mid_ref[:, cols] = acc
        squares = squares + jnp.sum(acc * acc, axis=-1, keepdims=True)
    inv = lax.rsqrt(squares * (1.0 / width) + epsilon)
    inv_ref[...] = jnp.broadcast_to(inv, inv_ref.shape)
    for n in range(width // tile):
        cols = slice(n * tile, (n + 1) * tile)
        nv[:, cols] = (mid_ref[:, cols] * inv).astype(bf16)
    n2_t = triple(15, nv, lambda r: n2_all.at[r])
    n2_t[1].start()
    n2_t[0].start()
    keeps = [keep(nv, n2_all.at[0], 0), keep(wq, w_qkv_out, 1)]
    for r in range(ns):
        part = ow.at[pl.ds(xor_small(s, r) * shards, shards)]
        keeps.append(keep(part, w_out_out.at[r], 2 + r))
        keeps.append(keep(att_in.at[r], att_tok_out.at[:, pl.ds(r * q_cols, q_cols)], 2 + ns + r))
    for a in keeps:
        a.start()
    for k in range(3, outer):
        up.step(k)
    if outer <= 3:
        for k in range(2, outer):
            up.step(k)
    down.finish()
    gate.finish()
    dy_t[1].wait_recv()
    dy_t[2].start()
    dy_t[0].wait()
    dy_t[1].wait_send()
    dy_t[2].wait()
    small_t[0].wait_send()
    small_t[1].wait_send()
    small_t[2].wait_send()
    for a in att_t:
        a.wait_send()
    n2_t[1].wait_recv()
    n2_t[2].start()
    up.finish()
    n2_t[2].wait()
    n2_t[0].wait()
    n2_t[1].wait_send()
    for a in keeps:
        a.wait()


def front_call(x, dy, small, w_query, w_key, w_value, out_mine, w_down, w_gate, w_up, gain_one, gain_two, gains,
               nf, ns, group, head, unit, kv_base, q_cols):
    outer = nf // 2
    blk, width = x.shape
    T = blk * ns
    pairs = q_cols // 128
    cols = q_cols + 256
    drows = w_query.shape[0]
    units = unit * nf
    hbm, vmem = pl.BlockSpec(memory_space=pl.ANY), pl.BlockSpec(memory_space=pltpu.VMEM)
    c = math.log2(math.e) * head**-0.5
    inv_log = -2.0 / head * math.log(rope_base)
    S = jax.ShapeDtypeStruct
    quarter = out_mine.shape[0]
    return pl.pallas_call(
        functools.partial(front_kernel, outer, ns, pairs, group, c, inv_log, unit, [b * head for b in kv_base]),
        in_specs=[hbm, hbm, vmem, vmem, vmem, vmem, hbm, hbm, hbm, hbm, vmem, vmem, vmem],
        out_specs=[hbm] * 8 + [vmem] * 11,
        out_shape=[
            S((ns, blk, width), bf16), S((ns, blk, width), bf16), S((ns, blk, width), bf16),
            S((nf, unit, width), bf16), S((2, nf, drows, units), bf16),
            S((width, cols), bf16), S((ns, nf // ns, ns, quarter, width), bf16), S((blk, ns * q_cols), bf16),
            S((T, q_cols), bf16), S((T, 128), bf16), S((T, 128), bf16), S((T, q_cols + 128), f32),
            S((ns, blk, 128), f32), S((ns, blk, 128), f32), S((T, q_cols), bf16), S((T, q_cols), bf16),
            S((blk, width), f32), S((blk, 128), f32), S((ns,) + small.shape, f32),
        ],
        scratch_shapes=[
            pltpu.VMEM((drows, cols), bf16), pltpu.VMEM((unit, width), bf16), pltpu.VMEM((2, drows, units), bf16),
            pltpu.VMEM(w_gate.shape, bf16), pltpu.VMEM(w_up.shape, bf16),
            pltpu.VMEM((ns, blk, width), bf16), pltpu.VMEM((width, cols), bf16),
            pltpu.VMEM((nf, ns, quarter, width), bf16), pltpu.VMEM((ns,) + small.shape, f32),
            pltpu.VMEM((ns, blk, 1), jnp.int32), pltpu.VMEM((ns, blk, q_cols), bf16), pltpu.VMEM((blk, width), bf16),
        ]
        + [pltpu.VMEM((T, 128), bf16)] * 2
        + [pltpu.VMEM((T, 256), bf16)] * 4
        + [
            pltpu.SemaphoreType.DMA((2, 5 * ring_sems(outer))), pltpu.SemaphoreType.DMA((2, 18)),
            pltpu.SemaphoreType.DMA((2 + 2 * ns,)),
        ],
        compiler_params=pltpu.CompilerParams(
            collective_id=0, has_side_effects=True, vmem_limit_bytes=67043328
        ),
        cost_estimate=tiny,
        name="front",
    )(x, dy, small, w_query, w_key, w_value, out_mine, w_down, w_gate, w_up, gain_one, gain_two, gains)


class Scatter:
    def __init__(self, sems, base, outer, ns, f, s, xz, own, part, zr, fin, out, local):
        self.sems, self.base, self.outer, self.f, self.s = sems, base, outer, f, s
        self.at, self.inner = f // 2, f % 2
        self.near = s + 1 - 2 * (s % 2)
        self.far = s + 2 - 4 * (s // 2)
        self.diag = self.far + 1 - 2 * (s % 2)
        self.xz, self.own, self.part, self.zr, self.fin, self.out, self.local = xz, own, part, zr, fin, out, local

    def copy(self, src, dst, send, recv, to):
        return pltpu.make_async_remote_copy(
            src, dst, self.sems.at[0, self.base + send], self.sems.at[1, self.base + recv],
            device_id=to, device_id_type=pl.DeviceIdType.MESH,
        )

    def cross(self, k):
        return self.copy(self.part(k), self.xz.at[k], k, k, (self.f + 1 - 2 * self.inner, self.s))

    def line(self, k, src=None):
        n = self.outer
        src = self.xz.at[k] if src is None else src
        return self.copy(src, self.zr.at[self.at], n + k, n + self.at, (2 * k + self.inner, self.s))

    def line_wait(self, k):
        n = self.outer
        return self.copy(self.zr.at[k], self.zr.at[k], n + k, n + k, (2 * k + self.inner, self.s))

    def take(self, k):
        self.cross(k).wait_recv()
        own = self.own(k)
        self.xz[k] = (self.xz[k].astype(f32) + own.astype(f32)).astype(bf16)
        pl.when(k != self.at)(lambda: self.line(k).start())

    def total(self, own=None, fetch=None):
        n = self.outer
        acc = (self.xz[self.at] if own is None else own).astype(f32)
        for m in range(1, n):
            k = (self.at + m) % n
            self.line_wait(k).wait_recv()
            acc = acc + (self.zr[k] if fetch is None else fetch(self.zr.at[k])).astype(f32)
        self.fin[...] = acc.astype(bf16)
        if self.out is None:
            return
        n = 2 * self.outer
        self.copy(self.fin, self.out.at[self.s], n + 1, n + 1, (self.f, self.far)).start()
        self.copy(self.fin, self.out.at[self.s], n, n, (self.f, self.near)).start()
        self.local(self.fin, self.out.at[self.s]).start()

    def forward(self):
        n = 2 * self.outer
        far = self.out.at[self.far]
        self.copy(far, far, n + 1, n + 1, (self.f, self.far)).wait_recv()
        self.copy(far, far, n + 2, n + 2, (self.f, self.near)).start()

    def finish(self, sent=None, crossed=True):
        n = 2 * self.outer
        if self.out is not None:
            near, diag = self.out.at[self.near], self.out.at[self.diag]
            self.copy(near, near, n, n, (self.f, self.near)).wait_recv()
            self.copy(diag, diag, n + 2, n + 2, (self.f, self.near)).wait_recv()
            self.copy(self.fin, near, n, n, (self.f, self.near)).wait_send()
            self.copy(self.fin, near, n + 1, n + 1, (self.f, self.far)).wait_send()
            self.copy(near, near, n + 2, n + 2, (self.f, self.near)).wait_send()
            self.local(self.fin, self.out.at[self.s]).wait()
        for k in range(self.outer):
            if crossed:
                self.cross(k).wait_send()
            pl.when(k != self.at)(lambda k=k: self.line(k, sent and sent(k)).wait_send())


def back_kernel(
    outer, ns, pairs, group, c, scale,
    datt_hbm, q_ref, laug_ref, o_ref, k_ref, v_ref, raw_hbm, cos_hbm, sin_hbm, start_ref, live_ref, gain_ref, wq_ref,
    xh_hbm, gd_hbm, gg_hbm, gu_hbm, att_hbm, dmid_hbm, lo_hbm,
    dn_out, lo_out, sd_out, sg_out, fin_u, so_out, fin_q, go_hbm, lo_g3, dn_g3, og1, zr_d, zr_g, zr_u, dgain_ref,
    do_v, qa, qb, qaug, doa, dob, doaug, kaug0, kaug1, vaug0, vaug1, dqacc, dq_v, dk_acc, dv_acc,
    dqkv, dnv, raw_t, cos_t, sin_t, xh_t, gq_send, xz_g, xz_u, xz_o, xz_q, zr_o, zr_q,
    fin_d, fin_g, fin_o, tile_g, o_t, o_g, gsum, gslot, gline, ssem, tsem, lsem,
):
    f, s = lax.axis_index("fsdp"), lax.axis_index("sp")
    core = s % 2
    near, far = s + 1 - 2 * core, s + 2 - 4 * (s // 2)
    diag = far + 1 - 2 * core
    at, inner = f // 2, f % 2
    cross_f = f + 1 - 2 * inner
    T = q_ref.shape[0]
    blk = T // ns
    q_cols = pairs * 128

    barrier = pltpu.get_barrier_semaphore()

    def greet(ff, ss):
        pl.semaphore_signal(barrier, inc=1, device_id=(ff, ss), device_id_type=pl.DeviceIdType.MESH)

    greet(f, near)
    greet(f, far)
    greet(f, diag)
    greet(cross_f, s)
    for m in range(1, outer):
        greet(2 * ((at + m) % outer) + inner, s)
    pl.semaphore_wait(barrier, 3 + outer)

    def send(src, dst, n, to, ff=None):
        return pltpu.make_async_remote_copy(
            src, dst, tsem.at[0, n], tsem.at[1, n], device_id=(f if ff is None else ff, to),
            device_id_type=pl.DeviceIdType.MESH,
        )

    def keep(src, dst, n):
        return pltpu.make_async_copy(src, dst, lsem.at[n])

    def fetch(src, dst, n=0):
        a = keep(src, dst, n)
        a.start()
        a.wait()
        return dst

    turn = [n // 2 if n % 2 else outer - 1 - n // 2 for n in range(outer)]
    per = 2 * outer + 3

    def local(n):
        return lambda src, dst: keep(src, dst, n)

    part = lambda ref: lambda k: ref.at[2 * k + 1 - inner]
    sd = Scatter(ssem, 0, outer, ns, f, s, None, None, None, zr_d, fin_d, sd_out, local(1))
    sg = Scatter(ssem, per, outer, ns, f, s, xz_g, lambda k: fetch(gg_hbm.at[2 * k + inner], tile_g)[...], part(gg_hbm),
                 zr_g, fin_g, sg_out, local(2))
    su = Scatter(ssem, 2 * per, outer, ns, f, s, xz_u, lambda k: fetch(gu_hbm.at[2 * k + inner], tile_g)[...], part(gu_hbm),
                 zr_u, fin_u, None, None)
    so = Scatter(ssem, 3 * per, outer, ns, f, s, xz_o, lambda k: o_t[2 * k + inner], part(o_t), zr_o, fin_o, so_out, local(4))
    sq = Scatter(ssem, 4 * per, outer, ns, f, s, xz_q, None, lambda k: gq_send.at[k], zr_q, fin_q, None, None)

    def do_part(r, to):
        return send(datt_hbm.at[:, pl.ds(r * q_cols, q_cols)], do_v.at[pl.ds(r * blk, blk)], r, to)

    datt_t = [do_part(2, far), do_part(3, diag), do_part(1, near)]
    for a in datt_t:
        a.start()
    own_do = keep(datt_hbm.at[:, pl.ds(0, q_cols)], do_v.at[pl.ds(0, blk)], 6)
    own_do.start()
    sent_d = lambda k: gd_hbm.at[k]
    for k in turn:
        pl.when(k != at)(lambda k=k: sd.line(k, sent_d(k)).start())
        sg.cross(k).start()
    for k in turn:
        su.cross(k).start()
    o1 = send(go_hbm.at[:, near], og1, 4, near)
    o3 = send(go_hbm.at[:, diag], o_g.at[0], 5, near)
    of = send(o_g.at[0], o_g.at[1], 6, far)
    lo1 = send(lo_hbm.at[1], lo_out.at[0], 7, near)
    lo3 = send(lo_hbm.at[3], lo_g3, 8, near)
    lof = send(dnv.at[2], lo_out.at[1], 9, far)
    lo3.start()
    lo1.start()
    load_d = keep(dmid_hbm, dnv.at[1], 0)
    load_d.start()
    load_a = [keep(att_hbm.at[:, pl.ds(r * q_cols, q_cols)], dq_v.at[pl.ds(r * blk, blk)], 1 + r) for r in range(ns)]
    for a in load_a:
        a.start()
    for a in load_a + [load_d]:
        a.wait()
    shards, quarter = 2 * outer // ns, o_t.shape[1]
    half_w = 512
    for r in range(ns):
        for n in range(dnv.shape[2] // half_w):
            cols = slice(n * half_w, (n + 1) * half_w)
            grad = dg(dq_v[r * blk : (r + 1) * blk, :], dnv[1, :, cols], TN).astype(bf16)
            o_t[:, :, cols] = grad.reshape(shards * ns, quarter, half_w)
        outs = [
            keep(o_t.at[pl.ds(a * ns, ns)], go_hbm.at[xor_small(s, r) * shards + a], 1 + a) for a in range(shards)
        ]
        for a in outs:
            a.start()
        for a in outs:
            a.wait()
    o3.start()
    o1.start()
    o3.wait_recv()
    fetch(go_hbm.at[:, far], o_t)
    for n in range(o_t.shape[0]):
        o_g[0, n] = (o_g[0, n].astype(f32) + o_t[n].astype(f32)).astype(bf16)
    of.start()
    lo3.wait_recv()
    fetch(lo_g3, dnv.at[2])
    fetch(lo_hbm.at[2], dnv.at[0])
    chunk = 128

    @pl.loop(0, blk // chunk)
    def _(i):
        rows = pl.ds(pl.multiple_of(i * chunk, chunk), chunk)
        dnv[2, rows, :] = (dnv[2, rows, :].astype(f32) + dnv[0, rows, :].astype(f32)).astype(bf16)

    fetch(go_hbm.at[:, s], o_t)
    lof.start()
    own_do.wait()
    for a in datt_t:
        a.wait_recv()

    dk_acc[...] = jnp.zeros_like(dk_acc)
    dv_acc[...] = jnp.zeros_like(dv_acc)
    low = lane_iota(blk, 128) < 64
    lane = lane_iota(blk, 128)
    n_live = live_ref[0:1, 0:1]
    krow = lax.broadcasted_iota(jnp.int32, (blk, blk), 0)
    qcol = lane_iota(blk, blk)

    def pos(t):
        return pl.multiple_of(xor_small(t, s) * blk, blk)

    def is_first(p):
        return (pairs * 2 * s + 2 * p) // group - (pairs * 2 * s) // group == 0

    def prepare(p):
        first = is_first(p)
        lanes = slice(128 * p, 128 * (p + 1))
        ones_a = jnp.where(lane < 3, 1.0, 0.0).astype(bf16)
        ones_b = jnp.where((lane >= 64) & (lane < 67), 1.0, 0.0).astype(bf16)
        for r in range(ns):
            here = slice(r * blk, (r + 1) * blk)
            kk, vv = k_ref[here, :].astype(f32), v_ref[here, :].astype(f32)
            ksw, vsw = pltpu.roll(kk, 64, 1), pltpu.roll(vv, 64, 1)
            k_a = jnp.where(low, jnp.where(first, kk, ksw), 0.0).astype(bf16)
            k_b = jnp.where(low, 0.0, jnp.where(first, ksw, kk)).astype(bf16)
            kaug0[here, :128], kaug0[here, 128:] = k_a, ones_a
            kaug1[here, :128], kaug1[here, 128:] = k_b, ones_b
            vaug0[here, :128] = jnp.where(low, jnp.where(first, vv, vsw), 0.0).astype(bf16)
            vaug0[here, 128:] = ones_a
            vaug1[here, :128] = jnp.where(low, 0.0, jnp.where(first, vsw, vv)).astype(bf16)
            vaug1[here, 128:] = ones_b
            q = q_ref[here, lanes]
            qf = q.astype(f32)
            qaug[here, :128], qaug[here, 128:] = q, laug_ref[here, lanes]
            qa[here, :] = jnp.where(low, qf, 0.0).astype(bf16)
            qb[here, :] = jnp.where(low, 0.0, qf).astype(bf16)
            do = do_v[here, lanes]
            dof = do.astype(f32)
            doa[here, :] = jnp.where(low, dof, 0.0).astype(bf16)
            dob[here, :] = jnp.where(low, 0.0, dof).astype(bf16)
            doaug[here, :128] = do
            doaug[here, 128:] = aug_lanes(-head_sums(dof * o_ref[here, lanes].astype(f32)))
        dqacc[...] = jnp.zeros_like(dqacc)

    def step(j, here, qo, ok, dk, dv):
        there = pl.ds(qo, blk)
        qg, dg_ = qaug[there, :], doaug[there, :]
        e0 = jnp.where(ok, jnp.exp2(dg(kaug0[here, :], qg, NT) * c), 0.0)
        e1 = jnp.where(ok, jnp.exp2(dg(kaug1[here, :], qg, NT) * c), 0.0)
        ds0 = (e0 * dg(vaug0[here, :], dg_, NT)).astype(bf16)
        ds1 = (e1 * dg(vaug1[here, :], dg_, NT)).astype(bf16)
        dv = dv + dg(e0.astype(bf16), doa[there, :], NN) + dg(e1.astype(bf16), dob[there, :], NN)
        dk = dk + dg(ds0, qa[there, :], NN) + dg(ds1, qb[there, :], NN)
        dqacc[there, :] += dg(ds0, kaug0[here, :128], TN) + dg(ds1, kaug1[here, :128], TN)
        return dk, dv

    def key_block(p, j):
        here = pl.ds(pos(j), blk)
        st = start_ref[0:1, here] - j * blk
        ok = (krow >= st) & (krow <= qcol) & ((krow < n_live - j * blk) | (krow == qcol))
        z = jnp.zeros((blk, 128), f32)
        dk, dv = step(j, here, pos(j), ok, z, z)

        def query_block(i, carry):
            qo = pos(i)
            st = start_ref[0:1, pl.ds(qo, blk)] - j * blk
            ok = (krow >= st) & (krow < n_live - j * blk)
            return step(j, here, qo, ok, *carry)

        dk, dv = lax.fori_loop(j + 1, ns, query_block, (dk, dv))
        first = is_first(p)
        dk, dv = dk * scale + pltpu.roll(dk * scale, 64, 1), dv + pltpu.roll(dv, 64, 1)
        dk_acc[here, :] += jnp.where(first, jnp.where(low, dk, 0.0), jnp.where(low, 0.0, dk))
        dv_acc[here, :] += jnp.where(first, jnp.where(low, dv, 0.0), jnp.where(low, 0.0, dv))

    def own_o():
        of.wait()
        o1.wait_recv()
        fetch(og1, o_g.at[0])
        for n in range(o_t.shape[0]):
            o_t[n] = (o_t[n].astype(f32) + o_g[0, n].astype(f32) + o_g[1, n].astype(f32)).astype(bf16)
        for k in turn:
            so.cross(k).start()

    jobs = {
        (0, 0): lambda: sg.take(turn[0]),
        (0, 1): lambda: (sg.take(turn[1]), sg.take(turn[2])),
        (1, 0): lambda: (sg.take(turn[3]) if outer > 3 else None, own_o()),
        (1, 1): lambda: (sd.total(fetch(gd_hbm.at[at], fin_d)[...], lambda r: fetch(r, fin_d)[...]), su.take(turn[0])),
        (2, 0): lambda: su.take(turn[1]),
        (2, 1): lambda: (su.take(turn[2]), sd.forward()),
    }
    for p in range(pairs):
        prepare(p)
        key_block(p, 0)
        jobs.get((p, 0), lambda: None)()
        pl.loop(1, ns)(lambda j, p=p: key_block(p, j))
        dq_v[:, 128 * p : 128 * (p + 1)] = (dqacc[...] * scale).astype(bf16)
        jobs.get((p, 1), lambda: None)()

    tile = min(256, blk)
    gsum[...] = jnp.zeros_like(gsum)

    def turn_block(r):
        @pl.loop(0, blk // tile)
        def _(i):
            rows = pl.ds(pl.multiple_of(r * blk + i * tile, tile), tile)
            part_rows = pl.ds(pl.multiple_of(i * tile, tile), tile)
            loads = [
                keep(raw_hbm.at[rows], raw_t, 0), keep(cos_hbm.at[r, part_rows], cos_t, 7), keep(sin_hbm.at[r, part_rows], sin_t, 8),
            ]
            for a in loads:
                a.start()
            for a in loads:
                a.wait()
            cosine, sine = cos_t[...], sin_t[...]
            for p in range(pairs + 1):
                which = 0 if p < pairs else 1
                lanes = slice(128 * p, 128 * (p + 1))
                grad = dq_v[rows, lanes].astype(f32) if p < pairs else dk_acc[rows, :].astype(bf16).astype(f32)
                raw = raw_t[:, lanes]
                inv = lax.rsqrt(head_sums(raw * raw) * (1.0 / 64) + epsilon)
                normal = raw * inv
                grad = grad * cosine - half_swap(grad) * sine
                gsum[which] += jnp.sum((grad * normal).reshape(tile // 8, 8, 128), axis=0)
                grad = grad * gain_ref[which : which + 1, :]
                mean = head_sums(grad * normal) * (1.0 / 64)
                dqkv[rows, lanes] = (inv * (grad - normal * mean)).astype(bf16)
            dqkv[rows, 128 * (pairs + 1) :] = dv_acc[rows, :].astype(bf16)
            dnv[{3: 0, 2: 1, 1: 2, 0: 0}[r], part_rows, :] = dg(dqkv[rows, :], wq_ref[...], NT).astype(bf16)

    dn1 = send(dnv.at[2], dn_out.at[1], 10, near)
    dn3 = send(dnv.at[0], dn_g3, 11, near)
    dnf = send(dnv.at[1], dn_out.at[2], 12, far)
    turn_block(3)
    dn3.start()
    turn_block(2)
    dn3.wait()
    fetch(dn_g3, dnv.at[0])

    @pl.loop(0, blk // chunk)
    def _(i):
        rows = pl.ds(pl.multiple_of(i * chunk, chunk), chunk)
        dnv[1, rows, :] = (dnv[1, rows, :].astype(f32) + dnv[0, rows, :].astype(f32)).astype(bf16)

    dnf.start()
    lof.wait_send()
    turn_block(1)
    dn1.start()
    su.take(turn[3]) if outer > 3 else None
    turn_block(0)
    own_dn = keep(dnv.at[0], dn_out.at[0], 9)
    own_dn.start()
    for k in turn[4:]:
        sg.take(k)
        su.take(k)

    drows, span = gq_send.shape[1], xh_t.shape[1]

    def grad_block(b):
        first = (b * drows) // span
        fetch(xh_hbm.at[:, pl.ds(pl.multiple_of(first * span, span), span)], xh_t)
        grad = dg(xh_t[...], dqkv[...], TN)
        if span > drows:
            grad = jnp.where(b % 2 == 0, grad[:drows], grad[drows:])
        return grad.astype(bf16)

    for k in turn:
        gq_send[k] = grad_block(2 * k + 1 - inner)
        if k != turn[0]:
            sq.cross(turn[turn.index(k) - 1]).start()
    so.take(turn[0])
    sq.cross(turn[-1]).start()
    for k in turn[1:]:
        so.take(k)
    sq.own = lambda k: grad_block(2 * k + inner)

    gslot[0] = jnp.concatenate(
        [jnp.sum(gsum[0], axis=0, keepdims=True), jnp.sum(gsum[1], axis=0, keepdims=True), jnp.zeros((6, 128), f32)]
    )
    hops = [
        send(gslot.at[0], gslot.at[3], 13, near), send(gslot.at[1], gslot.at[4], 14, far),
        send(gslot.at[2], gslot.at[5], 15, s, cross_f),
    ]
    hops[0].start()
    sg.total(None, lambda r: fetch(r, fin_g)[...])
    hops[0].wait_recv()
    gslot[1] = gslot[0] + gslot[3]
    hops[1].start()
    for k in turn:
        sq.take(k)
    hops[1].wait_recv()
    gslot[2] = gslot[1] + gslot[4]
    hops[2].start()
    so.total()
    hops[2].wait_recv()
    gline[at] = gslot[2] + gslot[5]
    lines = [
        send(gline.at[at], gline.at[at], 16 + m, s, 2 * ((at + m) % outer) + inner) for m in range(1, outer)
    ]
    for a in lines:
        a.start()
    su.total(None, lambda r: fetch(r, fin_u)[...])
    sg.forward()
    so.forward()
    for m in range(1, outer):
        k = (at + outer - m) % outer
        send(gline.at[k], gline.at[k], 16 + m, s, 2 * k + inner).wait_recv()
    total = gline[0]
    for k in range(1, outer):
        total = total + gline[k]
    dgain_ref[...] = total + pltpu.roll(total, 64, 1)
    sq.total()

    sd.finish(sent_d, False)
    for a in (sg, su, so, sq):
        a.finish()
    for a in lines + hops + datt_t + [o1, o3, lo1, lo3, dn1, dnf]:
        a.wait_send()
    for a in (lo1, lof, dn1, dnf):
        a.wait_recv()
    own_dn.wait()


def back_call(datt, q, laug, o, k, v, raw, cosine, sine, start_row, n_live, gains, w_qkv, xh, gd, gg, gu, att, dmid, lo, nf, ns, quarter, group, head):
    outer = gd.shape[0]
    T = q.shape[0]
    blk = T // ns
    width, cols = w_qkv.shape
    pairs = cols // 128 - 2
    q_cols = pairs * 128
    scale = head**-0.5
    c = math.log2(math.e) * scale
    hbm, vmem = pl.BlockSpec(memory_space=pl.ANY), pl.BlockSpec(memory_space=pltpu.VMEM)
    S, V = jax.ShapeDtypeStruct, pltpu.VMEM
    dblk, gblk, oblk = gd.shape[1:], gg.shape[1:], (quarter, width)
    drows = gblk[0]
    qblk = (drows, cols)
    half = (T, 128)
    wide = (T, 256)
    per = 2 * outer + 3
    return pl.pallas_call(
        functools.partial(back_kernel, outer, ns, pairs, group, c, scale),
        in_specs=[hbm] + [vmem] * 5 + [hbm] * 3 + [vmem] * 4 + [hbm] * 7,
        out_specs=[hbm] * 4 + [vmem, hbm, vmem] + [hbm] * 7 + [vmem],
        out_shape=[
            S((3, blk, width), bf16), S((2, blk, width), bf16),
            S((ns,) + dblk, bf16), S((ns,) + gblk, bf16), S(gblk, bf16), S((ns,) + oblk, bf16), S(qblk, bf16),
            S((2 * outer, ns) + oblk, bf16),
            S((blk, width), bf16), S((blk, width), bf16), S((2 * outer,) + oblk, bf16), S((outer,) + dblk, bf16), S((outer,) + gblk, bf16), S((outer,) + gblk, bf16),
            S((8, 128), f32),
        ],
        scratch_shapes=[
            V((T, q_cols), bf16), V(half, bf16), V(half, bf16), V(wide, bf16), V(half, bf16), V(half, bf16), V(wide, bf16),
            V(wide, bf16), V(wide, bf16), V(wide, bf16), V(wide, bf16),
            V(half, f32), V((T, q_cols), bf16), V(half, f32), V(half, f32),
            V((T, cols), bf16), V((3, blk, width), bf16),
            V((min(256, blk), q_cols + 128), f32), V((min(256, blk), 128), f32), V((min(256, blk), 128), f32),
            V((T, drows if drows % 128 == 0 else 2 * drows), bf16), V((outer,) + qblk, bf16),
            V((outer,) + gblk, bf16), V((outer,) + gblk, bf16), V((outer,) + oblk, bf16), V((outer,) + qblk, bf16),
            V((outer,) + oblk, bf16), V((outer,) + qblk, bf16),
            V(dblk, bf16), V(gblk, bf16), V(oblk, bf16),
            V(gblk, bf16), V((2 * outer,) + oblk, bf16), V((2, 2 * outer) + oblk, bf16),
            V((2, 8, 128), f32), V((6, 8, 128), f32), V((outer, 8, 128), f32),
            pltpu.SemaphoreType.DMA((2, 5 * per)), pltpu.SemaphoreType.DMA((2, 16 + outer)), pltpu.SemaphoreType.DMA((10 + outer,)),
        ],
        compiler_params=pltpu.CompilerParams(
            collective_id=1, has_side_effects=True, vmem_limit_bytes=63 * 2**20
        ),
        cost_estimate=tiny,
        name="back",
    )(datt, q, laug, o, k, v, raw, cosine, sine, start_row, n_live, gains, w_qkv, xh, gd, gg, gu, att, dmid, lo)


def ffn_kernel(tile, n2_ref, dy_ref, wg_ref, wu_ref, wd_ref, hid_ref, dg_ref, du_ref, dn_ref):
    n2, dy = n2_ref[...], dy_ref[...]
    units, width = wd_ref.shape
    for j in range(units // tile):
        cols = slice(j * tile, (j + 1) * tile)
        gate = dg(n2, wg_ref[0, :, cols], NN)
        up = dg(n2, wu_ref[0, :, cols], NN)
        dhid = dg(dy, wd_ref[cols, :], NT)
        sig = jax.nn.sigmoid(gate)
        act = gate * sig
        hid_ref[:, cols] = (act * up).astype(bf16)
        du_ref[:, cols] = (dhid * act).astype(bf16)
        dg_ref[:, cols] = (dhid * up * (sig * (1.0 + gate * (1.0 - sig)))).astype(bf16)
    for j in range(width // 512):
        rows = slice(j * 512, (j + 1) * 512)
        grad = dg(dg_ref[...], wg_ref[0, rows, :], NT) + dg(du_ref[...], wu_ref[0, rows, :], NT)
        dn_ref[:, rows] = grad.astype(bf16)


def ffn_call(n2_all, dy_all, w_gu, w_d, rows=256, tile=256):
    length, width = n2_all.shape
    units = w_d.shape[0]
    once = pl.Buffered(1)
    big = jax.ShapeDtypeStruct((length, units), bf16)
    return pl.pallas_call(
        functools.partial(ffn_kernel, tile),
        grid=(length // rows,),
        in_specs=[pl.BlockSpec((rows, width), lambda i: (i, 0))] * 2
        + [
            pl.BlockSpec((1, width, units), lambda i: (0, 0, 0), pipeline_mode=once),
            pl.BlockSpec((1, width, units), lambda i: (1, 0, 0), pipeline_mode=once),
            pl.BlockSpec((units, width), lambda i: (0, 0), pipeline_mode=once),
        ],
        out_specs=[pl.BlockSpec((rows, units), lambda i: (i, 0))] * 3 + [pl.BlockSpec((rows, width), lambda i: (i, 0))],
        out_shape=[big, big, big, jax.ShapeDtypeStruct((length, width), bf16)],
        compiler_params=pltpu.CompilerParams(vmem_limit_bytes=62 * 2**20),
        cost_estimate=tiny,
        name="ffn",
    )(n2_all, dy_all, w_gu, w_gu, w_d)


def join_kernel(members, shards, shard, unit, gain_ref, m_ref, w_ref, out_ref, sum_ref):
    for k in range(members):
        width = min(unit, shard - k * unit)
        for j in range(shards):
            part = m_ref[k, :, j * unit : j * unit + width].astype(f32)
            out_ref[:, j * shard + k * unit : j * shard + k * unit + width] = part
    full = out_ref[...]
    sum_ref[...] = jnp.broadcast_to(
        jnp.sum(full * w_ref[...].astype(f32), axis=-1, keepdims=True), sum_ref.shape
    )
    out_ref[...] = full * gain_ref[...]


def join_call(gain, stacked, weight, members, shards, shard, unit):
    rows, cols = weight.shape
    tile = min(64, rows)
    return pl.pallas_call(
        functools.partial(join_kernel, members, shards, shard, unit),
        grid=(rows // tile,),
        in_specs=[
            pl.BlockSpec((tile, 1), lambda i: (i, 0)),
            pl.BlockSpec((members, tile, shards * unit), lambda i: (0, i, 0)),
            pl.BlockSpec((tile, cols), lambda i: (i, 0)),
        ],
        out_specs=[
            pl.BlockSpec((tile, cols), lambda i: (i, 0)),
            pl.BlockSpec((tile, 128), lambda i: (i, 0)),
        ],
        out_shape=[
            jax.ShapeDtypeStruct((rows, cols), f32),
            jax.ShapeDtypeStruct((rows, 128), f32),
        ],
        compiler_params=pltpu.CompilerParams(vmem_limit_bytes=60 * 2**20),
        name="join_units",
    )(gain, stacked, weight)


def heads_kernel(members, q_cols, kv_base, gain_ref, m_ref, wq_ref, wk_ref, wv_ref, q_ref, k_ref, v_ref, sum_ref):
    for k in range(members):
        q_ref[:, k * q_cols : (k + 1) * q_cols] = m_ref[k, :, :q_cols].astype(f32)
    for n, ref in enumerate((k_ref, v_ref)):
        at = q_cols + 128 * n
        ref[...] = jnp.zeros_like(ref)
        for k in range(members):
            ref[:, kv_base[k] : kv_base[k] + 128] += m_ref[k, :, at : at + 128].astype(f32)
    total = 0.0
    for ref, w in ((q_ref, wq_ref), (k_ref, wk_ref), (v_ref, wv_ref)):
        full = ref[...]
        total = total + jnp.sum(full * w[...].astype(f32), axis=-1, keepdims=True)
        ref[...] = full * gain_ref[...]
    sum_ref[...] = jnp.broadcast_to(total, sum_ref.shape)


def heads_call(gain, stacked, w_query, w_key, w_value, kv_base, q_cols):
    members, rows, cols = stacked.shape
    tile = min(64, rows)
    outs = [w_query.shape[1], w_key.shape[1], w_value.shape[1], 128]
    return pl.pallas_call(
        functools.partial(heads_kernel, members, q_cols, kv_base),
        grid=(rows // tile,),
        in_specs=[pl.BlockSpec((tile, 1), lambda i: (i, 0)), pl.BlockSpec((members, tile, cols), lambda i: (0, i, 0))]
        + [pl.BlockSpec((tile, n), lambda i: (i, 0)) for n in outs[:3]],
        out_specs=[pl.BlockSpec((tile, n), lambda i: (i, 0)) for n in outs],
        out_shape=[jax.ShapeDtypeStruct((rows, n), f32) for n in outs],
        compiler_params=pltpu.CompilerParams(vmem_limit_bytes=60 * 2**20),
        name="join_heads",
    )(gain, stacked, w_query, w_key, w_value)


def dot_bf(a, b, dims):
    return dg(a, b, dims).astype(bf16)


def local(
    tokens, seg_ids, pad_mask, positions, attn_gain, w_query, w_key, w_value, query_gain,
    key_gain, w_out, ffn_gain, w_gate, w_up, w_down, cotangent,
):
    nf, ns = lax.axis_size("fsdp"), lax.axis_size("sp")
    f, s = lax.axis_index("fsdp"), lax.axis_index("sp")
    seq_count, blk, width = tokens.shape
    assert seq_count == 1 and ns == 4
    length = blk * ns
    head = query_gain.shape[0]
    q_heads, kv_heads = w_query.shape[1] // head, w_key.shape[1] // head
    group = q_heads // kv_heads
    q_local = q_heads // ns
    kv_base = [(q_local * k) // group for k in range(ns)]
    pairs = q_local // 2
    q_cols = q_local * head
    kv_map = jnp.array(
        [[(q_local * k + 2 * p) // group - kv_base[k] for p in range(pairs)] for k in range(ns)],
        jnp.int32,
    )[s]
    base = jnp.array(kv_base, jnp.int32)[s] * head
    shard = w_down.shape[0]
    unit = -(-(-(-shard // ns)) // 16) * 16
    units = unit * nf
    out_rows = w_out.shape[0]
    quarter = out_rows // ns
    sub = 512

    x = tokens[0]
    dy = cotangent[0]
    gain_one = attn_gain.astype(f32)[:, None]
    gain_two = ffn_gain.astype(f32)[:, None]

    kv_cols = 2 * head
    out_mine = lax.dynamic_slice_in_dim(w_out, s * quarter, quarter, 0)
    small = jnp.concatenate(
        [positions.astype(f32), pad_mask.astype(f32), jnp.zeros((6, blk), f32)]
    )
    gains = jnp.concatenate(
        [
            jnp.tile(query_gain.astype(f32), 2)[None],
            jnp.tile(key_gain.astype(f32), 2)[None],
            jnp.zeros((6, 2 * head), f32),
        ]
    )
    (
        xh, dy_all, n2_all, w_d, w_gu, w_qkv, w_out_rel, att, q, k, v, raw, cosine, sine,
        attended, laug, middle, inv_two, small_all,
    ) = front_call(
        x, dy, small, w_query, w_key, w_value, out_mine, w_down, w_gate, w_up,
        jnp.broadcast_to(gain_one, (width // nf, 128)), jnp.broadcast_to(gain_two, (width // nf, 128)), gains,
        nf, ns, group, head, unit, kv_base, q_cols,
    )
    xh = xh.reshape(length, width)
    w_d, w_gu = w_d.reshape(units, width), w_gu.reshape(2, width, units)
    w_out_rel = w_out_rel.reshape(ns * q_cols, width)
    pos_rel = small_all[:, 0].astype(jnp.int32)
    n_live = jnp.sum(small_all[:, 1]).astype(jnp.int32)
    true_block = s ^ jnp.arange(ns)
    start_rel = (true_block[:, None] * blk + jnp.arange(blk)[None] - pos_rel).reshape(length)
    xf = x.astype(f32)
    inv_two = inv_two[:, :1]

    n2_all, dy_all = n2_all.reshape(length, width), dy_all.reshape(length, width)
    hidden, dgate, dup, dn2 = ffn_call(n2_all, dy_all, w_gu, w_d)
    dn2 = [dn2[r * blk : (r + 1) * blk] for r in range(ns)]
    got3 = perm_s(dn2[3], 1)
    got1 = perm_s(dn2[1], 1)
    pair = (dn2[2].astype(f32) + got3.astype(f32)).astype(bf16)
    dn2_far = perm_s(pair, 2)

    hidden_a = after(hidden, pair, got1)
    grad_d = dot_bf(hidden_a, dy_all, TN).reshape(nf // 2, 2, unit, width)
    d_own = lax.dynamic_index_in_dim(grad_d, f % 2, 1, keepdims=False)
    d_other = lax.dynamic_index_in_dim(grad_d, 1 - f % 2, 1, keepdims=False)
    d_got = perm_f(d_other, 1)
    dgate_a, dup_a = after(dgate, d_other), after(dup, d_other)
    grad_g = dot_bf(n2_all, dgate_a, TN).reshape(nf, width // nf, units)
    grad_u = dot_bf(n2_all, dup_a, TN).reshape(nf, width // nf, units)
    lo = dot_bf(hidden_a, w_d, NN).reshape(ns, blk, width)

    dn2_own = dn2[0].astype(f32) + got1.astype(f32) + dn2_far.astype(f32)
    hat_two = middle * inv_two
    dmiddle = dy.astype(f32) + inv_two * (
        dn2_own - hat_two * jnp.mean(dn2_own * hat_two, axis=-1, keepdims=True)
    )
    dmid = dmiddle.astype(bf16)
    datt = dot_bf(dmid, w_out_rel, NT)
    gd = (d_own.astype(f32) + after(d_got, dmid).astype(f32)).astype(bf16)

    live_row = jnp.full((8, 128), n_live, jnp.int32)
    dn, lo_got, sum_d, sum_g, fin_u, sum_o, fin_q, _, _, _, _, _, _, _, dgain = back_call(
        datt, q, laug, attended, k, v, raw, cosine, sine, jnp.broadcast_to(start_rel[None], (8, length)),
        live_row, gains, w_qkv, xh, gd, grad_g, grad_u, att, dmid, lo, nf, ns, quarter, group, head,
    )
    u_pieces, q_pieces = gather_s(fin_u), gather_s(fin_q)
    layer_out = (
        middle + lo[0].astype(f32) + lo_got[0].astype(f32) + lo_got[1].astype(f32)
    ).astype(bf16)
    w_down_grad = sum_d.reshape(ns * unit, width)[:shard].astype(f32)
    w_gate_grad, gate_sum = join_call(gain_two, sum_g, w_gate, ns, nf, shard, unit)
    w_up_grad, up_sum = join_call(gain_two, place(u_pieces, s), w_up, ns, nf, shard, unit)
    ffn_gain_grad = (gate_sum + up_sum)[:, 0]
    w_out_grad = sum_o.reshape(out_rows, width).astype(f32)

    dn_own = dn[0].astype(f32) + dn[1].astype(f32) + dn[2].astype(f32)
    inv_one = lax.rsqrt(jnp.mean(xf * xf, axis=-1, keepdims=True) + epsilon)
    hat_one = xf * inv_one
    tokens_grad = (
        dmiddle + inv_one * (dn_own - hat_one * jnp.mean(dn_own * hat_one, axis=-1, keepdims=True))
    ).astype(bf16)
    query_gain_grad, key_gain_grad = dgain[0, :head], dgain[1, :head]

    w_query_grad, w_key_grad, w_value_grad, one_sum = heads_call(
        gain_one, place(q_pieces, s), w_query, w_key, w_value, [k * head for k in kv_base], q_cols
    )
    attn_gain_grad = one_sum[:, 0]
    return (
        layer_out[None], tokens_grad[None], attn_gain_grad, w_query_grad, w_key_grad,
        w_value_grad, query_gain_grad, key_gain_grad, w_out_grad, ffn_gain_grad,
        w_gate_grad, w_up_grad, w_down_grad,
    )


def solution(mesh):
    row, vec = P("fsdp", None), P("fsdp")
    tok, ids = P("fsdp", "sp", None), P("fsdp", "sp")
    in_specs = (tok, ids, ids, ids, vec, row, row, row, P(), P(), row, vec, row, row, row, tok)
    out_specs = (tok, tok, vec, row, row, row, P(), P(), row, vec, row, row, row)
    return jax.shard_map(local, mesh=mesh, in_specs=in_specs, out_specs=out_specs, check_vma=False)
```

```python
import functools, math
import jax, jax.numpy as jnp
from jax import lax
from jax.experimental import pallas as pl
from jax.experimental.pallas import tpu as pltpu
bf16=jnp.bfloat16; f32=jnp.float32
tiny=pl.CostEstimate(flops=1000000,bytes_accessed=1000000,transcendentals=0)
NT=(((1,),(1,)),((),()))
NN=(((1,),(0,)),((),()))
TN=(((0,),(0,)),((),()))

def dg(a,b,dims):
    return lax.dot_general(a,b,dims,preferred_element_type=f32)

def lane_iota(rows, cols):
    return lax.broadcasted_iota(jnp.int32,(rows,cols),1)

def split3(v):
    hi=v.astype(bf16); r=v-hi.astype(f32)
    mid=r.astype(bf16); lo=(r-mid.astype(f32)).astype(bf16)
    return hi,mid,lo

def aug_lanes(v):
    hi,mid,lo=split3(v)
    lane=lane_iota(*v.shape)%64
    z=jnp.zeros_like(v)
    return jnp.where(lane==0,hi.astype(f32),jnp.where(lane==1,mid.astype(f32),jnp.where(lane==2,lo.astype(f32),z))).astype(bf16)


from jax.sharding import PartitionSpec as P

epsilon = 1e-06
rope_base = 10000.0


def perm_f(x, m):
    n = lax.axis_size("fsdp")
    return lax.ppermute(x, "fsdp", [(i, i ^ m) for i in range(n)])


def perm_s(x, m):
    n = lax.axis_size("sp")
    return lax.ppermute(x, "sp", [(i, i ^ m) for i in range(n)])


def after(x, *deps):
    return lax.optimization_barrier((x,) + deps)[0]


def gather_f(x, *deps):
    outer = lax.axis_size("fsdp") // 2
    x_z = after(x, *deps) if deps else x
    firsts = [x] + [perm_f(x_z, 2 * m) for m in range(1, outer)]
    pieces = []
    for first in firsts:
        pieces += [first, perm_f(first, 1)]
    return pieces


def gather_s(x):
    far = perm_s(x, 2)
    near = perm_s(x, 1)
    return [x, near, far, perm_s(far, 1)]


def place(pieces, me):
    out = jnp.zeros((len(pieces),) + pieces[0].shape, pieces[0].dtype)
    for r, piece in enumerate(pieces):
        out = lax.dynamic_update_index_in_dim(out, piece, me ^ r, 0)
    return out


def scatter_f(blocks, *deps):
    outer = blocks.shape[0] // 2
    me = lax.axis_index("fsdp")
    pairs = blocks.reshape((outer, 2) + blocks.shape[1:])
    mine = lax.dynamic_index_in_dim(pairs, me % 2, 1, keepdims=False)
    other = lax.dynamic_index_in_dim(pairs, 1 - me % 2, 1, keepdims=False)
    got = perm_f(other, 1)
    if deps:
        got = after(got, *deps)
    both = (mine.astype(f32) + got.astype(f32)).astype(bf16)
    at = me // 2
    total = lax.dynamic_index_in_dim(both, at, 0, keepdims=False).astype(f32)
    for m in range(1, outer):
        part = perm_f(lax.dynamic_index_in_dim(both, at ^ m, 0, keepdims=False), 2 * m)
        total = total + part.astype(f32)
    return total.astype(bf16)


def scatter_s(parts):
    got3 = perm_s(parts[3], 1)
    got1 = perm_s(parts[1], 1)
    far = perm_s((parts[2].astype(f32) + got3.astype(f32)).astype(bf16), 2)
    return parts[0].astype(f32) + got1.astype(f32) + far.astype(f32)


def half_swap(v):
    lane = lane_iota(*v.shape) % 64
    return jnp.where(lane < 32, pltpu.roll(v, 96, 1), pltpu.roll(v, 32, 1))


def head_sums(v):
    row = lax.broadcasted_iota(jnp.int32, (128, 128), 0) // 64
    col = lane_iota(128, 128) // 64
    same = jnp.where(row == col, 1.0, 0.0).astype(bf16)
    hi, mid, lo = split3(v)
    return dg(hi, same, NN) + dg(mid, same, NN) + dg(lo, same, NN)


def xor_small(a, b, bits=2):
    out = 0
    for i in range(bits):
        p = (a // (1 << i)) % 2
        q = (b // (1 << i)) % 2
        out = out + (p + q - 2 * p * q) * (1 << i)
    return out


class Ring:
    def __init__(self, own, slot, sems, base, outer, f, s):
        self.own, self.slot, self.sems, self.base = own, slot, sems, base
        self.outer, self.f, self.s = outer, f, s
        self.at, self.inner = f // 2, f % 2

    def copy(self, src, dst, send, recv, to):
        return pltpu.make_async_remote_copy(
            src, dst, self.sems.at[0, self.base + send], self.sems.at[1, self.base + recv],
            device_id=(to, self.s), device_id_type=pl.DeviceIdType.MESH,
        )

    def line(self, k, sign):
        n = self.outer
        lane = 0 if sign > 0 else n
        b = self.f - 2 * k * sign
        src = self.own if k == 0 else self.slot(b)
        return self.copy(src, self.slot(b), lane + k, lane + k + 1, self.f + 2 * sign)

    def line_wait(self, k, sign):
        n = self.outer
        lane = 0 if sign > 0 else n
        b = self.f - 2 * k * sign
        return self.copy(self.slot(b), self.slot(b), lane + k, lane + k, self.f + 2 * sign)

    def cross(self, k, sign):
        n = self.outer
        lane = 2 * n if sign > 0 else 3 * n
        b = self.f - 2 * k * sign
        src = self.own if k == 0 else self.slot(b)
        return self.copy(src, self.slot(b), lane + k, lane + k, self.f + 1 - 2 * self.inner)

    def cross_wait(self, k, sign):
        n = self.outer
        lane = 2 * n if sign > 0 else 3 * n
        b = self.f + 1 - 2 * self.inner - 2 * k * sign
        return self.copy(self.slot(b), self.slot(b), lane + k, lane + k, self.f + 1 - 2 * self.inner)

    def has(self, k, sign):
        return self.at >= k if sign > 0 else self.at + k <= self.outer - 1

    def onward(self, k, sign):
        more = self.at < self.outer - 1 if sign > 0 else self.at > 0
        return more if k == 0 else jnp.logical_and(more, self.has(k, sign))

    def start(self):
        for sign in (1, -1):
            pl.when(self.onward(0, sign))(lambda sign=sign: self.line(0, sign).start())

    def start_cross(self):
        self.cross(0, 1).start()

    def step(self, k):
        for sign in (1, -1):
            @pl.when(self.has(k, sign))
            def _(sign=sign):
                self.line_wait(k, sign).wait_recv()

                @pl.when(self.onward(0, sign))
                def _():
                    self.line(k, sign).start()

                self.cross(k, sign).start()

    def finish(self):
        for k in range(self.outer):
            for sign in (1, -1) if k else (1,):
                if k:
                    @pl.when(self.has(k, sign))
                    def _(k=k, sign=sign):
                        self.cross_wait(k, sign).wait_recv()
                        self.cross(k, sign).wait_send()
                else:
                    self.cross_wait(0, 1).wait_recv()
                    self.cross(0, 1).wait_send()
        for k in range(self.outer - 1):
            for sign in (1, -1):
                @pl.when(self.onward(k, sign))
                def _(k=k, sign=sign):
                    self.line(k, sign).wait_send()


def ring_sems(outer):
    return 4 * outer


def front_kernel(outer, ns, pairs, group, c, inv_log, unit, kv_base,
                 x_hbm, dy_hbm, small_ref, wq_ref, wk_ref, wv_ref, out_hbm, down_w, gate_w, up_w, one_ref, two_ref, gain_ref,
                 xh_hbm, dy_all, n2_all, w_d, w_gu, w_qkv_out, w_out_out, att_tok_out,
                 q_ref, k_ref, v_ref, raw_ref, cos_ref, sin_ref, o_ref, laug_ref, mid_ref, inv_ref, small_out,
                 qkv_hbm, down_hbm, gu_hbm, gate_v, up_v, xv, wq, ow, smalls, start_col, att_in, nv, ka, kb, ra, rb, ral, rbl,
                 rsem, tsem, lsem):
    f, s = lax.axis_index("fsdp"), lax.axis_index("sp")
    nf = 2 * outer
    core = s % 2
    near, far = s + 1 - 2 * core, s + 2 - 4 * (s // 2)
    diag = far + 1 - 2 * core
    at, inner = f // 2, f % 2
    blk, width = x_hbm.shape
    T = ns * blk
    q_cols = pairs * 128
    drows = qkv_hbm.shape[0]
    quarter = out_hbm.shape[0]

    shard, units = down_w.shape[0], gu_hbm.shape[2]

    one = one_ref[:, 0:1]
    qkv_hbm[:, :q_cols] = (wq_ref[:, pl.ds(pl.multiple_of(s * q_cols, 128), q_cols)].astype(f32) * one).astype(bf16)
    for n in range(ns):

        @pl.when(s == n)
        def _(n=n):
            for m, ref in enumerate((wk_ref, wv_ref)):
                part = ref[:, kv_base[n] : kv_base[n] + 128].astype(f32)
                qkv_hbm[:, q_cols + 128 * m : q_cols + 128 * (m + 1)] = (part * one).astype(bf16)

    barrier = pltpu.get_barrier_semaphore()

    def greet(ff, ss):
        pl.semaphore_signal(barrier, inc=1, device_id=(ff, ss), device_id_type=pl.DeviceIdType.MESH)

    greet(f, near)
    greet(f, far)
    greet(f, diag)
    greet(f + 1 - 2 * inner, s)
    pl.when(at < outer - 1)(lambda: greet(f + 2, s))
    pl.when(at > 0)(lambda: greet(f - 2, s))
    middle_of_line = jnp.logical_and(at > 0, at < outer - 1)
    pl.when(middle_of_line)(lambda: pl.semaphore_wait(barrier, 6))
    pl.when(jnp.logical_not(middle_of_line))(lambda: pl.semaphore_wait(barrier, 5))

    def send(src, dst, n, to):
        return pltpu.make_async_remote_copy(
            src, dst, tsem.at[0, n], tsem.at[1, n], device_id=(f, to), device_id_type=pl.DeviceIdType.MESH
        )

    def keep(src, dst, n):
        return pltpu.make_async_copy(src, dst, lsem.at[n])

    per = ring_sems(outer)
    qkv = Ring(qkv_hbm, lambda b: wq.at[pl.ds(pl.multiple_of(b * drows, drows), drows)], rsem, 0, outer, f, s)
    out = Ring(out_hbm, lambda b: ow.at[b, s], rsem, per, outer, f, s)
    down = Ring(down_hbm, lambda b: w_d.at[b], rsem, 2 * per, outer, f, s)
    gate = Ring(gu_hbm.at[0], lambda b: w_gu.at[0, b], rsem, 3 * per, outer, f, s)
    up = Ring(gu_hbm.at[1], lambda b: w_gu.at[1, b], rsem, 4 * per, outer, f, s)

    def triple(base, own, slot):
        return (
            send(own, slot(1), base, near), send(own, slot(2), base + 1, far), send(slot(2), slot(3), base + 2, near),
        )

    load_g = pltpu.make_async_copy(gate_w, gate_v, lsem.at[3])
    load_u = pltpu.make_async_copy(up_w, up_v, lsem.at[4])
    small_t = triple(0, small_ref, lambda r: smalls.at[r])
    tok_t = triple(3, x_hbm, lambda r: xv.at[r])
    most = blk * 3 // 4
    rows_a, rows_b = pl.ds(0, most), pl.ds(most, blk - most)
    dy_t = triple(9, dy_hbm.at[rows_a], lambda r: dy_all.at[r, rows_a])
    dy_u = triple(18, dy_hbm.at[rows_b], lambda r: dy_all.at[r, rows_b])
    small_t[0].start()
    small_t[1].start()
    tok_t[1].start()
    tok_t[0].start()
    load_x = keep(x_hbm, xv.at[0], 0)
    load_x.start()
    wq[pl.ds(pl.multiple_of(f * drows, drows), drows), :] = qkv_hbm[...]
    load_o = keep(out_hbm, ow.at[f, s], 2)
    load_o.start()
    qkv.start()
    qkv.start_cross()
    out.start()
    out.start_cross()
    smalls[0] = small_ref[...]
    load_g.start()
    load_u.start()
    down_hbm[...] = jnp.zeros_like(down_hbm)
    for n in range(ns):
        count = min(unit, shard - n * unit)
        if count <= 0:
            continue

        @pl.when(s == n)
        def _(n=n, count=count):
            a = pltpu.make_async_copy(down_w.at[pl.ds(n * unit, count)], down_hbm.at[pl.ds(0, count)], lsem.at[5])
            a.start()
            a.wait()

    small_t[1].wait_recv()
    small_t[2].start()
    for k in range(1, outer):
        qkv.step(k)
        out.step(k)
    down.start()
    down.start_cross()
    load_g.wait()
    load_u.wait()
    two = two_ref[:, 0:1]
    gu_hbm[...] = jnp.zeros_like(gu_hbm)
    for n in range(ns):
        count = min(unit, shard - n * unit)
        if count <= 0:
            continue

        @pl.when(s == n)
        def _(n=n, count=count):
            for m, ref in enumerate((gate_v, up_v)):
                for j in range(nf):
                    part = ref[:, j * shard + n * unit : j * shard + n * unit + count].astype(f32)
                    gu_hbm[m, :, j * unit : j * unit + count] = (part * two).astype(bf16)

    own_w = [keep(down_hbm, w_d.at[f], 3), keep(gu_hbm.at[0], w_gu.at[0, f], 4), keep(gu_hbm.at[1], w_gu.at[1, f], 5)]

    small_t[0].wait_recv()
    small_t[2].wait_recv()
    half = 32
    lane = lane_iota(blk, 128)
    freq = jnp.exp((lane % half).astype(f32) * inv_log)
    sign = jnp.where(lane % 64 < half, -1.0, 1.0)
    row = lax.broadcasted_iota(jnp.int32, (blk, 1), 0)
    live = jnp.zeros((1, 1), f32)
    for r in range(ns):
        ints = smalls[r]
        small_out[r] = ints
        col = jnp.transpose(ints)[:, 0:1]
        angle = col * freq
        cos_ref[r] = jnp.cos(angle)
        sin_ref[r] = jnp.sin(angle) * sign
        t = xor_small(s, r)
        start_col[r] = t * blk + row - col.astype(jnp.int32)
        live = live + jnp.sum(ints[1:2, :], axis=1, keepdims=True)
    n_live = live.astype(jnp.int32)
    gate.start()
    gate.start_cross()
    for a in own_w:
        a.start()

    def project_block(r):
        tile = min(256, blk)

        @pl.loop(0, blk // tile)
        def _(i):
            rows = pl.ds(pl.multiple_of(i * tile, tile), tile)
            x = xv[r, rows, :].astype(f32)
            scale = lax.rsqrt(jnp.mean(x * x, axis=-1, keepdims=True) + epsilon)
            xh = (x * scale).astype(bf16)
            xv[r, rows, :] = xh
            raw = dg(xh, wq[...], NN)
            cosine, sine = cos_ref[r, rows, :], sin_ref[r, rows, :]
            to = pl.ds(pl.multiple_of(r * blk + i * tile, tile), tile)
            for p in range(pairs + 1):
                part = raw[:, 128 * p : 128 * (p + 1)]
                raw_ref[to, 128 * p : 128 * (p + 1)] = part
                inv = lax.rsqrt(head_sums(part * part) * (1.0 / 64) + epsilon)
                normal = part * inv * gain_ref[(0 if p < pairs else 1) : (1 if p < pairs else 2), :]
                turned = (normal * cosine + half_swap(normal) * sine).astype(bf16)
                if p < pairs:
                    q_ref[to, 128 * p : 128 * (p + 1)] = turned
                else:
                    k_ref[to, :] = turned
            v_ref[to, :] = raw[:, 128 * (pairs + 1) :].astype(bf16)

    load_x.wait()
    load_o.wait()
    qkv.finish()
    out.finish()
    out_t = (
        send(ow.at[:, s], ow.at[:, s], 6, near),
        send(ow.at[:, s], ow.at[:, s], 7, far),
        send(ow.at[:, far], ow.at[:, far], 8, near),
    )
    out_w = (
        send(ow.at[:, near], ow.at[:, near], 6, near),
        send(ow.at[:, far], ow.at[:, far], 7, far),
        send(ow.at[:, diag], ow.at[:, diag], 8, near),
    )
    out_t[0].start()
    out_t[1].start()
    dy_t[1].start()
    dy_t[0].start()
    project_block(0)
    keep(xv.at[0], xh_hbm.at[0], 0).start()
    tok_t[1].wait_recv()
    tok_t[2].start()
    tok_t[0].wait_recv()
    down.step(1)
    project_block(1)
    keep(xv.at[1], xh_hbm.at[1], 1).start()
    tok_t[2].wait_send()
    project_block(2)
    keep(xv.at[2], xh_hbm.at[2], 2).start()
    tok_t[2].wait_recv()
    up.start()
    up.start_cross()
    project_block(3)
    for a in own_w:
        a.wait()
    keep(xv.at[3], xh_hbm.at[3], 3).start()
    tok_t[0].wait_send()
    tok_t[1].wait_send()

    low = lane_iota(blk, 128) < 64
    row_b = lax.broadcasted_iota(jnp.int32, (blk, 128), 0)

    def pos(t):
        return pl.multiple_of(xor_small(t, s) * blk, blk)

    def prepare(p):
        kv = (pairs * 2 * s + 2 * p) // group - (pairs * 2 * s) // group
        first = kv == 0
        one_a = jnp.where(low, 1.0, 0.0)
        one_b = 1.0 - one_a
        for r in range(ns):
            here = slice(r * blk, (r + 1) * blk)
            kk, vv = k_ref[here, :].astype(f32), v_ref[here, :].astype(f32)
            ksw, vsw = pltpu.roll(kk, 64, 1), pltpu.roll(vv, 64, 1)
            k0, k1 = jnp.where(first, kk, ksw), jnp.where(first, ksw, kk)
            v0, v1 = jnp.where(first, vv, vsw), jnp.where(first, vsw, vv)
            ka[here, :] = jnp.where(low, k0, 0.0).astype(bf16)
            kb[here, :] = jnp.where(low, 0.0, k1).astype(bf16)
            va, vb = jnp.where(low, v0, 0.0), jnp.where(low, 0.0, v1)
            seen = row_b < n_live - xor_small(s, r) * blk
            ra[here, :128], ra[here, 128:] = va.astype(bf16), one_a.astype(bf16)
            rb[here, :128], rb[here, 128:] = vb.astype(bf16), one_b.astype(bf16)
            ral[here, :128] = jnp.where(seen, va, 0.0).astype(bf16)
            ral[here, 128:] = jnp.where(seen, one_a, 0.0).astype(bf16)
            rbl[here, :128] = jnp.where(seen, vb, 0.0).astype(bf16)
            rbl[here, 128:] = jnp.where(seen, one_b, 0.0).astype(bf16)

    kcol = lane_iota(blk, blk)
    qrow = lax.broadcasted_iota(jnp.int32, (blk, blk), 0)

    def query_block(p, i):
        qo = pos(i)
        here = pl.ds(qo, blk)
        lanes = slice(128 * p, 128 * (p + 1))
        q = q_ref[here, lanes]
        st = start_col[xor_small(i, s)]
        ok = (kcol >= st - i * blk) & (kcol <= qrow) & ((kcol < n_live - i * blk) | (kcol == qrow))
        p0 = jnp.where(ok, jnp.exp2(dg(q, ka[here, :], NT) * c), 0.0).astype(bf16)
        p1 = jnp.where(ok, jnp.exp2(dg(q, kb[here, :], NT) * c), 0.0).astype(bf16)
        acc = dg(p0, ra[here, :], NN) + dg(p1, rb[here, :], NN)

        def key_block(j, acc):
            there = pl.ds(pos(j), blk)
            ok = kcol >= (st - j * blk)
            p0 = jnp.where(ok, jnp.exp2(dg(q, ka[there, :], NT) * c), 0.0).astype(bf16)
            p1 = jnp.where(ok, jnp.exp2(dg(q, kb[there, :], NT) * c), 0.0).astype(bf16)
            return acc + dg(p0, ral[there, :], NN) + dg(p1, rbl[there, :], NN)

        acc = lax.fori_loop(0, i, key_block, acc)
        total = acc[:, 128:]
        o_ref[here, lanes] = (acc[:, :128] / total).astype(bf16)
        laug_ref[here, lanes] = aug_lanes(jnp.log(total) * (-8.0))

    jobs = [
        lambda: (gate.step(1), out_t[0].wait_send()),
        lambda: (down.step(2), out_w[1].wait_recv(), out_t[2].start()),
        lambda: gate.step(2),
        lambda: down.step(3) if outer > 3 else None,
        lambda: up.step(1) if outer > 3 else None,
        lambda: None,
    ]
    for p in range(pairs):
        prepare(p)
        pl.loop(0, ns - 1)(lambda i, p=p: query_block(p, i))
        if 2 * p < len(jobs):
            jobs[2 * p]()
        query_block(p, ns - 1)
        if 2 * p + 1 < len(jobs):
            jobs[2 * p + 1]()
    for job in jobs[2 * pairs :]:
        job()

    att_t = [
        send(o_ref.at[pl.ds(r * blk, blk)], att_in.at[r], 11 + r, to) for r, to in ((1, near), (2, far), (3, diag))
    ]
    att_t[1].start()
    att_t[2].start()
    att_t[0].start()
    dy_u[1].start()
    dy_u[0].start()
    gate.step(3) if outer > 3 else None
    up.step(2) if outer > 3 else None
    for k in range(4, outer):
        down.step(k)
        gate.step(k)
    for n in range(4):
        keep(xv.at[n], xh_hbm.at[n], n).wait()
    reload = keep(x_hbm, xv.at[0], 0)
    reload.start()
    load_dy = keep(dy_hbm, xv.at[1], 1)
    load_dy.start()
    out_w[0].wait_recv()
    out_w[2].wait_recv()
    out_t[1].wait_send()
    out_t[2].wait_send()
    att_in[0] = o_ref[pl.ds(0, blk), :]
    reload.wait()
    load_dy.wait()
    own_dy = keep(xv.at[1], dy_all.at[0], 1)
    own_dy.start()
    own_dy.wait()
    for a in att_t:
        a.wait_recv()
    tile = 512
    shards = nf // ns
    squares = jnp.zeros((blk, 1), f32)
    for n in range(width // tile):
        cols = slice(n * tile, (n + 1) * tile)
        acc = xv[0, :, cols].astype(f32)
        for r in range(ns):
            t = xor_small(s, r)
            w = ow[pl.ds(t * shards, shards), :, :, cols].reshape(q_cols, tile)
            acc = acc + dg(att_in[r], w, NN)
        mid_ref[:, cols] = acc
        squares = squares + jnp.sum(acc * acc, axis=-1, keepdims=True)
    inv = lax.rsqrt(squares * (1.0 / width) + epsilon)
    inv_ref[...] = jnp.broadcast_to(inv, inv_ref.shape)
    for n in range(width // tile):
        cols = slice(n * tile, (n + 1) * tile)
        nv[:, cols] = (mid_ref[:, cols] * inv).astype(bf16)
    n2_t = triple(15, nv, lambda r: n2_all.at[r])
    n2_t[1].start()
    n2_t[0].start()
    keeps = [keep(nv, n2_all.at[0], 0), keep(wq, w_qkv_out, 1)]
    for r in range(ns):
        part = ow.at[pl.ds(xor_small(s, r) * shards, shards)]
        keeps.append(keep(part, w_out_out.at[r], 2 + r))
        keeps.append(keep(att_in.at[r], att_tok_out.at[:, pl.ds(r * q_cols, q_cols)], 2 + ns + r))
    for a in keeps:
        a.start()
    for k in range(3, outer):
        up.step(k)
    if outer <= 3:
        for k in range(2, outer):
            up.step(k)
    down.finish()
    gate.finish()
    for a in (dy_t, dy_u):
        a[1].wait_recv()
        a[2].start()
    for a in (dy_t, dy_u):
        a[0].wait()
        a[1].wait_send()
        a[2].wait()
    small_t[0].wait_send()
    small_t[1].wait_send()
    small_t[2].wait_send()
    for a in att_t:
        a.wait_send()
    n2_t[1].wait_recv()
    n2_t[2].start()
    up.finish()
    n2_t[2].wait()
    n2_t[0].wait()
    n2_t[1].wait_send()
    for a in keeps:
        a.wait()


def front_call(x, dy, small, w_query, w_key, w_value, out_mine, w_down, w_gate, w_up, gain_one, gain_two, gains,
               nf, ns, group, head, unit, kv_base, q_cols):
    outer = nf // 2
    blk, width = x.shape
    T = blk * ns
    pairs = q_cols // 128
    cols = q_cols + 256
    drows = w_query.shape[0]
    units = unit * nf
    hbm, vmem = pl.BlockSpec(memory_space=pl.ANY), pl.BlockSpec(memory_space=pltpu.VMEM)
    c = math.log2(math.e) * head**-0.5
    inv_log = -2.0 / head * math.log(rope_base)
    S = jax.ShapeDtypeStruct
    quarter = out_mine.shape[0]
    return pl.pallas_call(
        functools.partial(front_kernel, outer, ns, pairs, group, c, inv_log, unit, [b * head for b in kv_base]),
        in_specs=[hbm, hbm, vmem, vmem, vmem, vmem, hbm, hbm, hbm, hbm, vmem, vmem, vmem],
        out_specs=[hbm] * 8 + [vmem] * 11,
        out_shape=[
            S((ns, blk, width), bf16), S((ns, blk, width), bf16), S((ns, blk, width), bf16),
            S((nf, unit, width), bf16), S((2, nf, drows, units), bf16),
            S((width, cols), bf16), S((ns, nf // ns, ns, quarter, width), bf16), S((blk, ns * q_cols), bf16),
            S((T, q_cols), bf16), S((T, 128), bf16), S((T, 128), bf16), S((T, q_cols + 128), f32),
            S((ns, blk, 128), f32), S((ns, blk, 128), f32), S((T, q_cols), bf16), S((T, q_cols), bf16),
            S((blk, width), f32), S((blk, 128), f32), S((ns,) + small.shape, f32),
        ],
        scratch_shapes=[
            pltpu.VMEM((drows, cols), bf16), pltpu.VMEM((unit, width), bf16), pltpu.VMEM((2, drows, units), bf16),
            pltpu.VMEM(w_gate.shape, bf16), pltpu.VMEM(w_up.shape, bf16),
            pltpu.VMEM((ns, blk, width), bf16), pltpu.VMEM((width, cols), bf16),
            pltpu.VMEM((nf, ns, quarter, width), bf16), pltpu.VMEM((ns,) + small.shape, f32),
            pltpu.VMEM((ns, blk, 1), jnp.int32), pltpu.VMEM((ns, blk, q_cols), bf16), pltpu.VMEM((blk, width), bf16),
        ]
        + [pltpu.VMEM((T, 128), bf16)] * 2
        + [pltpu.VMEM((T, 256), bf16)] * 4
        + [
            pltpu.SemaphoreType.DMA((2, 5 * ring_sems(outer))), pltpu.SemaphoreType.DMA((2, 21)),
            pltpu.SemaphoreType.DMA((2 + 2 * ns,)),
        ],
        compiler_params=pltpu.CompilerParams(
            collective_id=0, has_side_effects=True, vmem_limit_bytes=67043328
        ),
        cost_estimate=tiny,
        name="front",
    )(x, dy, small, w_query, w_key, w_value, out_mine, w_down, w_gate, w_up, gain_one, gain_two, gains)


class Scatter:
    def __init__(self, sems, base, outer, ns, f, s, xz, own, part, zr, fin, out, local):
        self.sems, self.base, self.outer, self.f, self.s = sems, base, outer, f, s
        self.at, self.inner = f // 2, f % 2
        self.near = s + 1 - 2 * (s % 2)
        self.far = s + 2 - 4 * (s // 2)
        self.diag = self.far + 1 - 2 * (s % 2)
        self.xz, self.own, self.part, self.zr, self.fin, self.out, self.local = xz, own, part, zr, fin, out, local

    def copy(self, src, dst, send, recv, to):
        return pltpu.make_async_remote_copy(
            src, dst, self.sems.at[0, self.base + send], self.sems.at[1, self.base + recv],
            device_id=to, device_id_type=pl.DeviceIdType.MESH,
        )

    def cross(self, k):
        return self.copy(self.part(k), self.xz.at[k], k, k, (self.f + 1 - 2 * self.inner, self.s))

    def line(self, k, src=None):
        n = self.outer
        src = self.xz.at[k] if src is None else src
        return self.copy(src, self.zr.at[self.at], n + k, n + self.at, (2 * k + self.inner, self.s))

    def line_wait(self, k):
        n = self.outer
        return self.copy(self.zr.at[k], self.zr.at[k], n + k, n + k, (2 * k + self.inner, self.s))

    def take(self, k):
        self.cross(k).wait_recv()
        own = self.own(k)
        self.xz[k] = (self.xz[k].astype(f32) + own.astype(f32)).astype(bf16)
        pl.when(k != self.at)(lambda: self.line(k).start())

    def total(self, own=None, fetch=None):
        n = self.outer
        acc = (self.xz[self.at] if own is None else own).astype(f32)
        for m in range(1, n):
            k = (self.at + m) % n
            self.line_wait(k).wait_recv()
            acc = acc + (self.zr[k] if fetch is None else fetch(self.zr.at[k])).astype(f32)
        self.fin[...] = acc.astype(bf16)
        if self.out is None:
            return
        n = 2 * self.outer
        self.copy(self.fin, self.out.at[self.s], n + 1, n + 1, (self.f, self.far)).start()
        self.copy(self.fin, self.out.at[self.s], n, n, (self.f, self.near)).start()
        self.local(self.fin, self.out.at[self.s]).start()

    def forward(self):
        n = 2 * self.outer
        far = self.out.at[self.far]
        self.copy(far, far, n + 1, n + 1, (self.f, self.far)).wait_recv()
        self.copy(far, far, n + 2, n + 2, (self.f, self.near)).start()

    def finish(self, sent=None, crossed=True):
        n = 2 * self.outer
        if self.out is not None:
            near, diag = self.out.at[self.near], self.out.at[self.diag]
            self.copy(near, near, n, n, (self.f, self.near)).wait_recv()
            self.copy(diag, diag, n + 2, n + 2, (self.f, self.near)).wait_recv()
            self.copy(self.fin, near, n, n, (self.f, self.near)).wait_send()
            self.copy(self.fin, near, n + 1, n + 1, (self.f, self.far)).wait_send()
            self.copy(near, near, n + 2, n + 2, (self.f, self.near)).wait_send()
            self.local(self.fin, self.out.at[self.s]).wait()
        for k in range(self.outer):
            if crossed:
                self.cross(k).wait_send()
            pl.when(k != self.at)(lambda k=k: self.line(k, sent and sent(k)).wait_send())


def back_kernel(
    outer, ns, pairs, group, c, scale,
    datt_hbm, q_ref, laug_ref, o_ref, k_ref, v_ref, raw_hbm, cos_hbm, sin_hbm, start_ref, live_ref, gain_ref, wq_ref,
    xh_hbm, gd_hbm, gg_hbm, gu_hbm, att_hbm, dmid_hbm, lo_hbm,
    dn_out, lo_out, sd_out, sg_out, fin_u, so_out, fin_q, go_hbm, lo_g3, dn_g3, og1, zr_d, zr_g, zr_u, dgain_ref,
    do_v, qa, qb, qaug, doa, dob, doaug, kaug0, kaug1, vaug0, vaug1, dqacc, dq_v, dk_acc, dv_acc,
    dqkv, dnv, raw_t, cos_t, sin_t, xh_t, gq_send, xz_g, xz_u, xz_o, xz_q, zr_o, zr_q,
    fin_d, fin_g, fin_o, tile_g, o_t, o_g, gsum, gslot, gline, ssem, tsem, lsem,
):
    f, s = lax.axis_index("fsdp"), lax.axis_index("sp")
    core = s % 2
    near, far = s + 1 - 2 * core, s + 2 - 4 * (s // 2)
    diag = far + 1 - 2 * core
    at, inner = f // 2, f % 2
    cross_f = f + 1 - 2 * inner
    T = q_ref.shape[0]
    blk = T // ns
    q_cols = pairs * 128

    barrier = pltpu.get_barrier_semaphore()

    def greet(ff, ss):
        pl.semaphore_signal(barrier, inc=1, device_id=(ff, ss), device_id_type=pl.DeviceIdType.MESH)

    greet(f, near)
    greet(f, far)
    greet(f, diag)
    greet(cross_f, s)
    for m in range(1, outer):
        greet(2 * ((at + m) % outer) + inner, s)
    pl.semaphore_wait(barrier, 3 + outer)

    def send(src, dst, n, to, ff=None):
        return pltpu.make_async_remote_copy(
            src, dst, tsem.at[0, n], tsem.at[1, n], device_id=(f if ff is None else ff, to),
            device_id_type=pl.DeviceIdType.MESH,
        )

    def keep(src, dst, n):
        return pltpu.make_async_copy(src, dst, lsem.at[n])

    def fetch(src, dst, n=0):
        a = keep(src, dst, n)
        a.start()
        a.wait()
        return dst

    turn = [n // 2 if n % 2 else outer - 1 - n // 2 for n in range(outer)]
    per = 2 * outer + 3

    def local(n):
        return lambda src, dst: keep(src, dst, n)

    part = lambda ref: lambda k: ref.at[2 * k + 1 - inner]
    sd = Scatter(ssem, 0, outer, ns, f, s, None, None, None, zr_d, fin_d, sd_out, local(1))
    sg = Scatter(ssem, per, outer, ns, f, s, xz_g, lambda k: fetch(gg_hbm.at[2 * k + inner], tile_g)[...], part(gg_hbm),
                 zr_g, fin_g, sg_out, local(2))
    su = Scatter(ssem, 2 * per, outer, ns, f, s, xz_u, lambda k: fetch(gu_hbm.at[2 * k + inner], tile_g)[...], part(gu_hbm),
                 zr_u, fin_u, None, None)
    so = Scatter(ssem, 3 * per, outer, ns, f, s, xz_o, lambda k: o_t[2 * k + inner], part(o_t), zr_o, fin_o, so_out, local(4))
    sq = Scatter(ssem, 4 * per, outer, ns, f, s, xz_q, None, lambda k: gq_send.at[k], zr_q, fin_q, None, None)

    def do_part(r, to):
        return send(datt_hbm.at[:, pl.ds(r * q_cols, q_cols)], do_v.at[pl.ds(r * blk, blk)], r, to)

    datt_t = [do_part(2, far), do_part(3, diag), do_part(1, near)]
    for a in datt_t:
        a.start()
    own_do = keep(datt_hbm.at[:, pl.ds(0, q_cols)], do_v.at[pl.ds(0, blk)], 6)
    own_do.start()
    sent_d = lambda k: gd_hbm.at[k]
    for k in turn:
        pl.when(k != at)(lambda k=k: sd.line(k, sent_d(k)).start())
        sg.cross(k).start()
    for k in turn:
        su.cross(k).start()
    o1 = send(go_hbm.at[:, near], og1, 4, near)
    o3 = send(go_hbm.at[:, diag], o_g.at[0], 5, near)
    of = send(o_g.at[0], o_g.at[1], 6, far)
    lo1 = send(lo_hbm.at[1], lo_out.at[0], 7, near)
    lo3 = send(lo_hbm.at[3], lo_g3, 8, near)
    lof = send(dnv.at[2], lo_out.at[1], 9, far)
    lo3.start()
    lo1.start()
    load_d = keep(dmid_hbm, dnv.at[1], 0)
    load_d.start()
    load_a = [keep(att_hbm.at[:, pl.ds(r * q_cols, q_cols)], dq_v.at[pl.ds(r * blk, blk)], 1 + r) for r in range(ns)]
    for a in load_a:
        a.start()
    for a in load_a + [load_d]:
        a.wait()
    shards, quarter = 2 * outer // ns, o_t.shape[1]
    half_w = 512
    for r in range(ns):
        for n in range(dnv.shape[2] // half_w):
            cols = slice(n * half_w, (n + 1) * half_w)
            grad = dg(dq_v[r * blk : (r + 1) * blk, :], dnv[1, :, cols], TN).astype(bf16)
            o_t[:, :, cols] = grad.reshape(shards * ns, quarter, half_w)
        outs = [
            keep(o_t.at[pl.ds(a * ns, ns)], go_hbm.at[xor_small(s, r) * shards + a], 1 + a) for a in range(shards)
        ]
        for a in outs:
            a.start()
        for a in outs:
            a.wait()
    o3.start()
    o1.start()
    o3.wait_recv()
    fetch(go_hbm.at[:, far], o_t)
    for n in range(o_t.shape[0]):
        o_g[0, n] = (o_g[0, n].astype(f32) + o_t[n].astype(f32)).astype(bf16)
    of.start()
    lo3.wait_recv()
    fetch(lo_g3, dnv.at[2])
    fetch(lo_hbm.at[2], dnv.at[0])
    chunk = 128

    @pl.loop(0, blk // chunk)
    def _(i):
        rows = pl.ds(pl.multiple_of(i * chunk, chunk), chunk)
        dnv[2, rows, :] = (dnv[2, rows, :].astype(f32) + dnv[0, rows, :].astype(f32)).astype(bf16)

    fetch(go_hbm.at[:, s], o_t)
    lof.start()
    own_do.wait()
    for a in datt_t:
        a.wait_recv()

    dk_acc[...] = jnp.zeros_like(dk_acc)
    dv_acc[...] = jnp.zeros_like(dv_acc)
    low = lane_iota(blk, 128) < 64
    lane = lane_iota(blk, 128)
    n_live = live_ref[0:1, 0:1]
    krow = lax.broadcasted_iota(jnp.int32, (blk, blk), 0)
    qcol = lane_iota(blk, blk)

    def pos(t):
        return pl.multiple_of(xor_small(t, s) * blk, blk)

    def is_first(p):
        return (pairs * 2 * s + 2 * p) // group - (pairs * 2 * s) // group == 0

    def prepare(p):
        first = is_first(p)
        lanes = slice(128 * p, 128 * (p + 1))
        ones_a = jnp.where(lane < 3, 1.0, 0.0).astype(bf16)
        ones_b = jnp.where((lane >= 64) & (lane < 67), 1.0, 0.0).astype(bf16)
        for r in range(ns):
            here = slice(r * blk, (r + 1) * blk)
            kk, vv = k_ref[here, :].astype(f32), v_ref[here, :].astype(f32)
            ksw, vsw = pltpu.roll(kk, 64, 1), pltpu.roll(vv, 64, 1)
            k_a = jnp.where(low, jnp.where(first, kk, ksw), 0.0).astype(bf16)
            k_b = jnp.where(low, 0.0, jnp.where(first, ksw, kk)).astype(bf16)
            kaug0[here, :128], kaug0[here, 128:] = k_a, ones_a
            kaug1[here, :128], kaug1[here, 128:] = k_b, ones_b
            vaug0[here, :128] = jnp.where(low, jnp.where(first, vv, vsw), 0.0).astype(bf16)
            vaug0[here, 128:] = ones_a
            vaug1[here, :128] = jnp.where(low, 0.0, jnp.where(first, vsw, vv)).astype(bf16)
            vaug1[here, 128:] = ones_b
            q = q_ref[here, lanes]
            qf = q.astype(f32)
            qaug[here, :128], qaug[here, 128:] = q, laug_ref[here, lanes]
            qa[here, :] = jnp.where(low, qf, 0.0).astype(bf16)
            qb[here, :] = jnp.where(low, 0.0, qf).astype(bf16)
            do = do_v[here, lanes]
            dof = do.astype(f32)
            doa[here, :] = jnp.where(low, dof, 0.0).astype(bf16)
            dob[here, :] = jnp.where(low, 0.0, dof).astype(bf16)
            doaug[here, :128] = do
            doaug[here, 128:] = aug_lanes(-head_sums(dof * o_ref[here, lanes].astype(f32)))
        dqacc[...] = jnp.zeros_like(dqacc)

    def step(j, here, qo, ok, dk, dv):
        there = pl.ds(qo, blk)
        qg, dg_ = qaug[there, :], doaug[there, :]
        e0 = jnp.where(ok, jnp.exp2(dg(kaug0[here, :], qg, NT) * c), 0.0)
        e1 = jnp.where(ok, jnp.exp2(dg(kaug1[here, :], qg, NT) * c), 0.0)
        ds0 = (e0 * dg(vaug0[here, :], dg_, NT)).astype(bf16)
        ds1 = (e1 * dg(vaug1[here, :], dg_, NT)).astype(bf16)
        dv = dv + dg(e0.astype(bf16), doa[there, :], NN) + dg(e1.astype(bf16), dob[there, :], NN)
        dk = dk + dg(ds0, qa[there, :], NN) + dg(ds1, qb[there, :], NN)
        dqacc[there, :] += dg(ds0, kaug0[here, :128], TN) + dg(ds1, kaug1[here, :128], TN)
        return dk, dv

    def key_block(p, j):
        here = pl.ds(pos(j), blk)
        st = start_ref[0:1, here] - j * blk
        ok = (krow >= st) & (krow <= qcol) & ((krow < n_live - j * blk) | (krow == qcol))
        z = jnp.zeros((blk, 128), f32)
        dk, dv = step(j, here, pos(j), ok, z, z)

        def query_block(i, carry):
            qo = pos(i)
            st = start_ref[0:1, pl.ds(qo, blk)] - j * blk
            ok = (krow >= st) & (krow < n_live - j * blk)
            return step(j, here, qo, ok, *carry)

        dk, dv = lax.fori_loop(j + 1, ns, query_block, (dk, dv))
        first = is_first(p)
        dk, dv = dk * scale + pltpu.roll(dk * scale, 64, 1), dv + pltpu.roll(dv, 64, 1)
        dk_acc[here, :] += jnp.where(first, jnp.where(low, dk, 0.0), jnp.where(low, 0.0, dk))
        dv_acc[here, :] += jnp.where(first, jnp.where(low, dv, 0.0), jnp.where(low, 0.0, dv))

    def own_o():
        of.wait()
        o1.wait_recv()
        fetch(og1, o_g.at[0])
        for n in range(o_t.shape[0]):
            o_t[n] = (o_t[n].astype(f32) + o_g[0, n].astype(f32) + o_g[1, n].astype(f32)).astype(bf16)
        for k in turn:
            so.cross(k).start()

    jobs = {
        (0, 0): lambda: sg.take(turn[0]),
        (0, 1): lambda: (sg.take(turn[1]), sg.take(turn[2])),
        (1, 0): lambda: (sg.take(turn[3]) if outer > 3 else None, own_o()),
        (1, 1): lambda: (sd.total(fetch(gd_hbm.at[at], fin_d)[...], lambda r: fetch(r, fin_d)[...]), su.take(turn[0])),
        (2, 0): lambda: su.take(turn[1]),
        (2, 1): lambda: (su.take(turn[2]), sd.forward()),
    }
    for p in range(pairs):
        prepare(p)
        key_block(p, 0)
        jobs.get((p, 0), lambda: None)()
        pl.loop(1, ns)(lambda j, p=p: key_block(p, j))
        dq_v[:, 128 * p : 128 * (p + 1)] = (dqacc[...] * scale).astype(bf16)
        jobs.get((p, 1), lambda: None)()

    tile = min(256, blk)
    gsum[...] = jnp.zeros_like(gsum)

    def turn_block(r):
        @pl.loop(0, blk // tile)
        def _(i):
            rows = pl.ds(pl.multiple_of(r * blk + i * tile, tile), tile)
            part_rows = pl.ds(pl.multiple_of(i * tile, tile), tile)
            loads = [
                keep(raw_hbm.at[rows], raw_t, 0), keep(cos_hbm.at[r, part_rows], cos_t, 7), keep(sin_hbm.at[r, part_rows], sin_t, 8),
            ]
            for a in loads:
                a.start()
            for a in loads:
                a.wait()
            cosine, sine = cos_t[...], sin_t[...]
            for p in range(pairs + 1):
                which = 0 if p < pairs else 1
                lanes = slice(128 * p, 128 * (p + 1))
                grad = dq_v[rows, lanes].astype(f32) if p < pairs else dk_acc[rows, :].astype(bf16).astype(f32)
                raw = raw_t[:, lanes]
                inv = lax.rsqrt(head_sums(raw * raw) * (1.0 / 64) + epsilon)
                normal = raw * inv
                grad = grad * cosine - half_swap(grad) * sine
                gsum[which] += jnp.sum((grad * normal).reshape(tile // 8, 8, 128), axis=0)
                grad = grad * gain_ref[which : which + 1, :]
                mean = head_sums(grad * normal) * (1.0 / 64)
                dqkv[rows, lanes] = (inv * (grad - normal * mean)).astype(bf16)
            dqkv[rows, 128 * (pairs + 1) :] = dv_acc[rows, :].astype(bf16)
            dnv[{3: 0, 2: 1, 1: 2, 0: 0}[r], part_rows, :] = dg(dqkv[rows, :], wq_ref[...], NT).astype(bf16)

    dn1 = send(dnv.at[2], dn_out.at[1], 10, near)
    dn3 = send(dnv.at[0], dn_g3, 11, near)
    dnf = send(dnv.at[1], dn_out.at[2], 12, far)
    turn_block(3)
    dn3.start()
    turn_block(2)
    dn3.wait()
    fetch(dn_g3, dnv.at[0])

    @pl.loop(0, blk // chunk)
    def _(i):
        rows = pl.ds(pl.multiple_of(i * chunk, chunk), chunk)
        dnv[1, rows, :] = (dnv[1, rows, :].astype(f32) + dnv[0, rows, :].astype(f32)).astype(bf16)

    dnf.start()
    lof.wait_send()
    turn_block(1)
    dn1.start()
    su.take(turn[3]) if outer > 3 else None
    turn_block(0)
    own_dn = keep(dnv.at[0], dn_out.at[0], 9)
    own_dn.start()
    for k in turn[4:]:
        sg.take(k)
        su.take(k)

    drows, span = gq_send.shape[1], xh_t.shape[1]

    def grad_block(b):
        first = (b * drows) // span
        fetch(xh_hbm.at[:, pl.ds(pl.multiple_of(first * span, span), span)], xh_t)
        grad = dg(xh_t[...], dqkv[...], TN)
        if span > drows:
            grad = jnp.where(b % 2 == 0, grad[:drows], grad[drows:])
        return grad.astype(bf16)

    for k in turn:
        gq_send[k] = grad_block(2 * k + 1 - inner)
        if k != turn[0]:
            sq.cross(turn[turn.index(k) - 1]).start()
    so.take(turn[0])
    sq.cross(turn[-1]).start()
    for k in turn[1:]:
        so.take(k)
    sq.own = lambda k: grad_block(2 * k + inner)

    gslot[0] = jnp.concatenate(
        [jnp.sum(gsum[0], axis=0, keepdims=True), jnp.sum(gsum[1], axis=0, keepdims=True), jnp.zeros((6, 128), f32)]
    )
    hops = [
        send(gslot.at[0], gslot.at[3], 13, near), send(gslot.at[1], gslot.at[4], 14, far),
        send(gslot.at[2], gslot.at[5], 15, s, cross_f),
    ]
    hops[0].start()
    sg.total(None, lambda r: fetch(r, fin_g)[...])
    hops[0].wait_recv()
    gslot[1] = gslot[0] + gslot[3]
    hops[1].start()
    for k in turn:
        sq.take(k)
    hops[1].wait_recv()
    gslot[2] = gslot[1] + gslot[4]
    hops[2].start()
    so.total()
    hops[2].wait_recv()
    gline[at] = gslot[2] + gslot[5]
    lines = [
        send(gline.at[at], gline.at[at], 16 + m, s, 2 * ((at + m) % outer) + inner) for m in range(1, outer)
    ]
    for a in lines:
        a.start()
    su.total(None, lambda r: fetch(r, fin_u)[...])
    sg.forward()
    so.forward()
    for m in range(1, outer):
        k = (at + outer - m) % outer
        send(gline.at[k], gline.at[k], 16 + m, s, 2 * k + inner).wait_recv()
    total = gline[0]
    for k in range(1, outer):
        total = total + gline[k]
    dgain_ref[...] = total + pltpu.roll(total, 64, 1)
    sq.total()

    sd.finish(sent_d, False)
    for a in (sg, su, so, sq):
        a.finish()
    for a in lines + hops + datt_t + [o1, o3, lo1, lo3, dn1, dnf]:
        a.wait_send()
    for a in (lo1, lof, dn1, dnf):
        a.wait_recv()
    own_dn.wait()


def back_call(datt, q, laug, o, k, v, raw, cosine, sine, start_row, n_live, gains, w_qkv, xh, gd, gg, gu, att, dmid, lo, nf, ns, quarter, group, head):
    outer = gd.shape[0]
    T = q.shape[0]
    blk = T // ns
    width, cols = w_qkv.shape
    pairs = cols // 128 - 2
    q_cols = pairs * 128
    scale = head**-0.5
    c = math.log2(math.e) * scale
    hbm, vmem = pl.BlockSpec(memory_space=pl.ANY), pl.BlockSpec(memory_space=pltpu.VMEM)
    S, V = jax.ShapeDtypeStruct, pltpu.VMEM
    dblk, gblk, oblk = gd.shape[1:], gg.shape[1:], (quarter, width)
    drows = gblk[0]
    qblk = (drows, cols)
    half = (T, 128)
    wide = (T, 256)
    per = 2 * outer + 3
    return pl.pallas_call(
        functools.partial(back_kernel, outer, ns, pairs, group, c, scale),
        in_specs=[hbm] + [vmem] * 5 + [hbm] * 3 + [vmem] * 4 + [hbm] * 7,
        out_specs=[hbm] * 4 + [vmem, hbm, vmem] + [hbm] * 7 + [vmem],
        out_shape=[
            S((3, blk, width), bf16), S((2, blk, width), bf16),
            S((ns,) + dblk, bf16), S((ns,) + gblk, bf16), S(gblk, bf16), S((ns,) + oblk, bf16), S(qblk, bf16),
            S((2 * outer, ns) + oblk, bf16),
            S((blk, width), bf16), S((blk, width), bf16), S((2 * outer,) + oblk, bf16), S((outer,) + dblk, bf16), S((outer,) + gblk, bf16), S((outer,) + gblk, bf16),
            S((8, 128), f32),
        ],
        scratch_shapes=[
            V((T, q_cols), bf16), V(half, bf16), V(half, bf16), V(wide, bf16), V(half, bf16), V(half, bf16), V(wide, bf16),
            V(wide, bf16), V(wide, bf16), V(wide, bf16), V(wide, bf16),
            V(half, f32), V((T, q_cols), bf16), V(half, f32), V(half, f32),
            V((T, cols), bf16), V((3, blk, width), bf16),
            V((min(256, blk), q_cols + 128), f32), V((min(256, blk), 128), f32), V((min(256, blk), 128), f32),
            V((T, drows if drows % 128 == 0 else 2 * drows), bf16), V((outer,) + qblk, bf16),
            V((outer,) + gblk, bf16), V((outer,) + gblk, bf16), V((outer,) + oblk, bf16), V((outer,) + qblk, bf16),
            V((outer,) + oblk, bf16), V((outer,) + qblk, bf16),
            V(dblk, bf16), V(gblk, bf16), V(oblk, bf16),
            V(gblk, bf16), V((2 * outer,) + oblk, bf16), V((2, 2 * outer) + oblk, bf16),
            V((2, 8, 128), f32), V((6, 8, 128), f32), V((outer, 8, 128), f32),
            pltpu.SemaphoreType.DMA((2, 5 * per)), pltpu.SemaphoreType.DMA((2, 16 + outer)), pltpu.SemaphoreType.DMA((10 + outer,)),
        ],
        compiler_params=pltpu.CompilerParams(
            collective_id=1, has_side_effects=True, vmem_limit_bytes=63 * 2**20
        ),
        cost_estimate=tiny,
        name="back",
    )(datt, q, laug, o, k, v, raw, cosine, sine, start_row, n_live, gains, w_qkv, xh, gd, gg, gu, att, dmid, lo)


def ffn_kernel(tile, n2_ref, dy_ref, wg_ref, wu_ref, wd_ref, hid_ref, dg_ref, du_ref, dn_ref):
    n2, dy = n2_ref[...], dy_ref[...]
    units, width = wd_ref.shape
    for j in range(units // tile):
        cols = slice(j * tile, (j + 1) * tile)
        gate = dg(n2, wg_ref[0, :, cols], NN)
        up = dg(n2, wu_ref[0, :, cols], NN)
        dhid = dg(dy, wd_ref[cols, :], NT)
        sig = jax.nn.sigmoid(gate)
        act = gate * sig
        hid_ref[:, cols] = (act * up).astype(bf16)
        du_ref[:, cols] = (dhid * act).astype(bf16)
        dg_ref[:, cols] = (dhid * up * (sig * (1.0 + gate * (1.0 - sig)))).astype(bf16)
    for j in range(width // 512):
        rows = slice(j * 512, (j + 1) * 512)
        grad = dg(dg_ref[...], wg_ref[0, rows, :], NT) + dg(du_ref[...], wu_ref[0, rows, :], NT)
        dn_ref[:, rows] = grad.astype(bf16)


def ffn_call(n2_all, dy_all, w_gu, w_d, rows=256, tile=256):
    length, width = n2_all.shape
    units = w_d.shape[0]
    once = pl.Buffered(1)
    big = jax.ShapeDtypeStruct((length, units), bf16)
    return pl.pallas_call(
        functools.partial(ffn_kernel, tile),
        grid=(length // rows,),
        in_specs=[pl.BlockSpec((rows, width), lambda i: (i, 0))] * 2
        + [
            pl.BlockSpec((1, width, units), lambda i: (0, 0, 0), pipeline_mode=once),
            pl.BlockSpec((1, width, units), lambda i: (1, 0, 0), pipeline_mode=once),
            pl.BlockSpec((units, width), lambda i: (0, 0), pipeline_mode=once),
        ],
        out_specs=[pl.BlockSpec((rows, units), lambda i: (i, 0))] * 3 + [pl.BlockSpec((rows, width), lambda i: (i, 0))],
        out_shape=[big, big, big, jax.ShapeDtypeStruct((length, width), bf16)],
        compiler_params=pltpu.CompilerParams(vmem_limit_bytes=62 * 2**20),
        cost_estimate=tiny,
        name="ffn",
    )(n2_all, dy_all, w_gu, w_gu, w_d)


def join_kernel(members, shards, shard, unit, gain_ref, m_ref, w_ref, out_ref, sum_ref):
    for k in range(members):
        width = min(unit, shard - k * unit)
        for j in range(shards):
            part = m_ref[k, :, j * unit : j * unit + width].astype(f32)
            out_ref[:, j * shard + k * unit : j * shard + k * unit + width] = part
    full = out_ref[...]
    sum_ref[...] = jnp.broadcast_to(
        jnp.sum(full * w_ref[...].astype(f32), axis=-1, keepdims=True), sum_ref.shape
    )
    out_ref[...] = full * gain_ref[...]


def join_call(gain, stacked, weight, members, shards, shard, unit):
    rows, cols = weight.shape
    tile = min(64, rows)
    return pl.pallas_call(
        functools.partial(join_kernel, members, shards, shard, unit),
        grid=(rows // tile,),
        in_specs=[
            pl.BlockSpec((tile, 1), lambda i: (i, 0)),
            pl.BlockSpec((members, tile, shards * unit), lambda i: (0, i, 0)),
            pl.BlockSpec((tile, cols), lambda i: (i, 0)),
        ],
        out_specs=[
            pl.BlockSpec((tile, cols), lambda i: (i, 0)),
            pl.BlockSpec((tile, 128), lambda i: (i, 0)),
        ],
        out_shape=[
            jax.ShapeDtypeStruct((rows, cols), f32),
            jax.ShapeDtypeStruct((rows, 128), f32),
        ],
        compiler_params=pltpu.CompilerParams(vmem_limit_bytes=60 * 2**20),
        name="join_units",
    )(gain, stacked, weight)


def heads_kernel(members, q_cols, kv_base, gain_ref, m_ref, wq_ref, wk_ref, wv_ref, q_ref, k_ref, v_ref, sum_ref):
    for k in range(members):
        q_ref[:, k * q_cols : (k + 1) * q_cols] = m_ref[k, :, :q_cols].astype(f32)
    for n, ref in enumerate((k_ref, v_ref)):
        at = q_cols + 128 * n
        ref[...] = jnp.zeros_like(ref)
        for k in range(members):
            ref[:, kv_base[k] : kv_base[k] + 128] += m_ref[k, :, at : at + 128].astype(f32)
    total = 0.0
    for ref, w in ((q_ref, wq_ref), (k_ref, wk_ref), (v_ref, wv_ref)):
        full = ref[...]
        total = total + jnp.sum(full * w[...].astype(f32), axis=-1, keepdims=True)
        ref[...] = full * gain_ref[...]
    sum_ref[...] = jnp.broadcast_to(total, sum_ref.shape)


def heads_call(gain, stacked, w_query, w_key, w_value, kv_base, q_cols):
    members, rows, cols = stacked.shape
    tile = min(64, rows)
    outs = [w_query.shape[1], w_key.shape[1], w_value.shape[1], 128]
    return pl.pallas_call(
        functools.partial(heads_kernel, members, q_cols, kv_base),
        grid=(rows // tile,),
        in_specs=[pl.BlockSpec((tile, 1), lambda i: (i, 0)), pl.BlockSpec((members, tile, cols), lambda i: (0, i, 0))]
        + [pl.BlockSpec((tile, n), lambda i: (i, 0)) for n in outs[:3]],
        out_specs=[pl.BlockSpec((tile, n), lambda i: (i, 0)) for n in outs],
        out_shape=[jax.ShapeDtypeStruct((rows, n), f32) for n in outs],
        compiler_params=pltpu.CompilerParams(vmem_limit_bytes=60 * 2**20),
        name="join_heads",
    )(gain, stacked, w_query, w_key, w_value)


def dot_bf(a, b, dims):
    return dg(a, b, dims).astype(bf16)


def local(
    tokens, seg_ids, pad_mask, positions, attn_gain, w_query, w_key, w_value, query_gain,
    key_gain, w_out, ffn_gain, w_gate, w_up, w_down, cotangent,
):
    nf, ns = lax.axis_size("fsdp"), lax.axis_size("sp")
    f, s = lax.axis_index("fsdp"), lax.axis_index("sp")
    seq_count, blk, width = tokens.shape
    assert seq_count == 1 and ns == 4
    length = blk * ns
    head = query_gain.shape[0]
    q_heads, kv_heads = w_query.shape[1] // head, w_key.shape[1] // head
    group = q_heads // kv_heads
    q_local = q_heads // ns
    kv_base = [(q_local * k) // group for k in range(ns)]
    pairs = q_local // 2
    q_cols = q_local * head
    kv_map = jnp.array(
        [[(q_local * k + 2 * p) // group - kv_base[k] for p in range(pairs)] for k in range(ns)],
        jnp.int32,
    )[s]
    base = jnp.array(kv_base, jnp.int32)[s] * head
    shard = w_down.shape[0]
    unit = -(-(-(-shard // ns)) // 16) * 16
    units = unit * nf
    out_rows = w_out.shape[0]
    quarter = out_rows // ns
    sub = 512

    x = tokens[0]
    dy = cotangent[0]
    gain_one = attn_gain.astype(f32)[:, None]
    gain_two = ffn_gain.astype(f32)[:, None]

    kv_cols = 2 * head
    out_mine = lax.dynamic_slice_in_dim(w_out, s * quarter, quarter, 0)
    small = jnp.concatenate(
        [positions.astype(f32), pad_mask.astype(f32), jnp.zeros((6, blk), f32)]
    )
    gains = jnp.concatenate(
        [
            jnp.tile(query_gain.astype(f32), 2)[None],
            jnp.tile(key_gain.astype(f32), 2)[None],
            jnp.zeros((6, 2 * head), f32),
        ]
    )
    (
        xh, dy_all, n2_all, w_d, w_gu, w_qkv, w_out_rel, att, q, k, v, raw, cosine, sine,
        attended, laug, middle, inv_two, small_all,
    ) = front_call(
        x, dy, small, w_query, w_key, w_value, out_mine, w_down, w_gate, w_up,
        jnp.broadcast_to(gain_one, (width // nf, 128)), jnp.broadcast_to(gain_two, (width // nf, 128)), gains,
        nf, ns, group, head, unit, kv_base, q_cols,
    )
    xh = xh.reshape(length, width)
    w_d, w_gu = w_d.reshape(units, width), w_gu.reshape(2, width, units)
    w_out_rel = w_out_rel.reshape(ns * q_cols, width)
    pos_rel = small_all[:, 0].astype(jnp.int32)
    n_live = jnp.sum(small_all[:, 1]).astype(jnp.int32)
    true_block = s ^ jnp.arange(ns)
    start_rel = (true_block[:, None] * blk + jnp.arange(blk)[None] - pos_rel).reshape(length)
    xf = x.astype(f32)
    inv_two = inv_two[:, :1]

    n2_all, dy_all = n2_all.reshape(length, width), dy_all.reshape(length, width)
    hidden, dgate, dup, dn2 = ffn_call(n2_all, dy_all, w_gu, w_d)
    dn2 = [dn2[r * blk : (r + 1) * blk] for r in range(ns)]
    got3 = perm_s(dn2[3], 1)
    got1 = perm_s(dn2[1], 1)
    pair = (dn2[2].astype(f32) + got3.astype(f32)).astype(bf16)
    dn2_far = perm_s(pair, 2)

    hidden_a = after(hidden, pair, got1)
    grad_d = dot_bf(hidden_a, dy_all, TN).reshape(nf // 2, 2, unit, width)
    d_own = lax.dynamic_index_in_dim(grad_d, f % 2, 1, keepdims=False)
    d_other = lax.dynamic_index_in_dim(grad_d, 1 - f % 2, 1, keepdims=False)
    d_got = perm_f(d_other, 1)
    dgate_a, dup_a = after(dgate, d_other), after(dup, d_other)
    grad_g = dot_bf(n2_all, dgate_a, TN).reshape(nf, width // nf, units)
    grad_u = dot_bf(n2_all, dup_a, TN).reshape(nf, width // nf, units)
    lo = dot_bf(hidden_a, w_d, NN).reshape(ns, blk, width)

    dn2_own = dn2[0].astype(f32) + got1.astype(f32) + dn2_far.astype(f32)
    hat_two = middle * inv_two
    dmiddle = dy.astype(f32) + inv_two * (
        dn2_own - hat_two * jnp.mean(dn2_own * hat_two, axis=-1, keepdims=True)
    )
    dmid = dmiddle.astype(bf16)
    datt = dot_bf(dmid, w_out_rel, NT)
    gd = (d_own.astype(f32) + after(d_got, dmid).astype(f32)).astype(bf16)

    live_row = jnp.full((8, 128), n_live, jnp.int32)
    dn, lo_got, sum_d, sum_g, fin_u, sum_o, fin_q, _, _, _, _, _, _, _, dgain = back_call(
        datt, q, laug, attended, k, v, raw, cosine, sine, jnp.broadcast_to(start_rel[None], (8, length)),
        live_row, gains, w_qkv, xh, gd, grad_g, grad_u, att, dmid, lo, nf, ns, quarter, group, head,
    )
    u_pieces, q_pieces = gather_s(fin_u), gather_s(fin_q)
    layer_out = (
        middle + lo[0].astype(f32) + lo_got[0].astype(f32) + lo_got[1].astype(f32)
    ).astype(bf16)
    w_down_grad = sum_d.reshape(ns * unit, width)[:shard].astype(f32)
    w_gate_grad, gate_sum = join_call(gain_two, sum_g, w_gate, ns, nf, shard, unit)
    w_up_grad, up_sum = join_call(gain_two, place(u_pieces, s), w_up, ns, nf, shard, unit)
    ffn_gain_grad = (gate_sum + up_sum)[:, 0]
    w_out_grad = sum_o.reshape(out_rows, width).astype(f32)

    dn_own = dn[0].astype(f32) + dn[1].astype(f32) + dn[2].astype(f32)
    inv_one = lax.rsqrt(jnp.mean(xf * xf, axis=-1, keepdims=True) + epsilon)
    hat_one = xf * inv_one
    tokens_grad = (
        dmiddle + inv_one * (dn_own - hat_one * jnp.mean(dn_own * hat_one, axis=-1, keepdims=True))
    ).astype(bf16)
    query_gain_grad, key_gain_grad = dgain[0, :head], dgain[1, :head]

    w_query_grad, w_key_grad, w_value_grad, one_sum = heads_call(
        gain_one, place(q_pieces, s), w_query, w_key, w_value, [k * head for k in kv_base], q_cols
    )
    attn_gain_grad = one_sum[:, 0]
    return (
        layer_out[None], tokens_grad[None], attn_gain_grad, w_query_grad, w_key_grad,
        w_value_grad, query_gain_grad, key_gain_grad, w_out_grad, ffn_gain_grad,
        w_gate_grad, w_up_grad, w_down_grad,
    )


def solution(mesh):
    row, vec = P("fsdp", None), P("fsdp")
    tok, ids = P("fsdp", "sp", None), P("fsdp", "sp")
    in_specs = (tok, ids, ids, ids, vec, row, row, row, P(), P(), row, vec, row, row, row, tok)
    out_specs = (tok, tok, vec, row, row, row, P(), P(), row, vec, row, row, row)
    return jax.shard_map(local, mesh=mesh, in_specs=in_specs, out_specs=out_specs, check_vma=False)
```

```python
import functools, math
import jax, jax.numpy as jnp
from jax import lax
from jax.experimental import pallas as pl
from jax.experimental.pallas import tpu as pltpu
bf16=jnp.bfloat16; f32=jnp.float32
tiny=pl.CostEstimate(flops=1000000,bytes_accessed=1000000,transcendentals=0)
NT=(((1,),(1,)),((),()))
NN=(((1,),(0,)),((),()))
TN=(((0,),(0,)),((),()))

def dg(a,b,dims):
    return lax.dot_general(a,b,dims,preferred_element_type=f32)

def lane_iota(rows, cols):
    return lax.broadcasted_iota(jnp.int32,(rows,cols),1)

def split3(v):
    hi=v.astype(bf16); r=v-hi.astype(f32)
    mid=r.astype(bf16); lo=(r-mid.astype(f32)).astype(bf16)
    return hi,mid,lo

def aug_lanes(v):
    hi,mid,lo=split3(v)
    lane=lane_iota(*v.shape)%64
    z=jnp.zeros_like(v)
    return jnp.where(lane==0,hi.astype(f32),jnp.where(lane==1,mid.astype(f32),jnp.where(lane==2,lo.astype(f32),z))).astype(bf16)


from jax.sharding import PartitionSpec as P

epsilon = 1e-06
rope_base = 10000.0


def perm_f(x, m):
    n = lax.axis_size("fsdp")
    return lax.ppermute(x, "fsdp", [(i, i ^ m) for i in range(n)])


def perm_s(x, m):
    n = lax.axis_size("sp")
    return lax.ppermute(x, "sp", [(i, i ^ m) for i in range(n)])


def after(x, *deps):
    return lax.optimization_barrier((x,) + deps)[0]


def gather_f(x, *deps):
    outer = lax.axis_size("fsdp") // 2
    x_z = after(x, *deps) if deps else x
    firsts = [x] + [perm_f(x_z, 2 * m) for m in range(1, outer)]
    pieces = []
    for first in firsts:
        pieces += [first, perm_f(first, 1)]
    return pieces


def gather_s(x):
    far = perm_s(x, 2)
    near = perm_s(x, 1)
    return [x, near, far, perm_s(far, 1)]


def place(pieces, me):
    out = jnp.zeros((len(pieces),) + pieces[0].shape, pieces[0].dtype)
    for r, piece in enumerate(pieces):
        out = lax.dynamic_update_index_in_dim(out, piece, me ^ r, 0)
    return out


def scatter_f(blocks, *deps):
    outer = blocks.shape[0] // 2
    me = lax.axis_index("fsdp")
    pairs = blocks.reshape((outer, 2) + blocks.shape[1:])
    mine = lax.dynamic_index_in_dim(pairs, me % 2, 1, keepdims=False)
    other = lax.dynamic_index_in_dim(pairs, 1 - me % 2, 1, keepdims=False)
    got = perm_f(other, 1)
    if deps:
        got = after(got, *deps)
    both = (mine.astype(f32) + got.astype(f32)).astype(bf16)
    at = me // 2
    total = lax.dynamic_index_in_dim(both, at, 0, keepdims=False).astype(f32)
    for m in range(1, outer):
        part = perm_f(lax.dynamic_index_in_dim(both, at ^ m, 0, keepdims=False), 2 * m)
        total = total + part.astype(f32)
    return total.astype(bf16)


def scatter_s(parts):
    got3 = perm_s(parts[3], 1)
    got1 = perm_s(parts[1], 1)
    far = perm_s((parts[2].astype(f32) + got3.astype(f32)).astype(bf16), 2)
    return parts[0].astype(f32) + got1.astype(f32) + far.astype(f32)


def half_swap(v):
    lane = lane_iota(*v.shape) % 64
    return jnp.where(lane < 32, pltpu.roll(v, 96, 1), pltpu.roll(v, 32, 1))


def head_sums(v):
    row = lax.broadcasted_iota(jnp.int32, (128, 128), 0) // 64
    col = lane_iota(128, 128) // 64
    same = jnp.where(row == col, 1.0, 0.0).astype(bf16)
    hi, mid, lo = split3(v)
    return dg(hi, same, NN) + dg(mid, same, NN) + dg(lo, same, NN)


def xor_small(a, b, bits=2):
    out = 0
    for i in range(bits):
        p = (a // (1 << i)) % 2
        q = (b // (1 << i)) % 2
        out = out + (p + q - 2 * p * q) * (1 << i)
    return out


class Ring:
    def __init__(self, own, slot, sems, base, outer, f, s):
        self.own, self.slot, self.sems, self.base = own, slot, sems, base
        self.outer, self.f, self.s = outer, f, s
        self.at, self.inner = f // 2, f % 2

    def copy(self, src, dst, send, recv, to):
        return pltpu.make_async_remote_copy(
            src, dst, self.sems.at[0, self.base + send], self.sems.at[1, self.base + recv],
            device_id=(to, self.s), device_id_type=pl.DeviceIdType.MESH,
        )

    def line(self, k, sign):
        n = self.outer
        lane = 0 if sign > 0 else n
        b = self.f - 2 * k * sign
        src = self.own if k == 0 else self.slot(b)
        return self.copy(src, self.slot(b), lane + k, lane + k + 1, self.f + 2 * sign)

    def line_wait(self, k, sign):
        n = self.outer
        lane = 0 if sign > 0 else n
        b = self.f - 2 * k * sign
        return self.copy(self.slot(b), self.slot(b), lane + k, lane + k, self.f + 2 * sign)

    def cross(self, k, sign):
        n = self.outer
        lane = 2 * n if sign > 0 else 3 * n
        b = self.f - 2 * k * sign
        src = self.own if k == 0 else self.slot(b)
        return self.copy(src, self.slot(b), lane + k, lane + k, self.f + 1 - 2 * self.inner)

    def cross_wait(self, k, sign):
        n = self.outer
        lane = 2 * n if sign > 0 else 3 * n
        b = self.f + 1 - 2 * self.inner - 2 * k * sign
        return self.copy(self.slot(b), self.slot(b), lane + k, lane + k, self.f + 1 - 2 * self.inner)

    def has(self, k, sign):
        return self.at >= k if sign > 0 else self.at + k <= self.outer - 1

    def onward(self, k, sign):
        more = self.at < self.outer - 1 if sign > 0 else self.at > 0
        return more if k == 0 else jnp.logical_and(more, self.has(k, sign))

    def start(self):
        for sign in (1, -1):
            pl.when(self.onward(0, sign))(lambda sign=sign: self.line(0, sign).start())

    def start_cross(self):
        self.cross(0, 1).start()

    def step(self, k):
        for sign in (1, -1):
            @pl.when(self.has(k, sign))
            def _(sign=sign):
                self.line_wait(k, sign).wait_recv()

                @pl.when(self.onward(0, sign))
                def _():
                    self.line(k, sign).start()

                self.cross(k, sign).start()

    def finish(self):
        for k in range(self.outer):
            for sign in (1, -1) if k else (1,):
                if k:
                    @pl.when(self.has(k, sign))
                    def _(k=k, sign=sign):
                        self.cross_wait(k, sign).wait_recv()
                        self.cross(k, sign).wait_send()
                else:
                    self.cross_wait(0, 1).wait_recv()
                    self.cross(0, 1).wait_send()
        for k in range(self.outer - 1):
            for sign in (1, -1):
                @pl.when(self.onward(k, sign))
                def _(k=k, sign=sign):
                    self.line(k, sign).wait_send()


def ring_sems(outer):
    return 4 * outer


def front_kernel(outer, ns, pairs, group, c, inv_log, unit, kv_base,
                 x_hbm, dy_hbm, small_ref, wq_ref, wk_ref, wv_ref, out_hbm, down_w, gate_w, up_w, one_ref, two_ref, gain_ref,
                 xh_hbm, dy_all, n2_all, w_d, w_gu, w_qkv_out, w_out_out, att_tok_out,
                 q_ref, k_ref, v_ref, raw_ref, cos_ref, sin_ref, o_ref, laug_ref, mid_ref, inv_ref, small_out,
                 qkv_hbm, down_hbm, gu_hbm, gate_v, up_v, xv, wq, ow, smalls, start_col, att_in, nv, ka, kb, ra, rb, ral, rbl,
                 rsem, tsem, lsem):
    f, s = lax.axis_index("fsdp"), lax.axis_index("sp")
    nf = 2 * outer
    core = s % 2
    near, far = s + 1 - 2 * core, s + 2 - 4 * (s // 2)
    diag = far + 1 - 2 * core
    at, inner = f // 2, f % 2
    blk, width = x_hbm.shape
    T = ns * blk
    q_cols = pairs * 128
    drows = qkv_hbm.shape[0]
    quarter = out_hbm.shape[0]

    shard, units = down_w.shape[0], gu_hbm.shape[2]

    one = one_ref[:, 0:1]
    qkv_hbm[:, :q_cols] = (wq_ref[:, pl.ds(pl.multiple_of(s * q_cols, 128), q_cols)].astype(f32) * one).astype(bf16)
    for n in range(ns):

        @pl.when(s == n)
        def _(n=n):
            for m, ref in enumerate((wk_ref, wv_ref)):
                part = ref[:, kv_base[n] : kv_base[n] + 128].astype(f32)
                qkv_hbm[:, q_cols + 128 * m : q_cols + 128 * (m + 1)] = (part * one).astype(bf16)

    barrier = pltpu.get_barrier_semaphore()

    def greet(ff, ss):
        pl.semaphore_signal(barrier, inc=1, device_id=(ff, ss), device_id_type=pl.DeviceIdType.MESH)

    greet(f, near)
    greet(f, far)
    greet(f, diag)
    greet(f + 1 - 2 * inner, s)
    pl.when(at < outer - 1)(lambda: greet(f + 2, s))
    pl.when(at > 0)(lambda: greet(f - 2, s))
    middle_of_line = jnp.logical_and(at > 0, at < outer - 1)
    pl.when(middle_of_line)(lambda: pl.semaphore_wait(barrier, 6))
    pl.when(jnp.logical_not(middle_of_line))(lambda: pl.semaphore_wait(barrier, 5))

    def send(src, dst, n, to):
        return pltpu.make_async_remote_copy(
            src, dst, tsem.at[0, n], tsem.at[1, n], device_id=(f, to), device_id_type=pl.DeviceIdType.MESH
        )

    def keep(src, dst, n):
        return pltpu.make_async_copy(src, dst, lsem.at[n])

    per = ring_sems(outer)
    qkv = Ring(qkv_hbm, lambda b: wq.at[pl.ds(pl.multiple_of(b * drows, drows), drows)], rsem, 0, outer, f, s)
    out = Ring(out_hbm, lambda b: ow.at[b, s], rsem, per, outer, f, s)
    down = Ring(down_hbm, lambda b: w_d.at[b], rsem, 2 * per, outer, f, s)
    gate = Ring(gu_hbm.at[0], lambda b: w_gu.at[0, b], rsem, 3 * per, outer, f, s)
    up = Ring(gu_hbm.at[1], lambda b: w_gu.at[1, b], rsem, 4 * per, outer, f, s)

    def triple(base, own, slot):
        return (
            send(own, slot(1), base, near), send(own, slot(2), base + 1, far), send(slot(2), slot(3), base + 2, near),
        )

    load_g = pltpu.make_async_copy(gate_w, gate_v, lsem.at[3])
    load_u = pltpu.make_async_copy(up_w, up_v, lsem.at[4])
    small_t = triple(0, small_ref, lambda r: smalls.at[r])
    tok_t = triple(3, x_hbm, lambda r: xv.at[r])
    most = blk * 3 // 4
    rows_a, rows_b = pl.ds(0, most), pl.ds(most, blk - most)
    dy_t = triple(9, dy_hbm.at[rows_a], lambda r: dy_all.at[r, rows_a])
    dy_u = triple(18, dy_hbm.at[rows_b], lambda r: dy_all.at[r, rows_b])
    small_t[0].start()
    small_t[1].start()
    tok_t[1].start()
    tok_t[0].start()
    load_x = keep(x_hbm, xv.at[0], 0)
    load_x.start()
    wq[pl.ds(pl.multiple_of(f * drows, drows), drows), :] = qkv_hbm[...]
    load_o = keep(out_hbm, ow.at[f, s], 2)
    load_o.start()
    qkv.start()
    qkv.start_cross()
    out.start()
    out.start_cross()
    smalls[0] = small_ref[...]
    load_g.start()
    load_u.start()
    down_hbm[...] = jnp.zeros_like(down_hbm)
    for n in range(ns):
        count = min(unit, shard - n * unit)
        if count <= 0:
            continue

        @pl.when(s == n)
        def _(n=n, count=count):
            a = pltpu.make_async_copy(down_w.at[pl.ds(n * unit, count)], down_hbm.at[pl.ds(0, count)], lsem.at[5])
            a.start()
            a.wait()

    small_t[1].wait_recv()
    small_t[2].start()
    for k in range(1, outer):
        qkv.step(k)
        out.step(k)
    down.start()
    down.start_cross()
    load_g.wait()
    load_u.wait()
    two = two_ref[:, 0:1]
    gu_hbm[...] = jnp.zeros_like(gu_hbm)
    for n in range(ns):
        count = min(unit, shard - n * unit)
        if count <= 0:
            continue

        @pl.when(s == n)
        def _(n=n, count=count):
            for m, ref in enumerate((gate_v, up_v)):
                for j in range(nf):
                    part = ref[:, j * shard + n * unit : j * shard + n * unit + count].astype(f32)
                    gu_hbm[m, :, j * unit : j * unit + count] = (part * two).astype(bf16)

    own_w = [keep(down_hbm, w_d.at[f], 3), keep(gu_hbm.at[0], w_gu.at[0, f], 4), keep(gu_hbm.at[1], w_gu.at[1, f], 5)]

    small_t[0].wait_recv()
    small_t[2].wait_recv()
    half = 32
    lane = lane_iota(blk, 128)
    freq = jnp.exp((lane % half).astype(f32) * inv_log)
    sign = jnp.where(lane % 64 < half, -1.0, 1.0)
    row = lax.broadcasted_iota(jnp.int32, (blk, 1), 0)
    live = jnp.zeros((1, 1), f32)
    for r in range(ns):
        ints = smalls[r]
        small_out[r] = ints
        col = jnp.transpose(ints)[:, 0:1]
        angle = col * freq
        cos_ref[r] = jnp.cos(angle)
        sin_ref[r] = jnp.sin(angle) * sign
        t = xor_small(s, r)
        start_col[r] = t * blk + row - col.astype(jnp.int32)
        live = live + jnp.sum(ints[1:2, :], axis=1, keepdims=True)
    n_live = live.astype(jnp.int32)
    gate.start()
    gate.start_cross()
    for a in own_w:
        a.start()

    def project_block(r):
        tile = min(256, blk)

        @pl.loop(0, blk // tile)
        def _(i):
            rows = pl.ds(pl.multiple_of(i * tile, tile), tile)
            x = xv[r, rows, :].astype(f32)
            scale = lax.rsqrt(jnp.mean(x * x, axis=-1, keepdims=True) + epsilon)
            xh = (x * scale).astype(bf16)
            xv[r, rows, :] = xh
            raw = dg(xh, wq[...], NN)
            cosine, sine = cos_ref[r, rows, :], sin_ref[r, rows, :]
            to = pl.ds(pl.multiple_of(r * blk + i * tile, tile), tile)
            for p in range(pairs + 1):
                part = raw[:, 128 * p : 128 * (p + 1)]
                raw_ref[to, 128 * p : 128 * (p + 1)] = part
                inv = lax.rsqrt(head_sums(part * part) * (1.0 / 64) + epsilon)
                normal = part * inv * gain_ref[(0 if p < pairs else 1) : (1 if p < pairs else 2), :]
                turned = (normal * cosine + half_swap(normal) * sine).astype(bf16)
                if p < pairs:
                    q_ref[to, 128 * p : 128 * (p + 1)] = turned
                else:
                    k_ref[to, :] = turned
            v_ref[to, :] = raw[:, 128 * (pairs + 1) :].astype(bf16)

    load_x.wait()
    load_o.wait()
    qkv.finish()
    out.finish()
    out_t = (
        send(ow.at[:, s], ow.at[:, s], 6, near),
        send(ow.at[:, s], ow.at[:, s], 7, far),
        send(ow.at[:, far], ow.at[:, far], 8, near),
    )
    out_w = (
        send(ow.at[:, near], ow.at[:, near], 6, near),
        send(ow.at[:, far], ow.at[:, far], 7, far),
        send(ow.at[:, diag], ow.at[:, diag], 8, near),
    )
    out_t[0].start()
    out_t[1].start()
    dy_t[1].start()
    dy_t[0].start()
    project_block(0)
    keep(xv.at[0], xh_hbm.at[0], 0).start()
    tok_t[1].wait_recv()
    tok_t[2].start()
    tok_t[0].wait_recv()
    down.step(1)
    project_block(1)
    keep(xv.at[1], xh_hbm.at[1], 1).start()
    tok_t[2].wait_send()
    project_block(2)
    keep(xv.at[2], xh_hbm.at[2], 2).start()
    tok_t[2].wait_recv()
    up.start()
    up.start_cross()
    project_block(3)
    for a in own_w:
        a.wait()
    keep(xv.at[3], xh_hbm.at[3], 3).start()
    tok_t[0].wait_send()
    tok_t[1].wait_send()

    low = lane_iota(blk, 128) < 64
    row_b = lax.broadcasted_iota(jnp.int32, (blk, 128), 0)

    def pos(t):
        return pl.multiple_of(xor_small(t, s) * blk, blk)

    def prepare(p):
        kv = (pairs * 2 * s + 2 * p) // group - (pairs * 2 * s) // group
        first = kv == 0
        one_a = jnp.where(low, 1.0, 0.0)
        one_b = 1.0 - one_a
        for r in range(ns):
            here = slice(r * blk, (r + 1) * blk)
            kk, vv = k_ref[here, :].astype(f32), v_ref[here, :].astype(f32)
            ksw, vsw = pltpu.roll(kk, 64, 1), pltpu.roll(vv, 64, 1)
            k0, k1 = jnp.where(first, kk, ksw), jnp.where(first, ksw, kk)
            v0, v1 = jnp.where(first, vv, vsw), jnp.where(first, vsw, vv)
            ka[here, :] = jnp.where(low, k0, 0.0).astype(bf16)
            kb[here, :] = jnp.where(low, 0.0, k1).astype(bf16)
            va, vb = jnp.where(low, v0, 0.0), jnp.where(low, 0.0, v1)
            seen = row_b < n_live - xor_small(s, r) * blk
            ra[here, :128], ra[here, 128:] = va.astype(bf16), one_a.astype(bf16)
            rb[here, :128], rb[here, 128:] = vb.astype(bf16), one_b.astype(bf16)
            ral[here, :128] = jnp.where(seen, va, 0.0).astype(bf16)
            ral[here, 128:] = jnp.where(seen, one_a, 0.0).astype(bf16)
            rbl[here, :128] = jnp.where(seen, vb, 0.0).astype(bf16)
            rbl[here, 128:] = jnp.where(seen, one_b, 0.0).astype(bf16)

    kcol = lane_iota(blk, blk)
    qrow = lax.broadcasted_iota(jnp.int32, (blk, blk), 0)

    def query_block(p, i):
        qo = pos(i)
        here = pl.ds(qo, blk)
        lanes = slice(128 * p, 128 * (p + 1))
        q = q_ref[here, lanes]
        st = start_col[xor_small(i, s)]
        ok = (kcol >= st - i * blk) & (kcol <= qrow) & ((kcol < n_live - i * blk) | (kcol == qrow))
        p0 = jnp.where(ok, jnp.exp2(dg(q, ka[here, :], NT) * c), 0.0).astype(bf16)
        p1 = jnp.where(ok, jnp.exp2(dg(q, kb[here, :], NT) * c), 0.0).astype(bf16)
        acc = dg(p0, ra[here, :], NN) + dg(p1, rb[here, :], NN)

        def key_block(j, acc):
            there = pl.ds(pos(j), blk)
            ok = kcol >= (st - j * blk)
            p0 = jnp.where(ok, jnp.exp2(dg(q, ka[there, :], NT) * c), 0.0).astype(bf16)
            p1 = jnp.where(ok, jnp.exp2(dg(q, kb[there, :], NT) * c), 0.0).astype(bf16)
            return acc + dg(p0, ral[there, :], NN) + dg(p1, rbl[there, :], NN)

        acc = lax.fori_loop(0, i, key_block, acc)
        total = acc[:, 128:]
        o_ref[here, lanes] = (acc[:, :128] / total).astype(bf16)
        laug_ref[here, lanes] = aug_lanes(jnp.log(total) * (-8.0))

    jobs = [
        lambda: (gate.step(1), out_t[0].wait_send()),
        lambda: (down.step(2), out_w[1].wait_recv(), out_t[2].start()),
        lambda: gate.step(2),
        lambda: down.step(3) if outer > 3 else None,
        lambda: None,
        lambda: None,
    ]
    for p in range(pairs):
        prepare(p)
        pl.loop(0, ns - 1)(lambda i, p=p: query_block(p, i))
        if 2 * p < len(jobs):
            jobs[2 * p]()
        query_block(p, ns - 1)
        if 2 * p + 1 < len(jobs):
            jobs[2 * p + 1]()
    for job in jobs[2 * pairs :]:
        job()

    att_t = [
        send(o_ref.at[pl.ds(r * blk, blk)], att_in.at[r], 11 + r, to) for r, to in ((1, near), (2, far), (3, diag))
    ]
    att_t[1].start()
    att_t[2].start()
    att_t[0].start()
    dy_u[1].start()
    dy_u[0].start()
    gate.step(3) if outer > 3 else None
    up.step(1) if outer > 3 else None
    up.step(2) if outer > 3 else None
    for k in range(4, outer):
        down.step(k)
        gate.step(k)
    for n in range(4):
        keep(xv.at[n], xh_hbm.at[n], n).wait()
    reload = keep(x_hbm, xv.at[0], 0)
    reload.start()
    load_dy = keep(dy_hbm, xv.at[1], 1)
    load_dy.start()
    out_w[0].wait_recv()
    out_w[2].wait_recv()
    out_t[1].wait_send()
    out_t[2].wait_send()
    att_in[0] = o_ref[pl.ds(0, blk), :]
    reload.wait()
    load_dy.wait()
    own_dy = keep(xv.at[1], dy_all.at[0], 1)
    own_dy.start()
    own_dy.wait()
    for a in att_t:
        a.wait_recv()
    tile = 512
    shards = nf // ns
    squares = jnp.zeros((blk, 1), f32)
    for n in range(width // tile):
        cols = slice(n * tile, (n + 1) * tile)
        acc = xv[0, :, cols].astype(f32)
        for r in range(ns):
            t = xor_small(s, r)
            w = ow[pl.ds(t * shards, shards), :, :, cols].reshape(q_cols, tile)
            acc = acc + dg(att_in[r], w, NN)
        mid_ref[:, cols] = acc
        squares = squares + jnp.sum(acc * acc, axis=-1, keepdims=True)
    inv = lax.rsqrt(squares * (1.0 / width) + epsilon)
    inv_ref[...] = jnp.broadcast_to(inv, inv_ref.shape)
    for n in range(width // tile):
        cols = slice(n * tile, (n + 1) * tile)
        nv[:, cols] = (mid_ref[:, cols] * inv).astype(bf16)
    n2_t = triple(15, nv, lambda r: n2_all.at[r])
    n2_t[1].start()
    n2_t[0].start()
    keeps = [keep(nv, n2_all.at[0], 0), keep(wq, w_qkv_out, 1)]
    for r in range(ns):
        part = ow.at[pl.ds(xor_small(s, r) * shards, shards)]
        keeps.append(keep(part, w_out_out.at[r], 2 + r))
        keeps.append(keep(att_in.at[r], att_tok_out.at[:, pl.ds(r * q_cols, q_cols)], 2 + ns + r))
    for a in keeps:
        a.start()
    for k in range(3, outer):
        up.step(k)
    if outer <= 3:
        for k in range(2, outer):
            up.step(k)
    down.finish()
    gate.finish()
    for a in (dy_t, dy_u):
        a[1].wait_recv()
        a[2].start()
    for a in (dy_t, dy_u):
        a[0].wait()
        a[1].wait_send()
        a[2].wait()
    small_t[0].wait_send()
    small_t[1].wait_send()
    small_t[2].wait_send()
    for a in att_t:
        a.wait_send()
    n2_t[1].wait_recv()
    n2_t[2].start()
    up.finish()
    n2_t[2].wait()
    n2_t[0].wait()
    n2_t[1].wait_send()
    for a in keeps:
        a.wait()


def front_call(x, dy, small, w_query, w_key, w_value, out_mine, w_down, w_gate, w_up, gain_one, gain_two, gains,
               nf, ns, group, head, unit, kv_base, q_cols):
    outer = nf // 2
    blk, width = x.shape
    T = blk * ns
    pairs = q_cols // 128
    cols = q_cols + 256
    drows = w_query.shape[0]
    units = unit * nf
    hbm, vmem = pl.BlockSpec(memory_space=pl.ANY), pl.BlockSpec(memory_space=pltpu.VMEM)
    c = math.log2(math.e) * head**-0.5
    inv_log = -2.0 / head * math.log(rope_base)
    S = jax.ShapeDtypeStruct
    quarter = out_mine.shape[0]
    return pl.pallas_call(
        functools.partial(front_kernel, outer, ns, pairs, group, c, inv_log, unit, [b * head for b in kv_base]),
        in_specs=[hbm, hbm, vmem, vmem, vmem, vmem, hbm, hbm, hbm, hbm, vmem, vmem, vmem],
        out_specs=[hbm] * 8 + [vmem] * 11,
        out_shape=[
            S((ns, blk, width), bf16), S((ns, blk, width), bf16), S((ns, blk, width), bf16),
            S((nf, unit, width), bf16), S((2, nf, drows, units), bf16),
            S((width, cols), bf16), S((ns, nf // ns, ns, quarter, width), bf16), S((blk, ns * q_cols), bf16),
            S((T, q_cols), bf16), S((T, 128), bf16), S((T, 128), bf16), S((T, q_cols + 128), f32),
            S((ns, blk, 128), f32), S((ns, blk, 128), f32), S((T, q_cols), bf16), S((T, q_cols), bf16),
            S((blk, width), f32), S((blk, 128), f32), S((ns,) + small.shape, f32),
        ],
        scratch_shapes=[
            pltpu.VMEM((drows, cols), bf16), pltpu.VMEM((unit, width), bf16), pltpu.VMEM((2, drows, units), bf16),
            pltpu.VMEM(w_gate.shape, bf16), pltpu.VMEM(w_up.shape, bf16),
            pltpu.VMEM((ns, blk, width), bf16), pltpu.VMEM((width, cols), bf16),
            pltpu.VMEM((nf, ns, quarter, width), bf16), pltpu.VMEM((ns,) + small.shape, f32),
            pltpu.VMEM((ns, blk, 1), jnp.int32), pltpu.VMEM((ns, blk, q_cols), bf16), pltpu.VMEM((blk, width), bf16),
        ]
        + [pltpu.VMEM((T, 128), bf16)] * 2
        + [pltpu.VMEM((T, 256), bf16)] * 4
        + [
            pltpu.SemaphoreType.DMA((2, 5 * ring_sems(outer))), pltpu.SemaphoreType.DMA((2, 21)),
            pltpu.SemaphoreType.DMA((2 + 2 * ns,)),
        ],
        compiler_params=pltpu.CompilerParams(
            collective_id=0, has_side_effects=True, vmem_limit_bytes=67043328
        ),
        cost_estimate=tiny,
        name="front",
    )(x, dy, small, w_query, w_key, w_value, out_mine, w_down, w_gate, w_up, gain_one, gain_two, gains)


class Scatter:
    def __init__(self, sems, base, outer, ns, f, s, xz, own, part, zr, fin, out, local):
        self.sems, self.base, self.outer, self.f, self.s = sems, base, outer, f, s
        self.at, self.inner = f // 2, f % 2
        self.near = s + 1 - 2 * (s % 2)
        self.far = s + 2 - 4 * (s // 2)
        self.diag = self.far + 1 - 2 * (s % 2)
        self.xz, self.own, self.part, self.zr, self.fin, self.out, self.local = xz, own, part, zr, fin, out, local

    def copy(self, src, dst, send, recv, to):
        return pltpu.make_async_remote_copy(
            src, dst, self.sems.at[0, self.base + send], self.sems.at[1, self.base + recv],
            device_id=to, device_id_type=pl.DeviceIdType.MESH,
        )

    def cross(self, k):
        return self.copy(self.part(k), self.xz.at[k], k, k, (self.f + 1 - 2 * self.inner, self.s))

    def line(self, k, src=None):
        n = self.outer
        src = self.xz.at[k] if src is None else src
        return self.copy(src, self.zr.at[self.at], n + k, n + self.at, (2 * k + self.inner, self.s))

    def line_wait(self, k):
        n = self.outer
        return self.copy(self.zr.at[k], self.zr.at[k], n + k, n + k, (2 * k + self.inner, self.s))

    def take(self, k):
        self.cross(k).wait_recv()
        own = self.own(k)
        self.xz[k] = (self.xz[k].astype(f32) + own.astype(f32)).astype(bf16)
        pl.when(k != self.at)(lambda: self.line(k).start())

    def total(self, own=None, fetch=None):
        n = self.outer
        acc = (self.xz[self.at] if own is None else own).astype(f32)
        for m in range(1, n):
            k = (self.at + m) % n
            self.line_wait(k).wait_recv()
            acc = acc + (self.zr[k] if fetch is None else fetch(self.zr.at[k])).astype(f32)
        self.fin[...] = acc.astype(bf16)
        if self.out is None:
            return
        n = 2 * self.outer
        self.copy(self.fin, self.out.at[self.s], n + 1, n + 1, (self.f, self.far)).start()
        self.copy(self.fin, self.out.at[self.s], n, n, (self.f, self.near)).start()
        self.local(self.fin, self.out.at[self.s]).start()

    def forward(self):
        n = 2 * self.outer
        far = self.out.at[self.far]
        self.copy(far, far, n + 1, n + 1, (self.f, self.far)).wait_recv()
        self.copy(far, far, n + 2, n + 2, (self.f, self.near)).start()

    def finish(self, sent=None, crossed=True):
        n = 2 * self.outer
        if self.out is not None:
            near, diag = self.out.at[self.near], self.out.at[self.diag]
            self.copy(near, near, n, n, (self.f, self.near)).wait_recv()
            self.copy(diag, diag, n + 2, n + 2, (self.f, self.near)).wait_recv()
            self.copy(self.fin, near, n, n, (self.f, self.near)).wait_send()
            self.copy(self.fin, near, n + 1, n + 1, (self.f, self.far)).wait_send()
            self.copy(near, near, n + 2, n + 2, (self.f, self.near)).wait_send()
            self.local(self.fin, self.out.at[self.s]).wait()
        for k in range(self.outer):
            if crossed:
                self.cross(k).wait_send()
            pl.when(k != self.at)(lambda k=k: self.line(k, sent and sent(k)).wait_send())


def back_kernel(
    outer, ns, pairs, group, c, scale,
    datt_hbm, q_ref, laug_ref, o_ref, k_ref, v_ref, raw_hbm, cos_hbm, sin_hbm, start_ref, live_ref, gain_ref, wq_ref,
    xh_hbm, gd_hbm, gg_hbm, gu_hbm, att_hbm, dmid_hbm, lo_hbm,
    dn_out, lo_out, sd_out, sg_out, fin_u, so_out, fin_q, go_hbm, lo_g3, dn_g3, og1, zr_d, zr_g, zr_u, dgain_ref,
    do_v, qa, qb, qaug, doa, dob, doaug, kaug0, kaug1, vaug0, vaug1, dqacc, dq_v, dk_acc, dv_acc,
    dqkv, dnv, raw_t, cos_t, sin_t, xh_t, gq_send, xz_g, xz_u, xz_o, xz_q, zr_o, zr_q,
    fin_d, fin_g, fin_o, tile_g, o_t, o_g, gsum, gslot, gline, ssem, tsem, lsem,
):
    f, s = lax.axis_index("fsdp"), lax.axis_index("sp")
    core = s % 2
    near, far = s + 1 - 2 * core, s + 2 - 4 * (s // 2)
    diag = far + 1 - 2 * core
    at, inner = f // 2, f % 2
    cross_f = f + 1 - 2 * inner
    T = q_ref.shape[0]
    blk = T // ns
    q_cols = pairs * 128

    barrier = pltpu.get_barrier_semaphore()

    def greet(ff, ss):
        pl.semaphore_signal(barrier, inc=1, device_id=(ff, ss), device_id_type=pl.DeviceIdType.MESH)

    greet(f, near)
    greet(f, far)
    greet(f, diag)
    greet(cross_f, s)
    for m in range(1, outer):
        greet(2 * ((at + m) % outer) + inner, s)
    pl.semaphore_wait(barrier, 3 + outer)

    def send(src, dst, n, to, ff=None):
        return pltpu.make_async_remote_copy(
            src, dst, tsem.at[0, n], tsem.at[1, n], device_id=(f if ff is None else ff, to),
            device_id_type=pl.DeviceIdType.MESH,
        )

    def keep(src, dst, n):
        return pltpu.make_async_copy(src, dst, lsem.at[n])

    def fetch(src, dst, n=0):
        a = keep(src, dst, n)
        a.start()
        a.wait()
        return dst

    turn = [n // 2 if n % 2 else outer - 1 - n // 2 for n in range(outer)]
    per = 2 * outer + 3

    def local(n):
        return lambda src, dst: keep(src, dst, n)

    part = lambda ref: lambda k: ref.at[2 * k + 1 - inner]
    sd = Scatter(ssem, 0, outer, ns, f, s, None, None, None, zr_d, fin_d, sd_out, local(1))
    sg = Scatter(ssem, per, outer, ns, f, s, xz_g, lambda k: fetch(gg_hbm.at[2 * k + inner], tile_g)[...], part(gg_hbm),
                 zr_g, fin_g, sg_out, local(2))
    su = Scatter(ssem, 2 * per, outer, ns, f, s, xz_u, lambda k: fetch(gu_hbm.at[2 * k + inner], tile_g)[...], part(gu_hbm),
                 zr_u, fin_u, None, None)
    so = Scatter(ssem, 3 * per, outer, ns, f, s, xz_o, lambda k: o_t[2 * k + inner], part(o_t), zr_o, fin_o, so_out, local(4))
    sq = Scatter(ssem, 4 * per, outer, ns, f, s, xz_q, None, lambda k: gq_send.at[k], zr_q, fin_q, None, None)

    def do_part(r, to):
        return send(datt_hbm.at[:, pl.ds(r * q_cols, q_cols)], do_v.at[pl.ds(r * blk, blk)], r, to)

    datt_t = [do_part(2, far), do_part(3, diag), do_part(1, near)]
    for a in datt_t:
        a.start()
    own_do = keep(datt_hbm.at[:, pl.ds(0, q_cols)], do_v.at[pl.ds(0, blk)], 6)
    own_do.start()
    sent_d = lambda k: gd_hbm.at[k]
    for k in turn:
        pl.when(k != at)(lambda k=k: sd.line(k, sent_d(k)).start())
        sg.cross(k).start()
    for k in turn:
        su.cross(k).start()
    o1 = send(go_hbm.at[:, near], og1, 4, near)
    o3 = send(go_hbm.at[:, diag], o_g.at[0], 5, near)
    of = send(o_g.at[0], o_g.at[1], 6, far)
    lo1 = send(lo_hbm.at[1], lo_out.at[0], 7, near)
    lo3 = send(lo_hbm.at[3], lo_g3, 8, near)
    lof = send(dnv.at[2], lo_out.at[1], 9, far)
    lo3.start()
    lo1.start()
    load_d = keep(dmid_hbm, dnv.at[1], 0)
    load_d.start()
    load_a = [keep(att_hbm.at[:, pl.ds(r * q_cols, q_cols)], dq_v.at[pl.ds(r * blk, blk)], 1 + r) for r in range(ns)]
    for a in load_a:
        a.start()
    for a in load_a + [load_d]:
        a.wait()
    shards, quarter = 2 * outer // ns, o_t.shape[1]
    half_w = 512
    for r in range(ns):
        for n in range(dnv.shape[2] // half_w):
            cols = slice(n * half_w, (n + 1) * half_w)
            grad = dg(dq_v[r * blk : (r + 1) * blk, :], dnv[1, :, cols], TN).astype(bf16)
            o_t[:, :, cols] = grad.reshape(shards * ns, quarter, half_w)
        outs = [
            keep(o_t.at[pl.ds(a * ns, ns)], go_hbm.at[xor_small(s, r) * shards + a], 1 + a) for a in range(shards)
        ]
        for a in outs:
            a.start()
        for a in outs:
            a.wait()
    o3.start()
    o1.start()
    o3.wait_recv()
    fetch(go_hbm.at[:, far], o_t)
    for n in range(o_t.shape[0]):
        o_g[0, n] = (o_g[0, n].astype(f32) + o_t[n].astype(f32)).astype(bf16)
    of.start()
    lo3.wait_recv()
    fetch(lo_g3, dnv.at[2])
    fetch(lo_hbm.at[2], dnv.at[0])
    chunk = 128

    @pl.loop(0, blk // chunk)
    def _(i):
        rows = pl.ds(pl.multiple_of(i * chunk, chunk), chunk)
        dnv[2, rows, :] = (dnv[2, rows, :].astype(f32) + dnv[0, rows, :].astype(f32)).astype(bf16)

    fetch(go_hbm.at[:, s], o_t)
    lof.start()
    own_do.wait()
    for a in datt_t:
        a.wait_recv()

    dk_acc[...] = jnp.zeros_like(dk_acc)
    dv_acc[...] = jnp.zeros_like(dv_acc)
    low = lane_iota(blk, 128) < 64
    lane = lane_iota(blk, 128)
    n_live = live_ref[0:1, 0:1]
    krow = lax.broadcasted_iota(jnp.int32, (blk, blk), 0)
    qcol = lane_iota(blk, blk)

    def pos(t):
        return pl.multiple_of(xor_small(t, s) * blk, blk)

    def is_first(p):
        return (pairs * 2 * s + 2 * p) // group - (pairs * 2 * s) // group == 0

    def prepare(p):
        first = is_first(p)
        lanes = slice(128 * p, 128 * (p + 1))
        ones_a = jnp.where(lane < 3, 1.0, 0.0).astype(bf16)
        ones_b = jnp.where((lane >= 64) & (lane < 67), 1.0, 0.0).astype(bf16)
        for r in range(ns):
            here = slice(r * blk, (r + 1) * blk)
            kk, vv = k_ref[here, :].astype(f32), v_ref[here, :].astype(f32)
            ksw, vsw = pltpu.roll(kk, 64, 1), pltpu.roll(vv, 64, 1)
            k_a = jnp.where(low, jnp.where(first, kk, ksw), 0.0).astype(bf16)
            k_b = jnp.where(low, 0.0, jnp.where(first, ksw, kk)).astype(bf16)
            kaug0[here, :128], kaug0[here, 128:] = k_a, ones_a
            kaug1[here, :128], kaug1[here, 128:] = k_b, ones_b
            vaug0[here, :128] = jnp.where(low, jnp.where(first, vv, vsw), 0.0).astype(bf16)
            vaug0[here, 128:] = ones_a
            vaug1[here, :128] = jnp.where(low, 0.0, jnp.where(first, vsw, vv)).astype(bf16)
            vaug1[here, 128:] = ones_b
            q = q_ref[here, lanes]
            qf = q.astype(f32)
            qaug[here, :128], qaug[here, 128:] = q, laug_ref[here, lanes]
            qa[here, :] = jnp.where(low, qf, 0.0).astype(bf16)
            qb[here, :] = jnp.where(low, 0.0, qf).astype(bf16)
            do = do_v[here, lanes]
            dof = do.astype(f32)
            doa[here, :] = jnp.where(low, dof, 0.0).astype(bf16)
            dob[here, :] = jnp.where(low, 0.0, dof).astype(bf16)
            doaug[here, :128] = do
            doaug[here, 128:] = aug_lanes(-head_sums(dof * o_ref[here, lanes].astype(f32)))
        dqacc[...] = jnp.zeros_like(dqacc)

    def step(j, here, qo, ok, dk, dv):
        there = pl.ds(qo, blk)
        qg, dg_ = qaug[there, :], doaug[there, :]
        e0 = jnp.where(ok, jnp.exp2(dg(kaug0[here, :], qg, NT) * c), 0.0)
        e1 = jnp.where(ok, jnp.exp2(dg(kaug1[here, :], qg, NT) * c), 0.0)
        ds0 = (e0 * dg(vaug0[here, :], dg_, NT)).astype(bf16)
        ds1 = (e1 * dg(vaug1[here, :], dg_, NT)).astype(bf16)
        dv = dv + dg(e0.astype(bf16), doa[there, :], NN) + dg(e1.astype(bf16), dob[there, :], NN)
        dk = dk + dg(ds0, qa[there, :], NN) + dg(ds1, qb[there, :], NN)
        dqacc[there, :] += dg(ds0, kaug0[here, :128], TN) + dg(ds1, kaug1[here, :128], TN)
        return dk, dv

    def key_block(p, j):
        here = pl.ds(pos(j), blk)
        st = start_ref[0:1, here] - j * blk
        ok = (krow >= st) & (krow <= qcol) & ((krow < n_live - j * blk) | (krow == qcol))
        z = jnp.zeros((blk, 128), f32)
        dk, dv = step(j, here, pos(j), ok, z, z)

        def query_block(i, carry):
            qo = pos(i)
            st = start_ref[0:1, pl.ds(qo, blk)] - j * blk
            ok = (krow >= st) & (krow < n_live - j * blk)
            return step(j, here, qo, ok, *carry)

        dk, dv = lax.fori_loop(j + 1, ns, query_block, (dk, dv))
        first = is_first(p)
        dk, dv = dk * scale + pltpu.roll(dk * scale, 64, 1), dv + pltpu.roll(dv, 64, 1)
        dk_acc[here, :] += jnp.where(first, jnp.where(low, dk, 0.0), jnp.where(low, 0.0, dk))
        dv_acc[here, :] += jnp.where(first, jnp.where(low, dv, 0.0), jnp.where(low, 0.0, dv))

    def own_o():
        of.wait()
        o1.wait_recv()
        fetch(og1, o_g.at[0])
        for n in range(o_t.shape[0]):
            o_t[n] = (o_t[n].astype(f32) + o_g[0, n].astype(f32) + o_g[1, n].astype(f32)).astype(bf16)
        for k in turn:
            so.cross(k).start()

    jobs = {
        (0, 0): lambda: sg.take(turn[0]),
        (0, 1): lambda: (sg.take(turn[1]), sg.take(turn[2])),
        (1, 0): lambda: (sg.take(turn[3]) if outer > 3 else None, own_o()),
        (1, 1): lambda: (sd.total(fetch(gd_hbm.at[at], fin_d)[...], lambda r: fetch(r, fin_d)[...]), su.take(turn[0])),
        (2, 0): lambda: su.take(turn[1]),
        (2, 1): lambda: (su.take(turn[2]), sd.forward()),
    }
    for p in range(pairs):
        prepare(p)
        key_block(p, 0)
        jobs.get((p, 0), lambda: None)()
        pl.loop(1, ns)(lambda j, p=p: key_block(p, j))
        dq_v[:, 128 * p : 128 * (p + 1)] = (dqacc[...] * scale).astype(bf16)
        jobs.get((p, 1), lambda: None)()

    tile = min(256, blk)
    gsum[...] = jnp.zeros_like(gsum)

    def turn_block(r):
        @pl.loop(0, blk // tile)
        def _(i):
            rows = pl.ds(pl.multiple_of(r * blk + i * tile, tile), tile)
            part_rows = pl.ds(pl.multiple_of(i * tile, tile), tile)
            loads = [
                keep(raw_hbm.at[rows], raw_t, 0), keep(cos_hbm.at[r, part_rows], cos_t, 7), keep(sin_hbm.at[r, part_rows], sin_t, 8),
            ]
            for a in loads:
                a.start()
            for a in loads:
                a.wait()
            cosine, sine = cos_t[...], sin_t[...]
            for p in range(pairs + 1):
                which = 0 if p < pairs else 1
                lanes = slice(128 * p, 128 * (p + 1))
                grad = dq_v[rows, lanes].astype(f32) if p < pairs else dk_acc[rows, :].astype(bf16).astype(f32)
                raw = raw_t[:, lanes]
                inv = lax.rsqrt(head_sums(raw * raw) * (1.0 / 64) + epsilon)
                normal = raw * inv
                grad = grad * cosine - half_swap(grad) * sine
                gsum[which] += jnp.sum((grad * normal).reshape(tile // 8, 8, 128), axis=0)
                grad = grad * gain_ref[which : which + 1, :]
                mean = head_sums(grad * normal) * (1.0 / 64)
                dqkv[rows, lanes] = (inv * (grad - normal * mean)).astype(bf16)
            dqkv[rows, 128 * (pairs + 1) :] = dv_acc[rows, :].astype(bf16)
            dnv[{3: 0, 2: 1, 1: 2, 0: 0}[r], part_rows, :] = dg(dqkv[rows, :], wq_ref[...], NT).astype(bf16)

    dn1 = send(dnv.at[2], dn_out.at[1], 10, near)
    dn3 = send(dnv.at[0], dn_g3, 11, near)
    dnf = send(dnv.at[1], dn_out.at[2], 12, far)
    turn_block(3)
    dn3.start()
    turn_block(2)
    dn3.wait()
    fetch(dn_g3, dnv.at[0])

    @pl.loop(0, blk // chunk)
    def _(i):
        rows = pl.ds(pl.multiple_of(i * chunk, chunk), chunk)
        dnv[1, rows, :] = (dnv[1, rows, :].astype(f32) + dnv[0, rows, :].astype(f32)).astype(bf16)

    dnf.start()
    lof.wait_send()
    turn_block(1)
    dn1.start()
    su.take(turn[3]) if outer > 3 else None
    turn_block(0)
    own_dn = keep(dnv.at[0], dn_out.at[0], 9)
    own_dn.start()
    for k in turn[4:]:
        sg.take(k)
        su.take(k)

    drows, span = gq_send.shape[1], xh_t.shape[1]

    def grad_block(b):
        first = (b * drows) // span
        fetch(xh_hbm.at[:, pl.ds(pl.multiple_of(first * span, span), span)], xh_t)
        grad = dg(xh_t[...], dqkv[...], TN)
        if span > drows:
            grad = jnp.where(b % 2 == 0, grad[:drows], grad[drows:])
        return grad.astype(bf16)

    for k in turn:
        gq_send[k] = grad_block(2 * k + 1 - inner)
        if k != turn[0]:
            sq.cross(turn[turn.index(k) - 1]).start()
    so.take(turn[0])
    sq.cross(turn[-1]).start()
    for k in turn[1:]:
        so.take(k)
    sq.own = lambda k: grad_block(2 * k + inner)

    gslot[0] = jnp.concatenate(
        [jnp.sum(gsum[0], axis=0, keepdims=True), jnp.sum(gsum[1], axis=0, keepdims=True), jnp.zeros((6, 128), f32)]
    )
    hops = [
        send(gslot.at[0], gslot.at[3], 13, near), send(gslot.at[1], gslot.at[4], 14, far),
        send(gslot.at[2], gslot.at[5], 15, s, cross_f),
    ]
    hops[0].start()
    sg.total(None, lambda r: fetch(r, fin_g)[...])
    hops[0].wait_recv()
    gslot[1] = gslot[0] + gslot[3]
    hops[1].start()
    for k in turn:
        sq.take(k)
    hops[1].wait_recv()
    gslot[2] = gslot[1] + gslot[4]
    hops[2].start()
    so.total()
    hops[2].wait_recv()
    gline[at] = gslot[2] + gslot[5]
    lines = [
        send(gline.at[at], gline.at[at], 16 + m, s, 2 * ((at + m) % outer) + inner) for m in range(1, outer)
    ]
    for a in lines:
        a.start()
    su.total(None, lambda r: fetch(r, fin_u)[...])
    sg.forward()
    so.forward()
    for m in range(1, outer):
        k = (at + outer - m) % outer
        send(gline.at[k], gline.at[k], 16 + m, s, 2 * k + inner).wait_recv()
    total = gline[0]
    for k in range(1, outer):
        total = total + gline[k]
    dgain_ref[...] = total + pltpu.roll(total, 64, 1)
    sq.total()

    sd.finish(sent_d, False)
    for a in (sg, su, so, sq):
        a.finish()
    for a in lines + hops + datt_t + [o1, o3, lo1, lo3, dn1, dnf]:
        a.wait_send()
    for a in (lo1, lof, dn1, dnf):
        a.wait_recv()
    own_dn.wait()


def back_call(datt, q, laug, o, k, v, raw, cosine, sine, start_row, n_live, gains, w_qkv, xh, gd, gg, gu, att, dmid, lo, nf, ns, quarter, group, head):
    outer = gd.shape[0]
    T = q.shape[0]
    blk = T // ns
    width, cols = w_qkv.shape
    pairs = cols // 128 - 2
    q_cols = pairs * 128
    scale = head**-0.5
    c = math.log2(math.e) * scale
    hbm, vmem = pl.BlockSpec(memory_space=pl.ANY), pl.BlockSpec(memory_space=pltpu.VMEM)
    S, V = jax.ShapeDtypeStruct, pltpu.VMEM
    dblk, gblk, oblk = gd.shape[1:], gg.shape[1:], (quarter, width)
    drows = gblk[0]
    qblk = (drows, cols)
    half = (T, 128)
    wide = (T, 256)
    per = 2 * outer + 3
    return pl.pallas_call(
        functools.partial(back_kernel, outer, ns, pairs, group, c, scale),
        in_specs=[hbm] + [vmem] * 5 + [hbm] * 3 + [vmem] * 4 + [hbm] * 7,
        out_specs=[hbm] * 4 + [vmem, hbm, vmem] + [hbm] * 7 + [vmem],
        out_shape=[
            S((3, blk, width), bf16), S((2, blk, width), bf16),
            S((ns,) + dblk, bf16), S((ns,) + gblk, bf16), S(gblk, bf16), S((ns,) + oblk, bf16), S(qblk, bf16),
            S((2 * outer, ns) + oblk, bf16),
            S((blk, width), bf16), S((blk, width), bf16), S((2 * outer,) + oblk, bf16), S((outer,) + dblk, bf16), S((outer,) + gblk, bf16), S((outer,) + gblk, bf16),
            S((8, 128), f32),
        ],
        scratch_shapes=[
            V((T, q_cols), bf16), V(half, bf16), V(half, bf16), V(wide, bf16), V(half, bf16), V(half, bf16), V(wide, bf16),
            V(wide, bf16), V(wide, bf16), V(wide, bf16), V(wide, bf16),
            V(half, f32), V((T, q_cols), bf16), V(half, f32), V(half, f32),
            V((T, cols), bf16), V((3, blk, width), bf16),
            V((min(256, blk), q_cols + 128), f32), V((min(256, blk), 128), f32), V((min(256, blk), 128), f32),
            V((T, drows if drows % 128 == 0 else 2 * drows), bf16), V((outer,) + qblk, bf16),
            V((outer,) + gblk, bf16), V((outer,) + gblk, bf16), V((outer,) + oblk, bf16), V((outer,) + qblk, bf16),
            V((outer,) + oblk, bf16), V((outer,) + qblk, bf16),
            V(dblk, bf16), V(gblk, bf16), V(oblk, bf16),
            V(gblk, bf16), V((2 * outer,) + oblk, bf16), V((2, 2 * outer) + oblk, bf16),
            V((2, 8, 128), f32), V((6, 8, 128), f32), V((outer, 8, 128), f32),
            pltpu.SemaphoreType.DMA((2, 5 * per)), pltpu.SemaphoreType.DMA((2, 16 + outer)), pltpu.SemaphoreType.DMA((10 + outer,)),
        ],
        compiler_params=pltpu.CompilerParams(
            collective_id=1, has_side_effects=True, vmem_limit_bytes=63 * 2**20
        ),
        cost_estimate=tiny,
        name="back",
    )(datt, q, laug, o, k, v, raw, cosine, sine, start_row, n_live, gains, w_qkv, xh, gd, gg, gu, att, dmid, lo)


def ffn_kernel(tile, n2_ref, dy_ref, wg_ref, wu_ref, wd_ref, hid_ref, dg_ref, du_ref, dn_ref):
    n2, dy = n2_ref[...], dy_ref[...]
    units, width = wd_ref.shape
    for j in range(units // tile):
        cols = slice(j * tile, (j + 1) * tile)
        gate = dg(n2, wg_ref[0, :, cols], NN)
        up = dg(n2, wu_ref[0, :, cols], NN)
        dhid = dg(dy, wd_ref[cols, :], NT)
        sig = jax.nn.sigmoid(gate)
        act = gate * sig
        hid_ref[:, cols] = (act * up).astype(bf16)
        du_ref[:, cols] = (dhid * act).astype(bf16)
        dg_ref[:, cols] = (dhid * up * (sig * (1.0 + gate * (1.0 - sig)))).astype(bf16)
    for j in range(width // 512):
        rows = slice(j * 512, (j + 1) * 512)
        grad = dg(dg_ref[...], wg_ref[0, rows, :], NT) + dg(du_ref[...], wu_ref[0, rows, :], NT)
        dn_ref[:, rows] = grad.astype(bf16)


def ffn_call(n2_all, dy_all, w_gu, w_d, rows=256, tile=256):
    length, width = n2_all.shape
    units = w_d.shape[0]
    once = pl.Buffered(1)
    big = jax.ShapeDtypeStruct((length, units), bf16)
    return pl.pallas_call(
        functools.partial(ffn_kernel, tile),
        grid=(length // rows,),
        in_specs=[pl.BlockSpec((rows, width), lambda i: (i, 0))] * 2
        + [
            pl.BlockSpec((1, width, units), lambda i: (0, 0, 0), pipeline_mode=once),
            pl.BlockSpec((1, width, units), lambda i: (1, 0, 0), pipeline_mode=once),
            pl.BlockSpec((units, width), lambda i: (0, 0), pipeline_mode=once),
        ],
        out_specs=[pl.BlockSpec((rows, units), lambda i: (i, 0))] * 3 + [pl.BlockSpec((rows, width), lambda i: (i, 0))],
        out_shape=[big, big, big, jax.ShapeDtypeStruct((length, width), bf16)],
        compiler_params=pltpu.CompilerParams(vmem_limit_bytes=62 * 2**20),
        cost_estimate=tiny,
        name="ffn",
    )(n2_all, dy_all, w_gu, w_gu, w_d)


def join_kernel(members, shards, shard, unit, gain_ref, m_ref, w_ref, out_ref, sum_ref):
    for k in range(members):
        width = min(unit, shard - k * unit)
        for j in range(shards):
            part = m_ref[k, :, j * unit : j * unit + width].astype(f32)
            out_ref[:, j * shard + k * unit : j * shard + k * unit + width] = part
    full = out_ref[...]
    sum_ref[...] = jnp.broadcast_to(
        jnp.sum(full * w_ref[...].astype(f32), axis=-1, keepdims=True), sum_ref.shape
    )
    out_ref[...] = full * gain_ref[...]


def join_call(gain, stacked, weight, members, shards, shard, unit):
    rows, cols = weight.shape
    tile = min(64, rows)
    return pl.pallas_call(
        functools.partial(join_kernel, members, shards, shard, unit),
        grid=(rows // tile,),
        in_specs=[
            pl.BlockSpec((tile, 1), lambda i: (i, 0)),
            pl.BlockSpec((members, tile, shards * unit), lambda i: (0, i, 0)),
            pl.BlockSpec((tile, cols), lambda i: (i, 0)),
        ],
        out_specs=[
            pl.BlockSpec((tile, cols), lambda i: (i, 0)),
            pl.BlockSpec((tile, 128), lambda i: (i, 0)),
        ],
        out_shape=[
            jax.ShapeDtypeStruct((rows, cols), f32),
            jax.ShapeDtypeStruct((rows, 128), f32),
        ],
        compiler_params=pltpu.CompilerParams(vmem_limit_bytes=60 * 2**20),
        name="join_units",
    )(gain, stacked, weight)


def heads_kernel(members, q_cols, kv_base, gain_ref, m_ref, wq_ref, wk_ref, wv_ref, q_ref, k_ref, v_ref, sum_ref):
    for k in range(members):
        q_ref[:, k * q_cols : (k + 1) * q_cols] = m_ref[k, :, :q_cols].astype(f32)
    for n, ref in enumerate((k_ref, v_ref)):
        at = q_cols + 128 * n
        ref[...] = jnp.zeros_like(ref)
        for k in range(members):
            ref[:, kv_base[k] : kv_base[k] + 128] += m_ref[k, :, at : at + 128].astype(f32)
    total = 0.0
    for ref, w in ((q_ref, wq_ref), (k_ref, wk_ref), (v_ref, wv_ref)):
        full = ref[...]
        total = total + jnp.sum(full * w[...].astype(f32), axis=-1, keepdims=True)
        ref[...] = full * gain_ref[...]
    sum_ref[...] = jnp.broadcast_to(total, sum_ref.shape)


def heads_call(gain, stacked, w_query, w_key, w_value, kv_base, q_cols):
    members, rows, cols = stacked.shape
    tile = min(64, rows)
    outs = [w_query.shape[1], w_key.shape[1], w_value.shape[1], 128]
    return pl.pallas_call(
        functools.partial(heads_kernel, members, q_cols, kv_base),
        grid=(rows // tile,),
        in_specs=[pl.BlockSpec((tile, 1), lambda i: (i, 0)), pl.BlockSpec((members, tile, cols), lambda i: (0, i, 0))]
        + [pl.BlockSpec((tile, n), lambda i: (i, 0)) for n in outs[:3]],
        out_specs=[pl.BlockSpec((tile, n), lambda i: (i, 0)) for n in outs],
        out_shape=[jax.ShapeDtypeStruct((rows, n), f32) for n in outs],
        compiler_params=pltpu.CompilerParams(vmem_limit_bytes=60 * 2**20),
        name="join_heads",
    )(gain, stacked, w_query, w_key, w_value)


def dot_bf(a, b, dims):
    return dg(a, b, dims).astype(bf16)


def local(
    tokens, seg_ids, pad_mask, positions, attn_gain, w_query, w_key, w_value, query_gain,
    key_gain, w_out, ffn_gain, w_gate, w_up, w_down, cotangent,
):
    nf, ns = lax.axis_size("fsdp"), lax.axis_size("sp")
    f, s = lax.axis_index("fsdp"), lax.axis_index("sp")
    seq_count, blk, width = tokens.shape
    assert seq_count == 1 and ns == 4
    length = blk * ns
    head = query_gain.shape[0]
    q_heads, kv_heads = w_query.shape[1] // head, w_key.shape[1] // head
    group = q_heads // kv_heads
    q_local = q_heads // ns
    kv_base = [(q_local * k) // group for k in range(ns)]
    pairs = q_local // 2
    q_cols = q_local * head
    kv_map = jnp.array(
        [[(q_local * k + 2 * p) // group - kv_base[k] for p in range(pairs)] for k in range(ns)],
        jnp.int32,
    )[s]
    base = jnp.array(kv_base, jnp.int32)[s] * head
    shard = w_down.shape[0]
    unit = -(-(-(-shard // ns)) // 16) * 16
    units = unit * nf
    out_rows = w_out.shape[0]
    quarter = out_rows // ns
    sub = 512

    x = tokens[0]
    dy = cotangent[0]
    gain_one = attn_gain.astype(f32)[:, None]
    gain_two = ffn_gain.astype(f32)[:, None]

    kv_cols = 2 * head
    out_mine = lax.dynamic_slice_in_dim(w_out, s * quarter, quarter, 0)
    small = jnp.concatenate(
        [positions.astype(f32), pad_mask.astype(f32), jnp.zeros((6, blk), f32)]
    )
    gains = jnp.concatenate(
        [
            jnp.tile(query_gain.astype(f32), 2)[None],
            jnp.tile(key_gain.astype(f32), 2)[None],
            jnp.zeros((6, 2 * head), f32),
        ]
    )
    (
        xh, dy_all, n2_all, w_d, w_gu, w_qkv, w_out_rel, att, q, k, v, raw, cosine, sine,
        attended, laug, middle, inv_two, small_all,
    ) = front_call(
        x, dy, small, w_query, w_key, w_value, out_mine, w_down, w_gate, w_up,
        jnp.broadcast_to(gain_one, (width // nf, 128)), jnp.broadcast_to(gain_two, (width // nf, 128)), gains,
        nf, ns, group, head, unit, kv_base, q_cols,
    )
    xh = xh.reshape(length, width)
    w_d, w_gu = w_d.reshape(units, width), w_gu.reshape(2, width, units)
    w_out_rel = w_out_rel.reshape(ns * q_cols, width)
    pos_rel = small_all[:, 0].astype(jnp.int32)
    n_live = jnp.sum(small_all[:, 1]).astype(jnp.int32)
    true_block = s ^ jnp.arange(ns)
    start_rel = (true_block[:, None] * blk + jnp.arange(blk)[None] - pos_rel).reshape(length)
    xf = x.astype(f32)
    inv_two = inv_two[:, :1]

    n2_all, dy_all = n2_all.reshape(length, width), dy_all.reshape(length, width)
    hidden, dgate, dup, dn2 = ffn_call(n2_all, dy_all, w_gu, w_d)
    dn2 = [dn2[r * blk : (r + 1) * blk] for r in range(ns)]
    got3 = perm_s(dn2[3], 1)
    got1 = perm_s(dn2[1], 1)
    pair = (dn2[2].astype(f32) + got3.astype(f32)).astype(bf16)
    dn2_far = perm_s(pair, 2)

    hidden_a = after(hidden, pair, got1)
    grad_d = dot_bf(hidden_a, dy_all, TN).reshape(nf // 2, 2, unit, width)
    d_own = lax.dynamic_index_in_dim(grad_d, f % 2, 1, keepdims=False)
    d_other = lax.dynamic_index_in_dim(grad_d, 1 - f % 2, 1, keepdims=False)
    d_got = perm_f(d_other, 1)
    dgate_a, dup_a = after(dgate, d_other), after(dup, d_other)
    grad_g = dot_bf(n2_all, dgate_a, TN).reshape(nf, width // nf, units)
    grad_u = dot_bf(n2_all, dup_a, TN).reshape(nf, width // nf, units)
    lo = dot_bf(hidden_a, w_d, NN).reshape(ns, blk, width)

    dn2_own = dn2[0].astype(f32) + got1.astype(f32) + dn2_far.astype(f32)
    hat_two = middle * inv_two
    dmiddle = dy.astype(f32) + inv_two * (
        dn2_own - hat_two * jnp.mean(dn2_own * hat_two, axis=-1, keepdims=True)
    )
    dmid = dmiddle.astype(bf16)
    datt = dot_bf(dmid, w_out_rel, NT)
    gd = (d_own.astype(f32) + after(d_got, dmid).astype(f32)).astype(bf16)

    live_row = jnp.full((8, 128), n_live, jnp.int32)
    dn, lo_got, sum_d, sum_g, fin_u, sum_o, fin_q, _, _, _, _, _, _, _, dgain = back_call(
        datt, q, laug, attended, k, v, raw, cosine, sine, jnp.broadcast_to(start_rel[None], (8, length)),
        live_row, gains, w_qkv, xh, gd, grad_g, grad_u, att, dmid, lo, nf, ns, quarter, group, head,
    )
    u_pieces, q_pieces = gather_s(fin_u), gather_s(fin_q)
    layer_out = (
        middle + lo[0].astype(f32) + lo_got[0].astype(f32) + lo_got[1].astype(f32)
    ).astype(bf16)
    w_down_grad = sum_d.reshape(ns * unit, width)[:shard].astype(f32)
    w_gate_grad, gate_sum = join_call(gain_two, sum_g, w_gate, ns, nf, shard, unit)
    w_up_grad, up_sum = join_call(gain_two, place(u_pieces, s), w_up, ns, nf, shard, unit)
    ffn_gain_grad = (gate_sum + up_sum)[:, 0]
    w_out_grad = sum_o.reshape(out_rows, width).astype(f32)

    dn_own = dn[0].astype(f32) + dn[1].astype(f32) + dn[2].astype(f32)
    inv_one = lax.rsqrt(jnp.mean(xf * xf, axis=-1, keepdims=True) + epsilon)
    hat_one = xf * inv_one
    tokens_grad = (
        dmiddle + inv_one * (dn_own - hat_one * jnp.mean(dn_own * hat_one, axis=-1, keepdims=True))
    ).astype(bf16)
    query_gain_grad, key_gain_grad = dgain[0, :head], dgain[1, :head]

    w_query_grad, w_key_grad, w_value_grad, one_sum = heads_call(
        gain_one, place(q_pieces, s), w_query, w_key, w_value, [k * head for k in kv_base], q_cols
    )
    attn_gain_grad = one_sum[:, 0]
    return (
        layer_out[None], tokens_grad[None], attn_gain_grad, w_query_grad, w_key_grad,
        w_value_grad, query_gain_grad, key_gain_grad, w_out_grad, ffn_gain_grad,
        w_gate_grad, w_up_grad, w_down_grad,
    )


def solution(mesh):
    row, vec = P("fsdp", None), P("fsdp")
    tok, ids = P("fsdp", "sp", None), P("fsdp", "sp")
    in_specs = (tok, ids, ids, ids, vec, row, row, row, P(), P(), row, vec, row, row, row, tok)
    out_specs = (tok, tok, vec, row, row, row, P(), P(), row, vec, row, row, row)
    return jax.shard_map(local, mesh=mesh, in_specs=in_specs, out_specs=out_specs, check_vma=False)
```
